32 devices in a mesh: dp: 8 (over z, y), head: 4 (over x, core).
Axes of the slice: x: 2, y: 2, z: 4, core: 2. Of those that a mesh axis runs over, the one named last changes fastest.
Arguments:
- tokens: bfloat16 [32768, 512], P(('dp', 'head')), may hold values from -6 to 6
- segments: int32 [32768], P('dp'), may hold values from 0 to 255, never falling along the last dimension, each value on 1 to 256 neighbouring positions
- out_grad: bfloat16 [32768, 512], P(('dp', 'head')), may hold values from -6 to 6
- norm_params: float32 [4, 512], replicated, may hold values from -0.6 to 1.3
- norm_first: float32 [4, 512], replicated, may hold values from -0.0024414062 to 0.0024414062
- norm_second: float32 [4, 512], replicated, may hold values from 7.947286e-08 to 1.2715658e-06
- qkv_weight: float32 [512, 1536], P(None, 'head'), may hold values from -0.25 to 0.25
- qkv_moment: float32 [512, 1536], P(None, 'head'), may hold values from -0.0078125 to 0.0078125
- out_weight: float32 [512, 512], P('head'), may hold values from -2 to 2
- out_moment: float32 [512, 512], P('head'), may hold values from -0.0078125 to 0.0078125
- up_weight: float32 [512, 2048], P(None, ('dp', 'head')), may hold values from -0.25 to 0.25
- up_moment: float32 [512, 2048], P(None, ('dp', 'head')), may hold values from -0.0078125 to 0.0078125
- down_weight: float32 [512, 2048], P(None, ('dp', 'head')), may hold values from -0.125 to 0.125
- down_moment: float32 [512, 2048], P(None, ('dp', 'head')), may hold values from -0.0078125 to 0.0078125
Outputs:
- layer_out: bfloat16 [32768, 512], P(('dp', 'head'))
- input_grad: float32 [32768, 512], P(('dp', 'head'))
- grad_norm: float32 [], replicated
- clipped_grads: float32 [4, 512], replicated
- new_norm_first: float32 [4, 512], replicated
- new_norm_second: float32 [4, 512], replicated
- new_qkv_weight: float32 [512, 1536], P(None, 'head')
- new_qkv_moment: float32 [512, 1536], P(None, 'head')
- new_out_weight: float32 [512, 512], P('head')
- new_out_moment: float32 [512, 512], P('head')
- new_up_weight: float32 [512, 2048], P(None, ('dp', 'head'))
- new_up_moment: float32 [512, 2048], P(None, ('dp', 'head'))
- new_down_weight: float32 [512, 2048], P(None, ('dp', 'head'))
- new_down_moment: float32 [512, 2048], P(None, ('dp', 'head'))
The draws below stay inside these ranges and needn't reach their ends.
Inputs may be any that keep to these rules, and one draw needn't show every extreme that they name: `segments`: segment ids never fall along the rows; each id covers 1 to 256 consecutive rows.
All inputs are finite; a program needn't handle non-finite values.
Results may differ from the reference program's by a relative error of at most 0.028.
Values may be sent and summed in bfloat16 or wider, within the bound.
A program may use at most 128 MiB of HBM per device.

```python
import math
import jax
import jax.numpy as jnp
import numpy as np
from jax import lax

D = 512
HEADS = 8
HEAD_DIM = 64
FF = 2048
SEQ = 512
NS_STEPS = 5
TOKENS = 32768
N_DP = 8
N_HEAD = 4
DEVICES = 32


def draw_norm_params(key, part):
    noise = jnp.clip(jax.random.normal(key, (4, D), jnp.float32), -3.0, 3.0)
    rows = jnp.arange(4)[:, None]
    gains = 1.0 + 0.1 * noise
    shifts = 0.2 * noise
    return jnp.where(rows % 2 == 0, gains, shifts)


def block_levels(rng, dims, pieces, low, largest):
    loudness = 1.0
    for dim, blocks in pieces:
        heights = jax.random.uniform(jax.random.fold_in(jax.random.fold_in(rng, 6), dim), (blocks,), jnp.float32, low / len(pieces), largest / len(pieces))
        loudness = loudness * jnp.repeat(jnp.exp(heights), dims[dim] // blocks).reshape((-1,) + (1,) * (len(dims) - 1 - dim))
    return loudness


def profile(number_of, total, reach, slope):
    weights = [(1 << 20) // math.isqrt(standing ** slope) + 1 for standing in range(2, number_of + 1)]
    rest, counts = total - reach - (number_of - 1), [1] * (number_of - 1)
    while rest > 0:
        movable = [i for i in range(number_of - 1) if counts[i] < reach]
        pool, remaining = sum([weights[i] for i in movable]), rest
        for i in movable:
            addition = min(reach - counts[i], max(1, remaining * weights[i] // pool), rest)
            counts[i] = counts[i] + addition
            rest = rest - addition
    return np.array([reach] + counts)


def uneven_parts(key, number_of, total, bound, lean):
    if number_of == 2:
        one = jax.random.randint(key, (), max(1, total - bound), min(bound, total - 1) + 1)
        return jnp.stack([one, total - one])
    sizes = jnp.asarray(profile(number_of, total, bound, lean), jnp.int32)
    pairs = (number_of - 1) // 2
    giver, receiver = sizes[1:1 + 2 * pairs:2], sizes[2:2 + 2 * pairs:2]
    slack = jnp.minimum(giver - 1, bound - receiver)
    moved = jax.random.randint(jax.random.fold_in(key, 1), (pairs,), 0, 1 << 20) % (slack + 1)
    sizes = sizes.at[1:1 + 2 * pairs:2].set(giver - moved).at[2:2 + 2 * pairs:2].set(receiver + moved)
    return sizes[jax.random.permutation(jax.random.fold_in(key, 2), number_of)]


def normal_values(key, shape, spread, reach, shards=(), kind=jnp.bfloat16):
    values = spread * jax.random.normal(key, shape, jnp.float32)
    if shards:
        values = values * block_levels(key, shape, shards, -0.22, 0.18)
    return jnp.clip(values, -reach, reach).astype(kind)


def setup_inputs(seed: int = 0) -> dict:
    splits = jax.random.split(jax.random.key(seed), 15)
    tokens = normal_values(splits[0], (TOKENS, D), 1.0, 6.0, ((0, 32),))
    segments = jnp.searchsorted(jnp.cumsum(uneven_parts(splits[1], TOKENS // (SEQ // 4), TOKENS, SEQ // 2, 1)), jnp.arange(TOKENS), side="right").astype(jnp.int32)
    out_grad = normal_values(splits[2], (TOKENS, D), 1.0, 6.0, ((0, 32),))
    norm_params = draw_norm_params(jax.random.fold_in(splits[14], 71), 0)
    norm_first = normal_values(splits[4], (4, D), (0.3 * (4 * D * D + 2 * D * FF) ** -0.5), 0.0024414062, (), jnp.float32)
    norm_second = jnp.clip(jnp.exp(jax.random.uniform(splits[5], (4, D), jnp.float32, math.log(7.947286206899662e-08), math.log(1.271565793103946e-06))), 7.947286206899662e-08, 1.271565793103946e-06)
    qkv_weight = normal_values(splits[6], (D, 3 * D), D ** -0.5, 0.25, ((1, 4),), jnp.float32)
    qkv_moment = normal_values(splits[7], (D, 3 * D), ((4 * D * D + 2 * D * FF) ** -0.5), 0.0078125, ((1, 4),), jnp.float32)
    out_weight = normal_values(splits[8], (D, D), (8 * D // SEQ) ** -0.5, 2.0, ((0, 4),), jnp.float32)
    out_moment = normal_values(splits[9], (D, D), ((4 * D * D + 2 * D * FF) ** -0.5), 0.0078125, ((0, 4),), jnp.float32)
    up_weight = normal_values(splits[10], (D, FF), D ** -0.5, 0.25, ((1, 32),), jnp.float32)
    up_moment = normal_values(splits[11], (D, FF), ((4 * D * D + 2 * D * FF) ** -0.5), 0.0078125, ((1, 32),), jnp.float32)
    down_weight = normal_values(splits[12], (D, FF), FF ** -0.5, 0.125, ((1, 32),), jnp.float32)
    down_moment = normal_values(splits[13], (D, FF), ((4 * D * D + 2 * D * FF) ** -0.5), 0.0078125, ((1, 32),), jnp.float32)
    return dict(tokens=tokens, segments=segments, out_grad=out_grad, norm_params=norm_params, norm_first=norm_first, norm_second=norm_second, qkv_weight=qkv_weight, qkv_moment=qkv_moment, out_weight=out_weight, out_moment=out_moment, up_weight=up_weight, up_moment=up_moment, down_weight=down_weight, down_moment=down_moment)


@jax.custom_vjp
def low(v):
    return lax.optimization_barrier(v.astype(jnp.bfloat16)).astype(jnp.float32)

@jax.custom_vjp
def low_back(v):
    return v

def low_keep(v):
    return (low(v), None)

def low_pass(kept, grad):
    return (grad,)

def back_keep(v):
    return (v, None)

def back_low(kept, grad):
    return (low(grad),)
low.defvjp(low_keep, low_pass)
low_back.defvjp(back_keep, back_low)
highest = lax.Precision.HIGHEST
neg_fill = -1000000000.0
norm_eps = 1e-05
ns_a = 3.4445
ns_b = -4.775
ns_c = 2.0315
momentum_decay = 0.95
muon_rate = 0.5
muon_decay = 0.01
beta_one = 0.9
beta_two = 0.95

def layer_norm(values, gain, shift):
    mean = lax.optimization_barrier(jnp.mean(values, axis=-1, keepdims=True))
    centered = values - mean
    var = lax.optimization_barrier(jnp.mean(centered * centered, axis=-1, keepdims=True))
    return centered * lax.rsqrt(var + norm_eps) * gain + shift

def attend(block):
    mixed, segment = block
    query = mixed[:, :, 0]
    keys = mixed[:, :, 1]
    values = mixed[:, :, 2]
    scores = low_back(jnp.einsum('qhd,khd->hqk', query, keys, precision=highest) * HEAD_DIM ** (-0.5))
    same = segment[:, None] == segment[None, :]
    scores = jnp.where(same[None], scores, neg_fill)
    top = lax.optimization_barrier(jnp.max(scores, axis=-1, keepdims=True))
    weights = jnp.exp(scores - top)
    probs = weights / lax.optimization_barrier(jnp.sum(weights, axis=-1, keepdims=True))
    context = jnp.einsum('hqk,khd->qhd', low(probs), values, precision=highest)
    return low_back(low(context)).reshape(SEQ, HEADS * HEAD_DIM)

def forward(tokens, segments, norm_params, qkv_weight, out_weight, up_weight, down_weight):
    first = low(layer_norm(tokens, norm_params[0], norm_params[1]))
    mixed = jnp.dot(first, low(qkv_weight), precision=highest)
    mixed = low(low_back(mixed)).reshape(TOKENS // SEQ, SEQ, HEADS, 3, HEAD_DIM)
    context = lax.map(jax.checkpoint(attend), (mixed, segments.reshape(TOKENS // SEQ, SEQ)))
    attended = low_back(jnp.dot(context.reshape(TOKENS, D), low(out_weight), precision=highest))
    middle = tokens + attended
    second = low(layer_norm(middle, norm_params[2], norm_params[3]))
    hidden = low_back(jnp.dot(second, low(up_weight), precision=highest))
    active = low(hidden * jax.nn.sigmoid(1.702 * hidden))
    return middle + jnp.dot(active, low(down_weight).T, precision=highest)

def gram_qkv(block):
    parts = block.reshape(D, N_HEAD, 3 * D // N_HEAD)
    return jnp.einsum('ahc,bhc->hab', parts, parts, precision=highest)

def gram_out(block):
    parts = block.reshape(N_HEAD, D // N_HEAD, D)
    return jnp.einsum('hra,hrb->hab', parts, parts, precision=highest)

def gram_wide(block):
    parts = block.reshape(D, N_DP, N_HEAD, FF // DEVICES)
    return jnp.einsum('adhf,bdhf->hab', parts, parts, precision=highest)

def orthogonal(start, partial_fn, on_left):
    block = start
    for turn in range(NS_STEPS):
        gram = low(lax.optimization_barrier(jnp.sum(low(partial_fn(block)), axis=0)))
        square = jnp.dot(gram, gram, precision=highest)
        mix = low(ns_b * gram + ns_c * square)
        if on_left:
            block = low(ns_a * block + jnp.dot(mix, block, precision=highest))
        else:
            block = low(ns_a * block + jnp.dot(block, mix, precision=highest))
    return block

def reference(tokens, segments, out_grad, norm_params, norm_first, norm_second, qkv_weight, qkv_moment, out_weight, out_moment, up_weight, up_moment, down_weight, down_moment):

    def wrapped(inputs, params, w_qkv, w_out, w_up, w_down):
        return forward(inputs, segments, params, w_qkv, w_out, w_up, w_down)
    result, pull = jax.vjp(wrapped, tokens.astype(jnp.float32), norm_params, qkv_weight, out_weight, up_weight, down_weight)
    input_grad, norm_grad, qkv_grad, out_grad_w, up_grad, down_grad = pull(out_grad.astype(jnp.float32))
    grads = [qkv_grad, out_grad_w, up_grad, down_grad]
    total = jnp.sum(norm_grad * norm_grad)
    for grad in grads:
        total = total + jnp.sum(grad * grad)
    grad_norm = jnp.sqrt(total)
    clip = jnp.minimum(1.0, 1.0 / (grad_norm + 1e-06))
    moments = [qkv_moment, out_moment, up_moment, down_moment]
    weights = [qkv_weight, out_weight, up_weight, down_weight]
    partial_fns = [gram_qkv, gram_out, gram_wide, gram_wide]
    sides = [True, False, True, True]
    factors = [math.sqrt(3.0), math.sqrt(SEQ / 8.0), math.sqrt(max(1.0, FF / D)), math.sqrt(max(1.0, FF / D))]
    new_weights = []
    new_moments = []
    for index in range(4):
        moment = momentum_decay * moments[index] + clip * grads[index]
        size = jnp.sqrt(jnp.sum(moment * moment))
        start = low(moment / (size + 1e-07))
        ortho = orthogonal(start, partial_fns[index], sides[index])
        new_weights.append(weights[index] * (1.0 - muon_rate * muon_decay) - muon_rate * factors[index] * ortho)
        new_moments.append(moment)
    clipped = clip * norm_grad
    first_new = beta_one * norm_first + (1.0 - beta_one) * clipped
    second_new = beta_two * norm_second + (1.0 - beta_two) * clipped * clipped
    return (result.astype(jnp.bfloat16), input_grad, grad_norm, clipped, first_new, second_new, new_weights[0], new_moments[0], new_weights[1], new_moments[1], new_weights[2], new_moments[2], new_weights[3], new_moments[3])
```

```python
import math

import jax
import jax.numpy as jnp
from jax import lax
from jax.experimental import pallas as pl
from jax.experimental.pallas import tpu as pltpu
from jax.sharding import PartitionSpec as P

HEAD_DIM = 64
FF = 2048
SEQ = 512
NS_STEPS = 5


neg_fill = -1000000000.0
norm_eps = 1e-05
ns_a = 3.4445
ns_b = -4.775
ns_c = 2.0315
momentum_decay = 0.95
muon_rate = 0.5
muon_decay = 0.01
beta_one = 0.9
beta_two = 0.95


def normalize(values, gain, shift):
    mean = jnp.mean(values, axis=-1, keepdims=True)
    centered = values - mean
    factor = lax.rsqrt(jnp.mean(centered * centered, axis=-1, keepdims=True) + norm_eps)
    plain = centered * factor
    return (plain * gain + shift, plain, factor)


def normalize_back(upper, plain, factor, gain):
    inner = upper * gain
    lower = factor * (
        inner
        - jnp.mean(inner, axis=-1, keepdims=True)
        - plain * jnp.mean(inner * plain, axis=-1, keepdims=True)
    )
    return (lower, jnp.sum(upper * plain, axis=0), jnp.sum(upper, axis=0))


def masked_scores(query, keys, segment):
    scores = jnp.einsum(
        "qhd,khd->hqk", query, keys, preferred_element_type=jnp.float32
    ) * HEAD_DIM ** (-0.5)
    same = segment[:, None] == segment[None, :]
    return jnp.where(same[None], scores, neg_fill)


def attend_forward(block):
    query, keys, values, segment = block
    scores = masked_scores(query, keys, segment)
    top = jnp.max(scores, axis=-1, keepdims=True)
    weights = jnp.exp(scores - top)
    total = jnp.sum(weights, axis=-1, keepdims=True)
    probs = (weights / total).astype(jnp.bfloat16)
    context = jnp.einsum("hqk,khd->qhd", probs, values, preferred_element_type=jnp.float32)
    return (context.astype(jnp.bfloat16), top + jnp.log(total))


def attend_backward(block):
    query, keys, values, segment, context_grad, lse = block
    scores = masked_scores(query, keys, segment)
    probs = jnp.exp(scores - lse)
    probs_low = probs.astype(jnp.bfloat16)
    probs_grad = jnp.einsum(
        "qhd,khd->hqk", context_grad, values, preferred_element_type=jnp.float32
    )
    inner = jnp.sum(probs * probs_grad, axis=-1, keepdims=True)
    score_grad = (probs * (probs_grad - inner)).astype(jnp.bfloat16)
    query_grad = jnp.einsum(
        "hqk,khd->qhd", score_grad, keys, preferred_element_type=jnp.float32
    ) * HEAD_DIM ** (-0.5)
    key_grad = jnp.einsum(
        "hqk,qhd->khd", score_grad, query, preferred_element_type=jnp.float32
    ) * HEAD_DIM ** (-0.5)
    value_grad = jnp.einsum(
        "hqk,qhd->khd", probs_low, context_grad, preferred_element_type=jnp.float32
    )
    return jnp.stack([query_grad, key_grad, value_grad], axis=2).astype(jnp.bfloat16)


def gram_left(block):
    return lax.dot_general(
        block, block, (((1,), (1,)), ((), ())), preferred_element_type=jnp.float32
    )


def gram_right(block):
    return lax.dot_general(
        block, block, (((0,), (0,)), ((), ())), preferred_element_type=jnp.float32
    )


def squares_of(moment, grad, weight):
    return (
        jnp.stack([jnp.sum(moment * moment), jnp.sum(moment * grad), jnp.sum(grad * grad)]) * weight
    )


COMM_ORDERS = ("cxylg", "cylgx", "clgxy")
WIDE = 2048


def coordinates():
    dp = lax.axis_index("dp")
    head = lax.axis_index("head")
    bits = {
        "c": head % 2,
        "x": head // 2,
        "y": dp % 2,
        "l": (dp // 2) % 2,
        "g": dp // 4,
    }
    steps = {"c": (0, 1), "x": (0, 2), "y": (1, 0), "l": (2, 0), "g": (4, 0)}
    peers = {}
    for name, (along_dp, along_head) in steps.items():
        turn = 1 - 2 * bits[name]
        peers[name] = (dp + along_dp * turn, head + along_head * turn)
    return dp, head, bits, peers


def remote(src, dst, send_sem, recv_sem, peer):
    return pltpu.make_async_remote_copy(
        src_ref=src,
        dst_ref=dst,
        send_sem=send_sem,
        recv_sem=recv_sem,
        device_id=peer,
        device_id_type=pl.DeviceIdType.MESH,
    )


def greet(head, dp, peers):
    barrier = pltpu.get_barrier_semaphore()
    across = (dp, 3 - head)
    everyone = list(peers.values()) + [across]
    for peer in everyone:
        pl.semaphore_signal(
            barrier, inc=1, device_id=peer, device_id_type=pl.DeviceIdType.MESH
        )
    pl.semaphore_wait(barrier, len(everyone))
    return across


def add_rows(dst, dst_at, one, one_at, two, two_at, count):
    def body(i, carry):
        here = pl.multiple_of(i * 16, 16)
        total = one[pl.ds(one_at + here, 16), :].astype(jnp.float32) + two[
            pl.ds(two_at + here, 16), :
        ].astype(jnp.float32)
        dst[pl.ds(dst_at + here, 16), :] = total.astype(jnp.bfloat16)
        return carry

    lax.fori_loop(0, count // 16, body, 0)


def update_kernel(
    a_ref, u_ref, d_ref, vec_ref, mom_ref,
    oq_ref, oo_ref, ou_ref, od_ref, gq_ref, go_ref, gu_ref, gd_ref, vsum_ref, scal_ref,
    got, acc, full, vgot, vnow, block, work, gram_ref, mix_ref,
    ssem, rsem, asem, bsem, vssem, vrsem, dssem, drsem,
):
    dp, head, bits, peers = coordinates()
    across = greet(head, dp, peers)
    sources = (a_ref, u_ref, d_ref)
    vnow[0] = vec_ref[...]
    spans = []
    for m in range(3):
        low = 0
        size = 512
        span = []
        for name in COMM_ORDERS[m]:
            size = size // 2
            keep = low + bits[name] * size
            give = low + (1 - bits[name]) * size
            span.append((name, size, keep, give))
            low = keep
        spans.append(span)
    for k in range(5):
        copies = []
        for m in range(3):
            name, size, keep, give = spans[m][k]
            place = 512 - 2 * size
            if k == 0:
                src = sources[m].at[pl.ds(pl.multiple_of(give, 16), size)]
            else:
                before = 512 - 4 * size
                src = acc.at[m, pl.ds(pl.multiple_of(before + (1 - bits[name]) * size, 16), size)]
            cp = remote(
                src, got.at[m, pl.ds(place, size)], ssem.at[m, k], rsem.at[m, k], peers[name]
            )
            cp.start()
            copies.append(cp)
        vcp = remote(vnow.at[k], vgot.at[k], vssem.at[k], vrsem.at[k], peers[COMM_ORDERS[0][k]])
        vcp.start()
        for m in range(3):
            name, size, keep, give = spans[m][k]
            place = 512 - 2 * size
            copies[m].wait()
            if k == 0:
                add_rows(acc.at[m], place, sources[m], pl.multiple_of(keep, 16), got.at[m], place, size)
            elif k < 4:
                before = 512 - 4 * size
                add_rows(
                    acc.at[m], place, acc.at[m],
                    pl.multiple_of(before + bits[name] * size, 16), got.at[m], place, size,
                )
            else:
                before = 512 - 4 * size
                add_rows(
                    full.at[m], pl.multiple_of(keep, 16), acc.at[m],
                    pl.multiple_of(before + bits[name] * size, 16), got.at[m], place, size,
                )
        vcp.wait()
        vnow[k + 1] = vnow[k] + vgot[k]
    for k in reversed(range(5)):
        copies = []
        for m in range(3):
            name, size, keep, give = spans[m][k]
            mine = full.at[m, pl.ds(pl.multiple_of(keep, 16), size)]
            cp = remote(mine, mine, asem.at[m, k], bsem.at[m, k], peers[name])
            cp.start()
            copies.append(cp)
        for cp in copies:
            cp.wait()
    vsum_ref[...] = vnow[5]
    chunk = 16

    def square_body(i, sums):
        here = pl.multiple_of(i * chunk, chunk)
        out = sums
        for m in range(3):
            part = full[m, pl.ds(here, chunk), :].astype(jnp.float32)
            out = out + jnp.sum(part * part, axis=0, keepdims=True)
        return out

    sums = lax.fori_loop(0, 512 // chunk, square_body, jnp.zeros((1, WIDE), jnp.float32))
    total = jnp.sum(sums, axis=1, keepdims=True)
    vector = vnow[5]
    total = total + jnp.sum(
        jnp.sum(vector * vector, axis=0, keepdims=True), axis=1, keepdims=True
    )
    norm = jnp.sqrt(total)
    clip = jnp.minimum(1.0, 1.0 / (norm + 1e-06))
    lane = lax.broadcasted_iota(jnp.int32, (8, 128), 1)
    scal_ref[...] = jnp.where(lane == 0, norm, clip)
    which = jnp.maximum(head - 1, 0)
    columns = lax.broadcasted_iota(jnp.int32, (chunk, WIDE), 1)
    first_column = jnp.where(head == 1, 1536, 0)
    past_column = jnp.where(head == 0, 1536, WIDE)
    inside = (columns >= first_column) & (columns < past_column)

    def moment_body(i, sums):
        here = pl.multiple_of(i * chunk, chunk)
        grad = full[which, pl.ds(here, chunk), :].astype(jnp.float32)
        grad = jnp.where(inside, grad, 0.0)
        moment = momentum_decay * mom_ref[pl.ds(here, chunk), :].astype(jnp.float32) + clip * grad
        work[pl.ds(here, chunk), :] = moment
        return sums + jnp.sum(moment * moment, axis=0, keepdims=True)

    sums = lax.fori_loop(0, 512 // chunk, moment_body, jnp.zeros((1, WIDE), jnp.float32))
    scale = 1.0 / (jnp.sqrt(jnp.sum(sums, axis=1, keepdims=True)) + 1e-07)

    def start_body(i, carry):
        here = pl.multiple_of(i * chunk, chunk)
        block[0, pl.ds(here, chunk), :] = (work[pl.ds(here, chunk), :] * scale).astype(jnp.bfloat16)
        return carry

    lax.fori_loop(0, 512 // chunk, start_body, 0)
    own = (gq_ref, go_ref, gu_ref, gd_ref)
    gq_ref[...] = full[0, :, pl.ds(pl.multiple_of(head * 384, 128), 384)]
    go_ref[...] = full[0, :, pl.ds(pl.multiple_of(1536 + head * 128, 128), 128)]
    pair = pl.multiple_of((dp * 2 + bits["x"]) * 128, 128)
    gu_ref[...] = full[1, :, pl.ds(pair, 128)]
    gd_ref[...] = full[2, :, pl.ds(pair, 128)]
    tile = 256

    def turn_body(turn, carry):
        now = turn % 2
        later = 1 - now

        def gram_body(i, c):
            rows = pl.ds(pl.multiple_of(i * tile, tile), tile)
            gram_ref[rows, :] = lax.dot_general(
                block[now, rows, :], block[now], (((1,), (1,)), ((), ())),
                preferred_element_type=jnp.float32,
            ).astype(jnp.bfloat16)
            return c

        lax.fori_loop(0, 512 // tile, gram_body, 0)

        def mix_body(i, c):
            rows = pl.ds(pl.multiple_of(i * tile, tile), tile)
            mine = gram_ref[rows, :]
            mix_ref[rows, :] = (
                ns_b * mine.astype(jnp.float32)
                + ns_c * jnp.dot(mine, gram_ref[...], preferred_element_type=jnp.float32)
            ).astype(jnp.bfloat16)
            return c

        lax.fori_loop(0, 512 // tile, mix_body, 0)

        def next_body(i, c):
            cols = pl.ds(pl.multiple_of(i * 512, 512), 512)
            block[later, :, cols] = (
                ns_a * block[now, :, cols].astype(jnp.float32)
                + jnp.dot(mix_ref[...], block[now, :, cols], preferred_element_type=jnp.float32)
            ).astype(jnp.bfloat16)
            return c

        lax.fori_loop(0, WIDE // 512, next_body, 0)
        return carry

    lax.fori_loop(0, NS_STEPS, turn_body, 0)
    last = NS_STEPS % 2
    outs = (oq_ref, oo_ref, ou_ref, od_ref)

    def piece(kind, who):
        if kind == 0:
            return block.at[last, :, pl.ds(pl.multiple_of(who * 384, 128), 384)]
        if kind == 1:
            return block.at[last, :, pl.ds(pl.multiple_of(1536 + who * 128, 128), 128)]
        return block.at[last, :, pl.ds(pl.multiple_of((dp * 2 + who // 2) * 128, 128), 128)]

    partners = (peers["c"], peers["x"], across)
    for kind in range(4):
        @pl.when(head == kind)
        def _(kind=kind):
            copies = []
            for j, partner in enumerate(partners):
                cp = remote(
                    piece(kind, partner[1]), outs[kind], dssem.at[j], drsem.at[kind], partner
                )
                cp.start()
                copies.append(cp)
            outs[kind][...] = piece(kind, head)[...]
            for cp in copies:
                cp.wait_send()

    for kind in range(4):
        @pl.when(head != kind)
        def _(kind=kind):
            remote(
                piece(kind, head), outs[kind], dssem.at[0], drsem.at[kind], partners[0]
            ).wait_recv()


def update_call(a, u, d, vec, mom):
    low = jnp.bfloat16
    shape = jax.ShapeDtypeStruct
    vmem = pl.BlockSpec(memory_space=pltpu.VMEM)
    return pl.pallas_call(
        update_kernel,
        out_shape=(
            shape((512, 384), low), shape((512, 128), low), shape((512, 128), low), shape((512, 128), low),
            shape((512, 384), low), shape((512, 128), low), shape((512, 128), low), shape((512, 128), low),
            shape((4, 512), jnp.float32), shape((8, 128), jnp.float32),
        ),
        in_specs=[vmem] * 5,
        out_specs=(vmem,) * 10,
        scratch_shapes=[
            pltpu.VMEM((3, 512, WIDE), low),
            pltpu.VMEM((3, 512, WIDE), low),
            pltpu.VMEM((3, 512, WIDE), low),
            pltpu.VMEM((5, 4, 512), jnp.float32),
            pltpu.VMEM((6, 4, 512), jnp.float32),
            pltpu.VMEM((2, 512, WIDE), low),
            pltpu.VMEM((512, WIDE), jnp.float32),
            pltpu.VMEM((512, 512), low),
            pltpu.VMEM((512, 512), low),
            pltpu.SemaphoreType.DMA((3, 5)),
            pltpu.SemaphoreType.DMA((3, 5)),
            pltpu.SemaphoreType.DMA((3, 5)),
            pltpu.SemaphoreType.DMA((3, 5)),
            pltpu.SemaphoreType.DMA((5,)),
            pltpu.SemaphoreType.DMA((5,)),
            pltpu.SemaphoreType.DMA((3,)),
            pltpu.SemaphoreType.DMA((4,)),
        ],
        compiler_params=pltpu.CompilerParams(
            collective_id=1, has_side_effects=True, vmem_limit_bytes=60 << 20
        ),
        name="update",
    )(a, u, d, vec, mom)


def general_update(
    whole_qkv, whole_out, up_grad, down_grad, vector_part,
    qkv_moment, out_moment, up_moment, down_moment,
):
    everywhere = ("dp", "head")
    narrow = out_moment.shape[0]
    up_part, down_part = (
        lax.psum_scatter(
            up_grad.astype(jnp.bfloat16), everywhere, scatter_dimension=1, tiled=True
        ).astype(jnp.float32),
        lax.psum_scatter(
            down_grad.astype(jnp.bfloat16), everywhere, scatter_dimension=1, tiled=True
        ).astype(jnp.float32),
    )
    qkv_part = lax.psum_scatter(
        whole_qkv.astype(jnp.bfloat16), "head", scatter_dimension=1, tiled=True
    )
    out_part = lax.psum_scatter(
        whole_out.astype(jnp.bfloat16), "head", scatter_dimension=0, tiled=True
    )
    qkv_sum, out_sum = (
        lax.psum(qkv_part, "dp").astype(jnp.float32),
        lax.psum(out_part, "dp").astype(jnp.float32),
    )
    leading = (lax.axis_index("dp") == 0).astype(jnp.float32)
    moments = [qkv_moment, out_moment, up_moment, down_moment]
    grads = [qkv_sum, out_sum, up_part, down_part]
    stats = jnp.stack(
        [
            squares_of(qkv_moment, qkv_sum, leading),
            squares_of(out_moment, out_sum, leading),
            squares_of(up_moment, up_part, 1.0),
            squares_of(down_moment, down_part, 1.0),
        ]
    )
    vector_sum, stat_sum = lax.psum((vector_part, stats), everywhere)
    grad_norm = jnp.sqrt(jnp.sum(stat_sum[:, 2]) + jnp.sum(vector_sum * vector_sum))
    clip = jnp.minimum(1.0, 1.0 / (grad_norm + 1e-06))
    sizes = jnp.sqrt(
        momentum_decay * momentum_decay * stat_sum[:, 0]
        + 2.0 * momentum_decay * clip * stat_sum[:, 1]
        + clip * clip * stat_sum[:, 2]
    )
    new_moments = [momentum_decay * moments[index] + clip * grads[index] for index in range(4)]
    starts = [
        (new_moments[index] / (sizes[index] + 1e-07)).astype(jnp.bfloat16) for index in range(4)
    ]
    blocks = [
        lax.all_gather(starts[0], "head", axis=1, tiled=True),
        lax.all_gather(starts[1], "head", axis=0, tiled=True),
        lax.all_gather(starts[2], everywhere, axis=1, tiled=True),
        lax.all_gather(starts[3], everywhere, axis=1, tiled=True),
    ]
    for turn in range(NS_STEPS):
        updated = []
        for index in range(4):
            form = gram_right if index == 1 else gram_left
            gram = form(blocks[index]).astype(jnp.bfloat16)
            mix = (
                ns_b * gram.astype(jnp.float32)
                + ns_c * jnp.dot(gram, gram, preferred_element_type=jnp.float32)
            ).astype(jnp.bfloat16)
            if index == 1:
                product = jnp.dot(blocks[index], mix, preferred_element_type=jnp.float32)
            else:
                product = jnp.dot(mix, blocks[index], preferred_element_type=jnp.float32)
            updated.append(
                (ns_a * blocks[index].astype(jnp.float32) + product).astype(jnp.bfloat16)
            )
        blocks = updated
    share = up_moment.shape[1]
    along = lax.axis_index("head")
    offset = (lax.axis_index("dp") * lax.axis_size("head") + along) * share
    owned = [
        lax.dynamic_slice_in_dim(blocks[0], along * qkv_moment.shape[1], qkv_moment.shape[1], 1),
        lax.dynamic_slice_in_dim(blocks[1], along * narrow, narrow, 0),
        lax.dynamic_slice_in_dim(blocks[2], offset, share, 1),
        lax.dynamic_slice_in_dim(blocks[3], offset, share, 1),
    ]
    return (owned, new_moments, vector_sum, grad_norm, clip)


def shards(
    tokens,
    segments,
    out_grad,
    norm_params,
    norm_first,
    norm_second,
    qkv_weight,
    qkv_moment,
    out_weight,
    out_moment,
    up_weight,
    up_moment,
    down_weight,
    down_moment,
):
    width = tokens.shape[1]
    rows = tokens.shape[0]
    narrow = out_weight.shape[0]
    sequences = rows // SEQ
    heads = width // HEAD_DIM
    everywhere = ("dp", "head")
    inputs = tokens.astype(jnp.float32)
    first, first_plain, first_factor = normalize(inputs, norm_params[0], norm_params[1])
    first_low = first.astype(jnp.bfloat16)
    qkv_full = lax.all_gather(qkv_weight.astype(jnp.bfloat16), "head", axis=1, tiled=True)
    out_full = lax.all_gather(out_weight.astype(jnp.bfloat16), "head", axis=0, tiled=True)
    up_all = lax.all_gather(up_weight.astype(jnp.bfloat16), everywhere, axis=1, tiled=True)
    down_all = lax.all_gather(down_weight.astype(jnp.bfloat16), everywhere, axis=1, tiled=True)
    mixed = jnp.dot(first_low, qkv_full, preferred_element_type=jnp.float32).astype(jnp.bfloat16)
    mixed = mixed.reshape(sequences, SEQ, heads, 3, HEAD_DIM)
    segment_rows = lax.dynamic_slice_in_dim(segments, lax.axis_index("head") * rows, rows, 0)
    segment_rows = segment_rows.reshape(sequences, SEQ)
    query = mixed[:, :, :, 0]
    keys = mixed[:, :, :, 1]
    values = mixed[:, :, :, 2]
    context, lse = lax.map(attend_forward, (query, keys, values, segment_rows))
    context = context.reshape(rows, width)
    attended = jnp.dot(context, out_full, preferred_element_type=jnp.float32)
    middle = inputs + attended
    second, second_plain, second_factor = normalize(middle, norm_params[2], norm_params[3])
    second_low = second.astype(jnp.bfloat16)
    hidden = jnp.dot(second_low, up_all, preferred_element_type=jnp.float32)
    switch = jax.nn.sigmoid(1.702 * hidden)
    active = (hidden * switch).astype(jnp.bfloat16)
    result = middle + lax.dot_general(
        active, down_all, (((1,), (1,)), ((), ())), preferred_element_type=jnp.float32
    )
    layer_out = result.astype(jnp.bfloat16)
    down_grad = lax.dot_general(
        out_grad, active, (((0,), (0,)), ((), ())), preferred_element_type=jnp.float32
    )
    active_grad = jnp.dot(out_grad, down_all, preferred_element_type=jnp.float32)
    hidden_grad = (active_grad * (switch + 1.702 * hidden * switch * (1.0 - switch))).astype(
        jnp.bfloat16
    )
    up_grad = lax.dot_general(
        second_low, hidden_grad, (((0,), (0,)), ((), ())), preferred_element_type=jnp.float32
    )
    second_grad = lax.dot_general(
        hidden_grad, up_all, (((1,), (1,)), ((), ())), preferred_element_type=jnp.float32
    )
    middle_lower, gain_two, shift_two = normalize_back(
        second_grad, second_plain, second_factor, norm_params[2]
    )
    middle_grad = out_grad.astype(jnp.float32) + middle_lower
    attended_low = middle_grad.astype(jnp.bfloat16)
    context_grad = lax.dot_general(
        attended_low, out_full, (((1,), (1,)), ((), ())), preferred_element_type=jnp.float32
    ).astype(jnp.bfloat16)
    whole_out = lax.dot_general(
        context, attended_low, (((0,), (0,)), ((), ())), preferred_element_type=jnp.float32
    )
    context_grad = context_grad.reshape(sequences, SEQ, heads, HEAD_DIM)
    mixed_grad = lax.map(attend_backward, (query, keys, values, segment_rows, context_grad, lse))
    mixed_grad = mixed_grad.reshape(rows, 3 * width)
    whole_qkv = lax.dot_general(
        first_low, mixed_grad, (((0,), (0,)), ((), ())), preferred_element_type=jnp.float32
    )
    first_grad = lax.dot_general(
        mixed_grad, qkv_full, (((1,), (1,)), ((), ())), preferred_element_type=jnp.float32
    )
    input_lower, gain_one, shift_one = normalize_back(
        first_grad, first_plain, first_factor, norm_params[0]
    )
    input_grad = middle_grad + input_lower
    vector_part = jnp.stack([gain_one, shift_one, gain_two, shift_two])
    fast = lax.axis_size("dp") == 8 and lax.axis_size("head") == 4
    if fast:
        out_t = lax.dot_general(
            attended_low, context, (((0,), (0,)), ((), ())), preferred_element_type=jnp.float32
        )
        both = jnp.concatenate([whole_qkv, out_t], axis=1).astype(jnp.bfloat16)
        along = lax.axis_index("head")
        low_m = [m.astype(jnp.bfloat16) for m in (qkv_moment, out_moment.T, up_moment, down_moment)]
        mq = lax.all_gather(low_m[0], "head", axis=1, tiled=True)
        mo = lax.all_gather(low_m[1], "head", axis=1, tiled=True)
        mu = lax.all_gather(low_m[2], everywhere, axis=1, tiled=True)
        md = lax.all_gather(low_m[3], everywhere, axis=1, tiled=True)
        mom = lax.select_n(
            along,
            jnp.pad(mq, ((0, 0), (0, 512))),
            jnp.pad(mo, ((0, 0), (1536, 0))),
            mu,
            md,
        )
        (oq, oo, ou, od, gq, go, gu, gd, vector_sum, scalars) = update_call(
            both, up_grad.astype(jnp.bfloat16), down_grad.astype(jnp.bfloat16), vector_part, mom
        )
        grad_norm = scalars[0, 0]
        clip = scalars[0, 1]
        half = (along % 2) * 64
        cut = lambda v: lax.dynamic_slice_in_dim(v, half, 64, 1)
        owned = [oq, oo.T, cut(ou), cut(od)]
        grads = [gq, go.T, cut(gu), cut(gd)]
        moments = [qkv_moment, out_moment, up_moment, down_moment]
        new_moments = [
            momentum_decay * moments[index] + clip * grads[index].astype(jnp.float32)
            for index in range(4)
        ]
    else:
        (owned, new_moments, vector_sum, grad_norm, clip) = general_update(
            whole_qkv, whole_out, up_grad, down_grad, vector_part,
            qkv_moment, out_moment, up_moment, down_moment,
        )
    weights = [qkv_weight, out_weight, up_weight, down_weight]
    factors = [
        math.sqrt(3.0),
        math.sqrt(SEQ / 8.0),
        math.sqrt(max(1.0, FF / width)),
        math.sqrt(max(1.0, FF / width)),
    ]
    new_weights = [
        weights[index] * (1.0 - muon_rate * muon_decay)
        - muon_rate * factors[index] * owned[index].astype(jnp.float32)
        for index in range(4)
    ]
    clipped = clip * vector_sum
    first_new = beta_one * norm_first + (1.0 - beta_one) * clipped
    second_new = beta_two * norm_second + (1.0 - beta_two) * clipped * clipped
    return (
        layer_out,
        input_grad,
        grad_norm,
        clipped,
        first_new,
        second_new,
        new_weights[0],
        new_moments[0],
        new_weights[1],
        new_moments[1],
        new_weights[2],
        new_moments[2],
        new_weights[3],
        new_moments[3],
    )


def solution(mesh):
    placed = (
        P(("dp", "head"), None),
        P("dp"),
        P(("dp", "head"), None),
        P(),
        P(),
        P(),
        P(None, "head"),
        P(None, "head"),
        P("head", None),
        P("head", None),
        P(None, ("dp", "head")),
        P(None, ("dp", "head")),
        P(None, ("dp", "head")),
        P(None, ("dp", "head")),
    )
    return jax.shard_map(
        shards,
        mesh=mesh,
        in_specs=placed,
        out_specs=(
            P(("dp", "head"), None),
            P(("dp", "head"), None),
            P(),
            P(),
            P(),
            P(),
            P(None, "head"),
            P(None, "head"),
            P("head", None),
            P("head", None),
            P(None, ("dp", "head")),
            P(None, ("dp", "head")),
            P(None, ("dp", "head")),
            P(None, ("dp", "head")),
        ),
        check_vma=False,
    )
```

```python
import math

import jax
import jax.numpy as jnp
from jax import lax
from jax.experimental import pallas as pl
from jax.experimental.pallas import tpu as pltpu
from jax.sharding import PartitionSpec as P

HEAD_DIM = 64
FF = 2048
SEQ = 512
NS_STEPS = 5


neg_fill = -1000000000.0
norm_eps = 1e-05
ns_a = 3.4445
ns_b = -4.775
ns_c = 2.0315
momentum_decay = 0.95
muon_rate = 0.5
muon_decay = 0.01
beta_one = 0.9
beta_two = 0.95


def normalize(values, gain, shift):
    mean = jnp.mean(values, axis=-1, keepdims=True)
    centered = values - mean
    factor = lax.rsqrt(jnp.mean(centered * centered, axis=-1, keepdims=True) + norm_eps)
    plain = centered * factor
    return (plain * gain + shift, plain, factor)


def normalize_back(upper, plain, factor, gain):
    inner = upper * gain
    lower = factor * (
        inner
        - jnp.mean(inner, axis=-1, keepdims=True)
        - plain * jnp.mean(inner * plain, axis=-1, keepdims=True)
    )
    return (lower, jnp.sum(upper * plain, axis=0), jnp.sum(upper, axis=0))


def masked_scores(query, keys, segment):
    scores = jnp.einsum(
        "qhd,khd->hqk", query, keys, preferred_element_type=jnp.float32
    ) * HEAD_DIM ** (-0.5)
    same = segment[:, None] == segment[None, :]
    return jnp.where(same[None], scores, neg_fill)


def attend_forward(block):
    query, keys, values, segment = block
    scores = masked_scores(query, keys, segment)
    top = jnp.max(scores, axis=-1, keepdims=True)
    weights = jnp.exp(scores - top)
    total = jnp.sum(weights, axis=-1, keepdims=True)
    probs = (weights / total).astype(jnp.bfloat16)
    context = jnp.einsum("hqk,khd->qhd", probs, values, preferred_element_type=jnp.float32)
    return (context.astype(jnp.bfloat16), top + jnp.log(total))


def attend_backward(block):
    query, keys, values, segment, context_grad, lse = block
    scores = masked_scores(query, keys, segment)
    probs = jnp.exp(scores - lse)
    probs_low = probs.astype(jnp.bfloat16)
    probs_grad = jnp.einsum(
        "qhd,khd->hqk", context_grad, values, preferred_element_type=jnp.float32
    )
    inner = jnp.sum(probs * probs_grad, axis=-1, keepdims=True)
    score_grad = (probs * (probs_grad - inner)).astype(jnp.bfloat16)
    query_grad = jnp.einsum(
        "hqk,khd->qhd", score_grad, keys, preferred_element_type=jnp.float32
    ) * HEAD_DIM ** (-0.5)
    key_grad = jnp.einsum(
        "hqk,qhd->khd", score_grad, query, preferred_element_type=jnp.float32
    ) * HEAD_DIM ** (-0.5)
    value_grad = jnp.einsum(
        "hqk,qhd->khd", probs_low, context_grad, preferred_element_type=jnp.float32
    )
    return jnp.stack([query_grad, key_grad, value_grad], axis=2).astype(jnp.bfloat16)


def gram_left(block):
    return lax.dot_general(
        block, block, (((1,), (1,)), ((), ())), preferred_element_type=jnp.float32
    )


def gram_right(block):
    return lax.dot_general(
        block, block, (((0,), (0,)), ((), ())), preferred_element_type=jnp.float32
    )


def squares_of(moment, grad, weight):
    return (
        jnp.stack([jnp.sum(moment * moment), jnp.sum(moment * grad), jnp.sum(grad * grad)]) * weight
    )


ROWS = 1024
TILE = 256
PAIRS = 4
WIDE = 2048
CHUNK = 512
VMEM_BYTES = 62 << 20
LOW = jnp.bfloat16
F32 = jnp.float32


def dot(one, two):
    return jnp.dot(one, two, preferred_element_type=F32)


def dot_back(one, two):
    return lax.dot_general(one, two, (((1,), (1,)), ((), ())), preferred_element_type=F32)


def dot_rows(one, two):
    return lax.dot_general(one, two, (((0,), (0,)), ((), ())), preferred_element_type=F32)


def each(count, body):
    def step(i, carry):
        body(i)
        return carry

    lax.fori_loop(0, count, step, 0)


def rows_at(i, size):
    return pl.ds(pl.multiple_of(i * size, size), size)


def first_phase(tokens, params, first):
    gain = params[0:1, :]
    shift = params[1:2, :]

    def body(i):
        here = rows_at(i, 128)
        plain_gain, _, _ = normalize(tokens[here, :].astype(F32), gain, shift)
        first[here, :] = plain_gain.astype(LOW)

    each(ROWS // 128, body)


def mixed_phase(pair, first, wqkv, mixed):
    def body(i):
        here = rows_at(i, TILE)
        mixed[pair, here, :] = dot(first[here, :], wqkv[pair]).astype(LOW)

    each(ROWS // TILE, body)


def bias_phase(seg_col, seg_row, bias):
    def body(i):
        here = rows_at(i, 128)
        row = seg_row[pl.ds(i // 4, 1), :]
        bias[here, :] = jnp.where(seg_col[here, :] == row, 0.0, neg_fill).astype(LOW)

    each(ROWS // 128, body)


def attend_phase(pair, mixed, bias, probs, context):
    tile = 256
    lane = lax.broadcasted_iota(jnp.int32, (1, 128), 1)
    left = (lane < HEAD_DIM).astype(LOW)

    def body(i):
        seq = i // (SEQ // tile)
        here = rows_at(i, tile)
        keys_at = rows_at(seq, SEQ)
        inside = rows_at(i % (SEQ // tile), tile)
        query = mixed[pair, here, 0:128] * LOW(HEAD_DIM ** (-0.5))
        keys = mixed[pair, keys_at, 128:256]
        values = mixed[pair, keys_at, 256:384]
        allowed = bias[here, :].astype(F32)
        outs = []
        for half in range(2):
            mask = left if half == 0 else LOW(1.0) - left
            scores = dot_back(query * mask, keys) + allowed
            top = jnp.max(scores, axis=-1, keepdims=True)
            weights = jnp.exp(scores - top)
            total = jnp.sum(weights, axis=-1, keepdims=True)
            prob = (weights * (1.0 / total)).astype(LOW)
            probs[pair * 4 + half * 2 + seq, inside, :] = prob
            outs.append(dot(prob, values))
        context[here, pl.ds(pl.multiple_of(pair * 128, 128), 128)] = jnp.where(
            lane < HEAD_DIM, outs[0], outs[1]
        ).astype(LOW)

    each(ROWS // tile, body)


def second_phase(tokens, context, wout, params, middle, second):
    gain = params[2:3, :]
    shift = params[3:4, :]

    def body(i):
        here = rows_at(i, TILE)
        value = tokens[here, :].astype(F32) + dot(context[here, :], wout[...])
        middle[here, :] = value
        normal, _, _ = normalize(value, gain, shift)
        second[here, :] = normal.astype(LOW)

    each(ROWS // TILE, body)


def turn_phase(src, dst):
    def body(i):
        here = rows_at(i, 256)
        dst[:, here] = src[here, :].T

    each(ROWS // 256, body)


def feed_phase(
    chunk, second, second_t, out_grad, out_grad_t, up, down, active, hidden_grad,
    result, second_grad, g_up, g_down,
):
    units = rows_at(chunk, CHUNK)

    def body(i):
        here = rows_at(i, TILE)
        hidden = dot_back(second[here, :], up[units, :])
        switch = 0.5 * jnp.tanh(0.851 * hidden) + 0.5
        act = (hidden * switch).astype(LOW)
        active[here, :] = act
        grad = dot_back(out_grad[here, :], down[units, :])
        back = (grad * (switch + 1.702 * hidden * switch * (1.0 - switch))).astype(LOW)
        hidden_grad[here, :] = back
        result[here, :] += dot(act, down[units, :])
        second_grad[here, :] += dot(back, up[units, :])

    each(ROWS // TILE, body)

    def grads(c):
        here = rows_at(c, 256)
        for turned, wide, out in ((out_grad_t, active, g_down), (second_t, hidden_grad, g_up)):
            grad = dot(turned[here, :], wide[...]).astype(LOW)
            for j in range(CHUNK // 128):
                out[chunk * 8 + j * 2 + c] = grad[:, j * 128 : j * 128 + 128]

    each(2, grads)


def middle_phase(
    params, middle, result, second_grad, out_grad, wout,
    layer_out, middle_grad, attended_low, context_grad, norms,
):
    gain = params[2:3, :]

    def body(i, sums):
        here = rows_at(i, TILE)
        value = middle[here, :]
        layer_out[here, :] = (value + result[here, :]).astype(LOW)
        _, plain, factor = normalize(value, gain, gain)
        upper = second_grad[here, :]
        lower, gains, shifts = normalize_back(upper, plain, factor, gain)
        total = out_grad[here, :].astype(F32) + lower
        middle_grad[here, :] = total
        low = total.astype(LOW)
        attended_low[here, :] = low
        context_grad[here, :] = dot_back(low, wout[...]).astype(LOW)
        return (sums[0] + gains[None], sums[1] + shifts[None])

    zero = jnp.zeros((1, 512), F32)
    sums = lax.fori_loop(0, ROWS // TILE, body, (zero, zero))
    norms[2:3, :] = sums[0]
    norms[3:4, :] = sums[1]


def out_phase(attended_t, context, g_attend):
    def body(i):
        grad = dot(attended_t[rows_at(i, 256), :], context[...]).astype(LOW)
        for j in range(4):
            for p in range(PAIRS):
                g_attend[i * 16 + j * 4 + p, :, 384:512] = grad[
                    j * 64 : j * 64 + 64, p * 128 : p * 128 + 128
                ]

    each(2, body)


def attend_back_phase(pair, mixed, probs, context_grad, pair_grad):
    lane = lax.broadcasted_iota(jnp.int32, (1, 128), 1)
    left = (lane < HEAD_DIM).astype(LOW)
    scale = HEAD_DIM ** (-0.5)

    def body(seq):
        here = rows_at(seq, SEQ)
        query = mixed[pair, here, 0:128]
        keys = mixed[pair, here, 128:256]
        values = mixed[pair, here, 256:384]
        upper = context_grad[here, pl.ds(pl.multiple_of(pair * 128, 128), 128)]
        outs = []
        for half in range(2):
            mask = left if half == 0 else LOW(1.0) - left
            above = upper * mask
            prob_low = probs[pair * 4 + half * 2 + seq]
            prob = prob_low.astype(F32)
            prob_grad = dot_back(above, values)
            inner = jnp.sum(prob * prob_grad, axis=-1, keepdims=True)
            score_grad = (prob * (prob_grad - inner)).astype(LOW)
            outs.append(
                (
                    dot(score_grad, keys),
                    dot_rows(score_grad, query),
                    dot_rows(prob_low, above),
                )
            )
        pick = lane < HEAD_DIM
        pair_grad[here, 0:128] = (jnp.where(pick, outs[0][0], outs[1][0]) * scale).astype(LOW)
        pair_grad[here, 128:256] = (jnp.where(pick, outs[0][1], outs[1][1]) * scale).astype(LOW)
        pair_grad[here, 256:384] = (outs[0][2] + outs[1][2]).astype(LOW)

    each(ROWS // SEQ, body)


def qkv_phase(pair, pair_grad, first_t, wqkv, g_attend, first_grad):
    def body(i):
        here = rows_at(i, TILE)
        first_grad[here, :] += dot_back(pair_grad[here, :], wqkv[pair])

    each(ROWS // TILE, body)

    def grads(i):
        grad = dot(first_t[rows_at(i, 256), :], pair_grad[...]).astype(LOW)
        for j in range(4):
            g_attend[i * 16 + j * 4 + pair, :, 0:384] = grad[j * 64 : j * 64 + 64, :]

    each(2, grads)


def input_phase(params, tokens, first_grad, input_grad, norms):
    gain = params[0:1, :]

    def body(i, sums):
        here = rows_at(i, TILE)
        _, plain, factor = normalize(tokens[here, :].astype(F32), gain, gain)
        lower, gains, shifts = normalize_back(first_grad[here, :], plain, factor, gain)
        input_grad[here, :] += lower
        return (sums[0] + gains[None], sums[1] + shifts[None])

    zero = jnp.zeros((1, 512), F32)
    sums = lax.fori_loop(0, ROWS // TILE, body, (zero, zero))
    norms[0:1, :] = sums[0]
    norms[1:2, :] = sums[1]


def local_call(kernel, outs, scratch, args, name):
    vmem = pl.BlockSpec(memory_space=pltpu.VMEM)
    return pl.pallas_call(
        kernel,
        out_shape=tuple(jax.ShapeDtypeStruct(*o) for o in outs),
        in_specs=[vmem] * len(args),
        out_specs=(vmem,) * len(outs),
        scratch_shapes=[pltpu.VMEM(*v) for v in scratch],
        compiler_params=pltpu.CompilerParams(vmem_limit_bytes=60 << 20),
        name=name,
    )(*args)


STEP_DIMS = {"c": 1, "x": 2, "y": 4, "l": 8, "g": 16}
GATHER_UP = ("g", "l", "y", "x", "c")
GATHER_DOWN = ("l", "g", "x", "y", "c")
STARTS = (("g", "l", "y", "x", "c"), ("g", "x", "l", "y", "c"), ("g", "y", "x", "l", "c"))
ATTEND_ORDER = ("c", "x", "y", "l", "g")


def coordinates():
    dp = lax.axis_index("dp")
    head = lax.axis_index("head")
    bits = {
        "c": head % 2,
        "x": head // 2,
        "y": dp % 2,
        "l": (dp // 2) % 2,
        "g": dp // 4,
    }
    steps = {"c": (0, 1), "x": (0, 2), "y": (1, 0), "l": (2, 0), "g": (4, 0)}
    peers = {}
    for name, (along_dp, along_head) in steps.items():
        turn = 1 - 2 * bits[name]
        peers[name] = (dp + along_dp * turn, head + along_head * turn)
    return dp, head, bits, peers


def remote(src, dst, send_sem, recv_sem, peer):
    return pltpu.make_async_remote_copy(
        src_ref=src,
        dst_ref=dst,
        send_sem=send_sem,
        recv_sem=recv_sem,
        device_id=peer,
        device_id_type=pl.DeviceIdType.MESH,
    )


def tile_of(fixed, free, place):
    total = 0
    for name, bit in fixed.items():
        total = total + STEP_DIMS[name] * bit
    for i, name in enumerate(free):
        total = total + STEP_DIMS[name] * ((place // 2**i) % 2)
    return total


def scatter_start(acc, got, base, fixed, name, free, bits, peer, sems, slot):
    for place in range(2 ** len(free)):
        away = tile_of({**fixed, name: 1 - bits[name]}, free, place)
        remote(
            acc.at[away], got.at[base + place], sems[0].at[slot], sems[1].at[slot], peer
        ).start()


def scatter_end(acc, got, base, fixed, name, free, bits, peer, sems, slot):
    count = 2 ** len(free)
    span = got.at[pl.ds(base, count)]
    remote(span, span, sems[0].at[slot], sems[1].at[slot], peer).wait()
    rows = acc.shape[1]

    def body(i):
        here = tile_of({**fixed, name: bits[name]}, free, i)
        acc[here] = (acc[here].astype(F32) + got[base + i].astype(F32)).astype(LOW)

    each(count, body)


def gather_start(ref, rows, done, name, bits, peer, sems, slot):
    fixed = {d: bits[d] for d in STEP_DIMS if d not in done}
    for place in range(2 ** len(done)):
        tile = tile_of(fixed, done, place)
        if rows:
            part = ref.at[pl.ds(pl.multiple_of(tile * rows, rows), rows)]
        else:
            part = ref.at[tile]
        remote(part, part, sems[0].at[slot], sems[1].at[slot], peer).start()


def gather_end(ref, rows, done, peer, sems, slot):
    span = ref.at[pl.ds(0, 2 ** len(done) * (rows or 1))]
    remote(span, span, sems[0].at[slot], sems[1].at[slot], peer).wait()


def paired(block):
    parts = [block[:, i * 64 : i * 64 + 64] for i in (0, 3, 1, 4, 2, 5)]
    return jnp.concatenate(parts, axis=1)


def unpaired(block):
    parts = [block[:, i * 64 : i * 64 + 64] for i in (0, 2, 4, 1, 3, 5)]
    return jnp.concatenate(parts, axis=1)


def layer_kernel(
    tokens, seg_col, seg_row, out_grad, params, w_qkv, m_qkv, w_out, m_out, w_up, m_up, w_down, m_down,
    layer_out, input_grad, start_a, start_u, start_d, ortho_q, ortho_o, ortho_u, ortho_d, norm_sum, scal,
    first, mixed, context, bias, wqkv, wout, wup, wdown, pool, middle, second, second_t, out_grad_t,
    active, hidden_grad, result, second_grad, pair_grad, acc_a, acc_u, acc_d, got_a, got_u, got_d,
    mom_t, mom_x, mom_u, mom_d, mom_a, norm_now, norm_got, stat_got, gram, mix, send, recv,
):
    dp, head, bits, peers = coordinates()
    me = dp * 4 + head
    sems = (send, recv)
    across = (dp, 3 - head)
    S_Q, S_O, S_M, S_UP, S_DOWN, S_CHUNK, S_LG, S_A, S_NORM, S_STAT, S_START, S_ORTHO = (
        0, 4, 8, 10, 15, 20, 44, 48, 53, 58, 59, 74
    )
    barrier = pltpu.get_barrier_semaphore()

    def greet(i):
        other = (me + 1 + i) % 32
        pl.semaphore_signal(
            barrier, inc=1, device_id=(other // 4, other % 4), device_id_type=pl.DeviceIdType.MESH
        )

    each(31, greet)
    wqkv[head] = paired(w_qkv[...].astype(LOW))
    wout[pl.ds(pl.multiple_of(head * 128, 128), 128), :] = w_out[...].astype(LOW)
    mine = pl.ds(pl.multiple_of(me * 64, 64), 64)
    wup[mine, :] = w_up[...].astype(LOW)
    wdown[mine, :] = w_down[...].astype(LOW)
    pl.semaphore_wait(barrier, 31)

    def block_q(who):
        return wqkv.at[who]

    def block_o(who):
        return wout.at[pl.ds(pl.multiple_of(who * 128, 128), 128)]

    def weight_copy(block, who, slot, peer):
        return remote(block(who), block(who), send.at[slot], recv.at[slot], peer)

    sibling = peers["c"]
    weight_copy(block_q, head, S_Q + 1, sibling).start()
    weight_copy(block_q, head, S_Q + 2, peers["x"]).start()
    gather_start(wup, 64, (), GATHER_UP[0], bits, peers[GATHER_UP[0]], sems, S_UP)
    gather_start(wdown, 64, (), GATHER_DOWN[0], bits, peers[GATHER_DOWN[0]], sems, S_DOWN)
    weight_copy(block_o, head, S_O + 1, sibling).start()
    weight_copy(block_o, head, S_O + 2, peers["x"]).start()
    other_half = pl.ds(pl.multiple_of((1 - bits["c"]) * 256, 256), 256)

    def moment_copy(i, ref):
        return remote(ref.at[:, other_half], mom_x.at[i], send.at[S_M + i], recv.at[S_M + i], sibling)

    moment_copy(0, m_up).start()
    moment_copy(1, m_down).start()

    def weight_step(k):
        for ref, order, slot in ((wup, GATHER_UP, S_UP), (wdown, GATHER_DOWN, S_DOWN)):
            gather_end(ref, 64, order[:k], peers[order[k]], sems, slot + k)
            if k < 4:
                gather_start(
                    ref, 64, order[: k + 1], order[k + 1], bits, peers[order[k + 1]], sems, slot + k + 1
                )

    first_phase(tokens, params, first)
    bias_phase(seg_col, seg_row, bias)
    weight_step(0)
    turn_phase(out_grad, out_grad_t)

    def pair_body(j):
        pair = (bits["c"] + j % 2) % 2 + 2 * ((bits["x"] + j // 2) % 2)
        mixed_phase(pair, first, wqkv, mixed)
        attend_phase(pair, mixed, bias, pool, context)

        @pl.when(j == 0)
        def _():
            weight_step(1)
            weight_copy(block_q, head, S_Q + 1, sibling).wait()
            weight_copy(block_o, head, S_O + 1, sibling).wait()
            weight_copy(block_q, head, S_Q + 2, peers["x"]).wait()
            weight_copy(block_q, peers["x"][1], S_Q + 3, sibling).start()
            weight_copy(block_o, head, S_O + 2, peers["x"]).wait()
            weight_copy(block_o, peers["x"][1], S_O + 3, sibling).start()

        @pl.when(j == 1)
        def _():
            weight_step(2)

        @pl.when(j == 2)
        def _():
            weight_copy(block_q, head, S_Q + 3, sibling).wait()
            weight_copy(block_o, head, S_O + 3, sibling).wait()

    each(PAIRS, pair_body)
    second_phase(tokens, context, wout, params, middle, second)
    weight_step(3)
    turn_phase(second, second_t)
    result[...] = jnp.zeros_like(result)
    second_grad[...] = jnp.zeros_like(second_grad)
    weight_step(4)

    chunk_orders = ((acc_u, got_u, ("c", "x", "y")), (acc_d, got_d, ("c", "y", "x")))

    def chunk_args(q, k, order):
        fixed = {"g": q // 2, "l": q % 2}
        for name in order[:k]:
            fixed[name] = bits[name]
        return fixed, order[k], order[k + 1 :]

    def chunk_start(q, k):
        for i, (acc, got, order) in enumerate(chunk_orders):
            fixed, name, free = chunk_args(q, k, order)
            scatter_start(
                acc, got, q * 7 + (0, 4, 6)[k], fixed, name, free, bits, peers[name], sems,
                S_CHUNK + q * 6 + i * 3 + k,
            )

    def chunk_end(q, k):
        for i, (acc, got, order) in enumerate(chunk_orders):
            fixed, name, free = chunk_args(q, k, order)
            scatter_end(
                acc, got, q * 7 + (0, 4, 6)[k], fixed, name, free, bits, peers[name], sems,
                S_CHUNK + q * 6 + i * 3 + k,
            )

    def feed_body(q):
        feed_phase(
            q, second, second_t, out_grad, out_grad_t, wup, wdown, active, hidden_grad,
            result, second_grad, acc_u, acc_d,
        )
        chunk_start(q, 0)

        @pl.when(q >= 1)
        def _():
            chunk_end(q - 1, 0)
            chunk_start(q - 1, 1)

        @pl.when(q >= 2)
        def _():
            chunk_end(q - 2, 1)
            chunk_start(q - 2, 2)

        @pl.when(q >= 3)
        def _():
            chunk_end(q - 3, 2)

    each(WIDE // CHUNK, feed_body)
    chunk_end(3, 0)
    chunk_start(3, 1)
    middle_phase(
        params, middle, result, second_grad, out_grad, wout,
        layer_out, input_grad, second, active, norm_now.at[0],
    )
    chunk_end(2, 1)
    chunk_start(2, 2)
    turn_phase(second, second_t)
    out_phase(second_t, context, acc_a)
    chunk_end(1, 2)
    chunk_end(3, 1)
    chunk_start(3, 2)
    turn_phase(first, second_t)
    result[...] = jnp.zeros_like(result)

    def last_args(k):
        fixed = {"c": bits["c"], "x": bits["x"], "y": bits["y"]}
        if k == 1:
            fixed["l"] = bits["l"]
            return fixed, "g", ()
        return fixed, "l", ("g",)

    def last_step(k, ending):
        for i, (acc, got, _) in enumerate(chunk_orders):
            fixed, name, free = last_args(k)
            (scatter_end if ending else scatter_start)(
                acc, got, 28 + 2 * k, fixed, name, free, bits, peers[name], sems, S_LG + 2 * k + i
            )

    def back_body(pair):
        attend_back_phase(pair, mixed, pool, active, pair_grad)
        qkv_phase(pair, pair_grad, second_t, wqkv, acc_a, result)

        @pl.when(pair == 0)
        def _():
            chunk_end(2, 2)
            chunk_end(3, 2)
            last_step(0, False)

        @pl.when(pair == 1)
        def _():
            last_step(0, True)
            last_step(1, False)

        @pl.when(pair == 2)
        def _():
            last_step(1, True)

    each(PAIRS, back_body)

    def attend_args(k):
        order = ATTEND_ORDER
        return {d: bits[d] for d in order[:k]}, order[k], order[k + 1 :]

    def norm_copy(k):
        return remote(
            norm_now.at[k], norm_got.at[k], send.at[S_NORM + k], recv.at[S_NORM + k],
            peers[ATTEND_ORDER[k]],
        )

    for k in range(5):
        fixed, name, free = attend_args(k)
        base = 32 - 2 ** (5 - k)
        scatter_start(acc_a, got_a, base, fixed, name, free, bits, peers[name], sems, S_A + k)
        if k == 0:
            input_phase(params, tokens, result, input_grad, norm_now.at[0])
            moment_copy(0, m_up).wait()
            moment_copy(1, m_down).wait()
            keep = pl.ds(pl.multiple_of(bits["c"] * 256, 256), 256)
            for i, (ref, out) in enumerate(((m_up, mom_u), (m_down, mom_d))):
                own = ref[:, keep]
                far = mom_x[i]
                low_half = jnp.where(bits["c"] == 0, own, far)
                high_half = jnp.where(bits["c"] == 0, far, own)
                out[...] = jnp.concatenate([low_half, high_half], axis=0).T
            mom_t[...] = m_out[...].T
            here = pl.ds(pl.multiple_of(dp * 64, 64), 64)
            mom_a[:, 0:384] = paired(m_qkv[here, :])
            mom_a[:, 384:512] = mom_t[here, :]
        norm_copy(k).start()
        scatter_end(acc_a, got_a, base, fixed, name, free, bits, peers[name], sems, S_A + k)
        norm_copy(k).wait()
        norm_now[k + 1] = norm_now[k] + norm_got[k]

    def total_of(value):
        return jnp.sum(jnp.sum(value, axis=0, keepdims=True), axis=1, keepdims=True)

    lane = lax.broadcasted_iota(jnp.int32, (8, 128), 1)
    column = lax.broadcasted_iota(jnp.int32, (1, 512), 1)
    grad_a = acc_a[me].astype(F32)
    grad_u = acc_u[me].astype(F32)
    grad_d = acc_d[me].astype(F32)
    stats = jnp.zeros((8, 128), F32)
    products = []
    for moment, grad in ((mom_a[...], grad_a), (mom_u[...], grad_u), (mom_d[...], grad_d)):
        products.append((moment * moment, moment * grad, grad * grad))
    for i in range(3):
        inside = column < 384
        stats = jnp.where(lane == i, total_of(jnp.where(inside, products[0][i], 0.0)), stats)
        stats = jnp.where(lane == 3 + i, total_of(jnp.where(inside, 0.0, products[0][i])), stats)
        stats = jnp.where(lane == 6 + i, total_of(products[1][i]), stats)
        stats = jnp.where(lane == 9 + i, total_of(products[2][i]), stats)
    stat_got[me] = stats

    def tell(i):
        other = (me + 1 + i) % 32
        remote(
            stat_got.at[me], stat_got.at[me], send.at[S_STAT], recv.at[S_STAT], (other // 4, other % 4)
        ).start()

    each(31, tell)
    span = stat_got.at[pl.ds(0, 31)]
    remote(span, span, send.at[S_STAT], recv.at[S_STAT], sibling).wait()
    stats = jnp.sum(stat_got[...], axis=0)

    def stat(i):
        return jnp.sum(jnp.where(lane == i, stats, 0.0), axis=1, keepdims=True)[0:1]

    vector = norm_now[5]
    norm_sum[...] = vector
    norm = jnp.sqrt(stat(2) + stat(5) + stat(8) + stat(11) + total_of(vector * vector))
    clip = jnp.minimum(1.0, 1.0 / (norm + 1e-06))
    sizes = []
    for m in range(4):
        square = (
            momentum_decay * momentum_decay * stat(3 * m)
            + 2.0 * momentum_decay * clip * stat(3 * m + 1)
            + clip * clip * stat(3 * m + 2)
        )
        sizes.append(jnp.sqrt(jnp.maximum(square, 0.0)) + 1e-07)
    told = jnp.where(lane == 0, norm, clip)
    for m in range(4):
        told = jnp.where(lane == 2 + m, sizes[m], told)
    scal[...] = told
    scale_a = jnp.where(column < 384, 1.0 / sizes[0], 1.0 / sizes[1])
    got_a[me] = ((momentum_decay * mom_a[...] + clip * grad_a) * scale_a).astype(LOW)
    got_u[me] = ((momentum_decay * mom_u[...] + clip * grad_u) * (1.0 / sizes[2])).astype(LOW)
    got_d[me] = ((momentum_decay * mom_d[...] + clip * grad_d) * (1.0 / sizes[3])).astype(LOW)

    starts = (got_a, got_u, got_d)
    for k in range(5):
        for m in range(3):
            order = STARTS[m]
            gather_start(
                starts[m], 0, order[:k], order[k], bits, peers[order[k]], sems, S_START + 3 * k + m
            )
        for m in range(3):
            order = STARTS[m]
            gather_end(starts[m], 0, order[:k], peers[order[k]], sems, S_START + 3 * k + m)

    @pl.when(head < 2)
    def _():
        wanted = jnp.where(head == 0, 1.0, 0.0)
        here_only = jnp.where(column < 384, wanted, 1.0 - wanted).astype(LOW)

        def body(i):
            rows = pl.ds(pl.multiple_of((i // 4) * 64, 64), 64)
            pool[i % 4, rows, :] = got_a[i] * here_only

        each(32, body)

    for kind, got in ((2, got_u), (3, got_d)):
        @pl.when(head == kind)
        def _(got=got):
            def body(i):
                for j in range(4):
                    for c in range(2):
                        pool[i, c * 256 : c * 256 + 256, j * 128 : j * 128 + 128] = got[i * 8 + j * 2 + c]

            each(4, body)

    def slice_body(i):
        rows = pl.ds(pl.multiple_of(i * 64, 64), 64)
        start_a[rows, :] = got_a[i * 4 + head]

    each(8, slice_body)
    left = me - bits["c"]
    for c in range(2):
        start_u[c * 256 : c * 256 + 256, :] = got_u[left + c]
        start_d[c * 256 : c * 256 + 256, :] = got_d[left + c]

    def turn_body(turn):
        now = (turn % 2) * 4
        later = 4 - now

        def gram_body(i):
            rows = rows_at(i, TILE)
            total = dot_back(pool[now, rows, :], pool[now])
            for b in range(1, 4):
                total = total + dot_back(pool[now + b, rows, :], pool[now + b])
            gram[rows, :] = total.astype(LOW)

        each(512 // TILE, gram_body)

        def mix_body(i):
            rows = rows_at(i, TILE)
            own = gram[rows, :]
            mix[rows, :] = (ns_b * own.astype(F32) + ns_c * dot(own, gram[...])).astype(LOW)

        each(512 // TILE, mix_body)

        def next_body(b):
            value = pool[now + b]
            pool[later + b] = (ns_a * value.astype(F32) + dot(mix[...], value)).astype(LOW)

        each(4, next_body)

    each(NS_STEPS, turn_body)
    last = (NS_STEPS % 2) * 4
    outs = (ortho_q, ortho_o, ortho_u, ortho_d)

    def piece(kind, who):
        if kind == 0:
            return pool.at[last + who, :, pl.ds(0, 384)]
        if kind == 1:
            return pool.at[last + who, :, pl.ds(384, 128)]
        block = dp * 2 + who // 2
        return pool.at[last + block // 4, :, pl.ds(pl.multiple_of((block % 4) * 128, 128), 128)]

    partners = (peers["c"], peers["x"], across)
    for kind in range(4):
        @pl.when(head == kind)
        def _(kind=kind):
            for j, partner in enumerate(partners):
                remote(
                    piece(kind, partner[1]), outs[kind], send.at[S_ORTHO + j], recv.at[S_ORTHO + kind], partner
                ).start()
            outs[kind][...] = piece(kind, head)[...]
            for j, partner in enumerate(partners):
                remote(
                    piece(kind, partner[1]), outs[kind], send.at[S_ORTHO + j], recv.at[S_ORTHO + kind], partner
                ).wait_send()

    for kind in range(4):
        @pl.when(head != kind)
        def _(kind=kind):
            remote(
                piece(kind, head), outs[kind], send.at[S_ORTHO], recv.at[S_ORTHO + kind], sibling
            ).wait_recv()


def layer_call(*args):
    shape = jax.ShapeDtypeStruct
    vmem = pl.BlockSpec(memory_space=pltpu.VMEM)
    outs = (
        shape((ROWS, 512), LOW), shape((ROWS, 512), F32),
        shape((512, 512), LOW), shape((512, 128), LOW), shape((512, 128), LOW),
        shape((512, 384), LOW), shape((512, 128), LOW), shape((512, 128), LOW), shape((512, 128), LOW),
        shape((4, 512), F32), shape((8, 128), F32),
    )
    scratch = [
        ((ROWS, 512), LOW),
        ((PAIRS, ROWS, 384), LOW),
        ((ROWS, 512), LOW),
        ((ROWS, SEQ), LOW),
        ((PAIRS, 512, 384), LOW),
        ((512, 512), LOW),
        ((WIDE, 512), LOW),
        ((WIDE, 512), LOW),
        ((16, 512, 512), LOW),
        ((ROWS, 512), F32),
        ((ROWS, 512), LOW),
        ((512, ROWS), LOW),
        ((512, ROWS), LOW),
        ((ROWS, CHUNK), LOW),
        ((ROWS, CHUNK), LOW),
        ((ROWS, 512), F32),
        ((ROWS, 512), F32),
        ((ROWS, 384), LOW),
        ((32, 64, 512), LOW),
        ((32, 256, 128), LOW),
        ((32, 256, 128), LOW),
        ((32, 64, 512), LOW),
        ((32, 256, 128), LOW),
        ((32, 256, 128), LOW),
        ((512, 128), F32),
        ((2, 64, 256), F32),
        ((256, 128), F32),
        ((256, 128), F32),
        ((64, 512), F32),
        ((6, 4, 512), F32),
        ((5, 4, 512), F32),
        ((32, 8, 128), F32),
        ((512, 512), LOW),
        ((512, 512), LOW),
    ]
    return pl.pallas_call(
        layer_kernel,
        out_shape=outs,
        in_specs=[vmem] * len(args),
        out_specs=(vmem,) * len(outs),
        scratch_shapes=[pltpu.VMEM(*v) for v in scratch]
        + [pltpu.SemaphoreType.DMA((80,)), pltpu.SemaphoreType.DMA((80,))],
        compiler_params=pltpu.CompilerParams(
            collective_id=1, has_side_effects=True, vmem_limit_bytes=VMEM_BYTES
        ),
        name="layer",
    )(*args)


def update_kernel(
    start_a, start_u, start_d, ortho_q, ortho_o, ortho_u, ortho_d, norm_sum, scal,
    w_qkv, w_out, w_up, w_down, norm_first, norm_second,
    new_q, mom_q, new_o, mom_o, new_u, mom_u, new_d, mom_d, clipped, first_new, second_new,
):
    core = lax.axis_index("head") % 2
    clip = scal[0:1, 1:2]
    keep = 1.0 - muon_rate * muon_decay

    def fresh(weight, factor, ortho):
        return weight * keep - muon_rate * factor * ortho

    new_q[...] = fresh(w_qkv[...], math.sqrt(3.0), unpaired(ortho_q[...].astype(F32)))
    mom_q[...] = unpaired(start_a[:, 0:384].astype(F32)) * scal[0:1, 2:3]
    new_o[...] = fresh(w_out[...], math.sqrt(SEQ / 8.0), ortho_o[...].astype(F32).T)
    mom_o[...] = start_a[:, 384:512].astype(F32).T * scal[0:1, 3:4]
    for weight, ortho, start, new, mom, i in (
        (w_up, ortho_u, start_u, new_u, mom_u, 4),
        (w_down, ortho_d, start_d, new_d, mom_d, 5),
    ):
        turned = ortho[...].astype(F32).T
        turned = jnp.where(core == 0, turned[0:64], turned[64:128])
        new[...] = fresh(weight[...], math.sqrt(max(1.0, FF / 512)), turned)
        turned = start[...].astype(F32).T
        mom[...] = jnp.where(core == 0, turned[0:64], turned[64:128]) * scal[0:1, i : i + 1]
    clip_grad = clip * norm_sum[...]
    clipped[...] = clip_grad
    first_new[...] = beta_one * norm_first[...] + (1.0 - beta_one) * clip_grad
    second_new[...] = beta_two * norm_second[...] + (1.0 - beta_two) * clip_grad * clip_grad


def fast_shards(
    tokens,
    segments,
    out_grad,
    norm_params,
    norm_first,
    norm_second,
    qkv_weight,
    qkv_moment,
    out_weight,
    out_moment,
    up_weight,
    up_moment,
    down_weight,
    down_moment,
):
    seg = lax.dynamic_slice_in_dim(segments, lax.axis_index("head") * ROWS, ROWS, 0)
    (
        layer_out, input_grad, start_a, start_u, start_d, ortho_q, ortho_o, ortho_u, ortho_d, norm_sum, scal
    ) = layer_call(
        tokens, seg[:, None], seg.reshape(ROWS // SEQ, SEQ), out_grad, norm_params,
        qkv_weight, qkv_moment, out_weight, out_moment,
        up_weight.T, up_moment.T, down_weight.T, down_moment.T,
    )
    tall = ((64, 512), F32)
    new_q, mom_q, new_o, mom_o, new_u, mom_u, new_d, mom_d, clipped, first_new, second_new = local_call(
        update_kernel,
        [((512, 384), F32)] * 2 + [((128, 512), F32)] * 2 + [tall] * 4 + [((4, 512), F32)] * 3,
        [],
        (
            start_a, start_u, start_d, ortho_q, ortho_o, ortho_u, ortho_d, norm_sum, scal,
            qkv_weight, out_weight, up_weight.T, down_weight.T, norm_first, norm_second,
        ),
        "update",
    )
    return (
        layer_out, input_grad, scal[0, 0], clipped, first_new, second_new,
        new_q, mom_q, new_o, mom_o, new_u.T, mom_u.T, new_d.T, mom_d.T,
    )


def general_update(
    whole_qkv, whole_out, up_grad, down_grad, vector_part,
    qkv_moment, out_moment, up_moment, down_moment,
):
    everywhere = ("dp", "head")
    narrow = out_moment.shape[0]
    up_part, down_part = (
        lax.psum_scatter(
            up_grad.astype(jnp.bfloat16), everywhere, scatter_dimension=1, tiled=True
        ).astype(jnp.float32),
        lax.psum_scatter(
            down_grad.astype(jnp.bfloat16), everywhere, scatter_dimension=1, tiled=True
        ).astype(jnp.float32),
    )
    qkv_part = lax.psum_scatter(
        whole_qkv.astype(jnp.bfloat16), "head", scatter_dimension=1, tiled=True
    )
    out_part = lax.psum_scatter(
        whole_out.astype(jnp.bfloat16), "head", scatter_dimension=0, tiled=True
    )
    qkv_sum, out_sum = (
        lax.psum(qkv_part, "dp").astype(jnp.float32),
        lax.psum(out_part, "dp").astype(jnp.float32),
    )
    leading = (lax.axis_index("dp") == 0).astype(jnp.float32)
    moments = [qkv_moment, out_moment, up_moment, down_moment]
    grads = [qkv_sum, out_sum, up_part, down_part]
    stats = jnp.stack(
        [
            squares_of(qkv_moment, qkv_sum, leading),
            squares_of(out_moment, out_sum, leading),
            squares_of(up_moment, up_part, 1.0),
            squares_of(down_moment, down_part, 1.0),
        ]
    )
    vector_sum, stat_sum = lax.psum((vector_part, stats), everywhere)
    grad_norm = jnp.sqrt(jnp.sum(stat_sum[:, 2]) + jnp.sum(vector_sum * vector_sum))
    clip = jnp.minimum(1.0, 1.0 / (grad_norm + 1e-06))
    sizes = jnp.sqrt(
        momentum_decay * momentum_decay * stat_sum[:, 0]
        + 2.0 * momentum_decay * clip * stat_sum[:, 1]
        + clip * clip * stat_sum[:, 2]
    )
    new_moments = [momentum_decay * moments[index] + clip * grads[index] for index in range(4)]
    starts = [
        (new_moments[index] / (sizes[index] + 1e-07)).astype(jnp.bfloat16) for index in range(4)
    ]
    blocks = [
        lax.all_gather(starts[0], "head", axis=1, tiled=True),
        lax.all_gather(starts[1], "head", axis=0, tiled=True),
        lax.all_gather(starts[2], everywhere, axis=1, tiled=True),
        lax.all_gather(starts[3], everywhere, axis=1, tiled=True),
    ]
    for turn in range(NS_STEPS):
        updated = []
        for index in range(4):
            form = gram_right if index == 1 else gram_left
            gram = form(blocks[index]).astype(jnp.bfloat16)
            mix = (
                ns_b * gram.astype(jnp.float32)
                + ns_c * jnp.dot(gram, gram, preferred_element_type=jnp.float32)
            ).astype(jnp.bfloat16)
            if index == 1:
                product = jnp.dot(blocks[index], mix, preferred_element_type=jnp.float32)
            else:
                product = jnp.dot(mix, blocks[index], preferred_element_type=jnp.float32)
            updated.append(
                (ns_a * blocks[index].astype(jnp.float32) + product).astype(jnp.bfloat16)
            )
        blocks = updated
    share = up_moment.shape[1]
    along = lax.axis_index("head")
    offset = (lax.axis_index("dp") * lax.axis_size("head") + along) * share
    owned = [
        lax.dynamic_slice_in_dim(blocks[0], along * qkv_moment.shape[1], qkv_moment.shape[1], 1),
        lax.dynamic_slice_in_dim(blocks[1], along * narrow, narrow, 0),
        lax.dynamic_slice_in_dim(blocks[2], offset, share, 1),
        lax.dynamic_slice_in_dim(blocks[3], offset, share, 1),
    ]
    return (owned, new_moments, vector_sum, grad_norm, clip)


def general_shards(
    tokens,
    segments,
    out_grad,
    norm_params,
    norm_first,
    norm_second,
    qkv_weight,
    qkv_moment,
    out_weight,
    out_moment,
    up_weight,
    up_moment,
    down_weight,
    down_moment,
):
    width = tokens.shape[1]
    rows = tokens.shape[0]
    narrow = out_weight.shape[0]
    sequences = rows // SEQ
    heads = width // HEAD_DIM
    everywhere = ("dp", "head")
    inputs = tokens.astype(jnp.float32)
    first, first_plain, first_factor = normalize(inputs, norm_params[0], norm_params[1])
    first_low = first.astype(jnp.bfloat16)
    qkv_full = lax.all_gather(qkv_weight.astype(jnp.bfloat16), "head", axis=1, tiled=True)
    out_full = lax.all_gather(out_weight.astype(jnp.bfloat16), "head", axis=0, tiled=True)
    up_all = lax.all_gather(up_weight.astype(jnp.bfloat16), everywhere, axis=1, tiled=True)
    down_all = lax.all_gather(down_weight.astype(jnp.bfloat16), everywhere, axis=1, tiled=True)
    mixed = jnp.dot(first_low, qkv_full, preferred_element_type=jnp.float32).astype(jnp.bfloat16)
    mixed = mixed.reshape(sequences, SEQ, heads, 3, HEAD_DIM)
    segment_rows = lax.dynamic_slice_in_dim(segments, lax.axis_index("head") * rows, rows, 0)
    segment_rows = segment_rows.reshape(sequences, SEQ)
    query = mixed[:, :, :, 0]
    keys = mixed[:, :, :, 1]
    values = mixed[:, :, :, 2]
    context, lse = lax.map(attend_forward, (query, keys, values, segment_rows))
    context = context.reshape(rows, width)
    attended = jnp.dot(context, out_full, preferred_element_type=jnp.float32)
    middle = inputs + attended
    second, second_plain, second_factor = normalize(middle, norm_params[2], norm_params[3])
    second_low = second.astype(jnp.bfloat16)
    hidden = jnp.dot(second_low, up_all, preferred_element_type=jnp.float32)
    switch = jax.nn.sigmoid(1.702 * hidden)
    active = (hidden * switch).astype(jnp.bfloat16)
    result = middle + lax.dot_general(
        active, down_all, (((1,), (1,)), ((), ())), preferred_element_type=jnp.float32
    )
    layer_out = result.astype(jnp.bfloat16)
    down_grad = lax.dot_general(
        out_grad, active, (((0,), (0,)), ((), ())), preferred_element_type=jnp.float32
    )
    active_grad = jnp.dot(out_grad, down_all, preferred_element_type=jnp.float32)
    hidden_grad = (active_grad * (switch + 1.702 * hidden * switch * (1.0 - switch))).astype(
        jnp.bfloat16
    )
    up_grad = lax.dot_general(
        second_low, hidden_grad, (((0,), (0,)), ((), ())), preferred_element_type=jnp.float32
    )
    second_grad = lax.dot_general(
        hidden_grad, up_all, (((1,), (1,)), ((), ())), preferred_element_type=jnp.float32
    )
    middle_lower, gain_two, shift_two = normalize_back(
        second_grad, second_plain, second_factor, norm_params[2]
    )
    middle_grad = out_grad.astype(jnp.float32) + middle_lower
    attended_low = middle_grad.astype(jnp.bfloat16)
    context_grad = lax.dot_general(
        attended_low, out_full, (((1,), (1,)), ((), ())), preferred_element_type=jnp.float32
    ).astype(jnp.bfloat16)
    whole_out = lax.dot_general(
        context, attended_low, (((0,), (0,)), ((), ())), preferred_element_type=jnp.float32
    )
    context_grad = context_grad.reshape(sequences, SEQ, heads, HEAD_DIM)
    mixed_grad = lax.map(attend_backward, (query, keys, values, segment_rows, context_grad, lse))
    mixed_grad = mixed_grad.reshape(rows, 3 * width)
    whole_qkv = lax.dot_general(
        first_low, mixed_grad, (((0,), (0,)), ((), ())), preferred_element_type=jnp.float32
    )
    first_grad = lax.dot_general(
        mixed_grad, qkv_full, (((1,), (1,)), ((), ())), preferred_element_type=jnp.float32
    )
    input_lower, gain_one, shift_one = normalize_back(
        first_grad, first_plain, first_factor, norm_params[0]
    )
    input_grad = middle_grad + input_lower
    vector_part = jnp.stack([gain_one, shift_one, gain_two, shift_two])
    (owned, new_moments, vector_sum, grad_norm, clip) = general_update(
        whole_qkv, whole_out, up_grad, down_grad, vector_part,
        qkv_moment, out_moment, up_moment, down_moment,
    )
    weights = [qkv_weight, out_weight, up_weight, down_weight]
    factors = [
        math.sqrt(3.0),
        math.sqrt(SEQ / 8.0),
        math.sqrt(max(1.0, FF / width)),
        math.sqrt(max(1.0, FF / width)),
    ]
    new_weights = [
        weights[index] * (1.0 - muon_rate * muon_decay)
        - muon_rate * factors[index] * owned[index].astype(jnp.float32)
        for index in range(4)
    ]
    clipped = clip * vector_sum
    first_new = beta_one * norm_first + (1.0 - beta_one) * clipped
    second_new = beta_two * norm_second + (1.0 - beta_two) * clipped * clipped
    return (
        layer_out,
        input_grad,
        grad_norm,
        clipped,
        first_new,
        second_new,
        new_weights[0],
        new_moments[0],
        new_weights[1],
        new_moments[1],
        new_weights[2],
        new_moments[2],
        new_weights[3],
        new_moments[3],
    )


def solution(mesh):
    placed = (
        P(("dp", "head"), None),
        P("dp"),
        P(("dp", "head"), None),
        P(),
        P(),
        P(),
        P(None, "head"),
        P(None, "head"),
        P("head", None),
        P("head", None),
        P(None, ("dp", "head")),
        P(None, ("dp", "head")),
        P(None, ("dp", "head")),
        P(None, ("dp", "head")),
    )
    fast = mesh.shape["dp"] == 8 and mesh.shape["head"] == 4
    return jax.shard_map(
        fast_shards if fast else general_shards,
        mesh=mesh,
        in_specs=placed,
        out_specs=(
            P(("dp", "head"), None),
            P(("dp", "head"), None),
            P(),
            P(),
            P(),
            P(),
            P(None, "head"),
            P(None, "head"),
            P("head", None),
            P("head", None),
            P(None, ("dp", "head")),
            P(None, ("dp", "head")),
            P(None, ("dp", "head")),
            P(None, ("dp", "head")),
        ),
        check_vma=False,
    )
```

```python
import math

import jax
import jax.numpy as jnp
from jax import lax
from jax.experimental import pallas as pl
from jax.experimental.pallas import tpu as pltpu
from jax.sharding import PartitionSpec as P

HEAD_DIM = 64
FF = 2048
SEQ = 512
NS_STEPS = 5


neg_fill = -1000000000.0
norm_eps = 1e-05
ns_a = 3.4445
ns_b = -4.775
ns_c = 2.0315
momentum_decay = 0.95
muon_rate = 0.5
muon_decay = 0.01
beta_one = 0.9
beta_two = 0.95


def normalize(values, gain, shift):
    mean = jnp.mean(values, axis=-1, keepdims=True)
    centered = values - mean
    factor = lax.rsqrt(jnp.mean(centered * centered, axis=-1, keepdims=True) + norm_eps)
    plain = centered * factor
    return (plain * gain + shift, plain, factor)


def normalize_back(upper, plain, factor, gain):
    inner = upper * gain
    lower = factor * (
        inner
        - jnp.mean(inner, axis=-1, keepdims=True)
        - plain * jnp.mean(inner * plain, axis=-1, keepdims=True)
    )
    return (lower, jnp.sum(upper * plain, axis=0), jnp.sum(upper, axis=0))


def masked_scores(query, keys, segment):
    scores = jnp.einsum(
        "qhd,khd->hqk", query, keys, preferred_element_type=jnp.float32
    ) * HEAD_DIM ** (-0.5)
    same = segment[:, None] == segment[None, :]
    return jnp.where(same[None], scores, neg_fill)


def attend_forward(block):
    query, keys, values, segment = block
    scores = masked_scores(query, keys, segment)
    top = jnp.max(scores, axis=-1, keepdims=True)
    weights = jnp.exp(scores - top)
    total = jnp.sum(weights, axis=-1, keepdims=True)
    probs = (weights / total).astype(jnp.bfloat16)
    context = jnp.einsum("hqk,khd->qhd", probs, values, preferred_element_type=jnp.float32)
    return (context.astype(jnp.bfloat16), top + jnp.log(total))


def attend_backward(block):
    query, keys, values, segment, context_grad, lse = block
    scores = masked_scores(query, keys, segment)
    probs = jnp.exp(scores - lse)
    probs_low = probs.astype(jnp.bfloat16)
    probs_grad = jnp.einsum(
        "qhd,khd->hqk", context_grad, values, preferred_element_type=jnp.float32
    )
    inner = jnp.sum(probs * probs_grad, axis=-1, keepdims=True)
    score_grad = (probs * (probs_grad - inner)).astype(jnp.bfloat16)
    query_grad = jnp.einsum(
        "hqk,khd->qhd", score_grad, keys, preferred_element_type=jnp.float32
    ) * HEAD_DIM ** (-0.5)
    key_grad = jnp.einsum(
        "hqk,qhd->khd", score_grad, query, preferred_element_type=jnp.float32
    ) * HEAD_DIM ** (-0.5)
    value_grad = jnp.einsum(
        "hqk,qhd->khd", probs_low, context_grad, preferred_element_type=jnp.float32
    )
    return jnp.stack([query_grad, key_grad, value_grad], axis=2).astype(jnp.bfloat16)


def gram_left(block):
    return lax.dot_general(
        block, block, (((1,), (1,)), ((), ())), preferred_element_type=jnp.float32
    )


def gram_right(block):
    return lax.dot_general(
        block, block, (((0,), (0,)), ((), ())), preferred_element_type=jnp.float32
    )


def squares_of(moment, grad, weight):
    return (
        jnp.stack([jnp.sum(moment * moment), jnp.sum(moment * grad), jnp.sum(grad * grad)]) * weight
    )


ROWS = 1024
TILE = 256
PAIRS = 4
WIDE = 2048
CHUNK = 512
VMEM_BYTES = 62 << 20
LOW = jnp.bfloat16
F32 = jnp.float32


def dot(one, two):
    return jnp.dot(one, two, preferred_element_type=F32)


def dot_back(one, two):
    return lax.dot_general(one, two, (((1,), (1,)), ((), ())), preferred_element_type=F32)


def dot_rows(one, two):
    return lax.dot_general(one, two, (((0,), (0,)), ((), ())), preferred_element_type=F32)


def each(count, body):
    def step(i, carry):
        body(i)
        return carry

    lax.fori_loop(0, count, step, 0)


def rows_at(i, size):
    return pl.ds(pl.multiple_of(i * size, size), size)


def first_phase(tokens, params, first):
    gain = params[0:1, :]
    shift = params[1:2, :]

    def body(i):
        here = rows_at(i, 128)
        plain_gain, _, _ = normalize(tokens[here, :].astype(F32), gain, shift)
        first[here, :] = plain_gain.astype(LOW)

    each(ROWS // 128, body)


def mixed_phase(pair, first, wqkv, mixed):
    def body(i):
        here = rows_at(i, TILE)
        mixed[pair, here, :] = dot(first[here, :], wqkv[pair]).astype(LOW)

    each(ROWS // TILE, body)


def bias_phase(segments, head, bias):
    turned = segments[...].astype(F32).T
    lane = lax.broadcasted_iota(jnp.int32, (1, segments.shape[0]), 1)

    for seq in range(ROWS // SEQ):
        which = head * (ROWS // SEQ) + seq
        row = segments[pl.ds(which, 1), :].astype(F32)
        column = jnp.sum(jnp.where(lane == which, turned, 0.0), axis=1, keepdims=True)
        bias[seq * SEQ : seq * SEQ + SEQ, :] = jnp.where(column == row, 0.0, neg_fill).astype(LOW)


def attend_phase(pair, mixed, bias, probs, context):
    tile = 256
    lane = lax.broadcasted_iota(jnp.int32, (1, 128), 1)
    left = (lane < HEAD_DIM).astype(LOW)

    def body(i):
        seq = i // (SEQ // tile)
        here = rows_at(i, tile)
        keys_at = rows_at(seq, SEQ)
        inside = rows_at(i % (SEQ // tile), tile)
        query = mixed[pair, here, 0:128] * LOW(HEAD_DIM ** (-0.5))
        keys = mixed[pair, keys_at, 128:256]
        values = mixed[pair, keys_at, 256:384]
        allowed = bias[here, :].astype(F32)
        outs = []
        for half in range(2):
            mask = left if half == 0 else LOW(1.0) - left
            scores = dot_back(query * mask, keys) + allowed
            top = jnp.max(scores, axis=-1, keepdims=True)
            weights = jnp.exp(scores - top)
            total = jnp.sum(weights, axis=-1, keepdims=True)
            prob = (weights * (1.0 / total)).astype(LOW)
            probs[pair * 4 + half * 2 + seq, inside, :] = prob
            outs.append(dot(prob, values))
        context[here, pl.ds(pl.multiple_of(pair * 128, 128), 128)] = jnp.where(
            lane < HEAD_DIM, outs[0], outs[1]
        ).astype(LOW)

    each(ROWS // tile, body)


def second_phase(tokens, context, wout, params, middle, second):
    gain = params[2:3, :]
    shift = params[3:4, :]

    def body(i):
        here = rows_at(i, TILE)
        value = tokens[here, :].astype(F32) + dot(context[here, :], wout[...])
        middle[here, :] = value
        normal, _, _ = normalize(value, gain, shift)
        second[here, :] = normal.astype(LOW)

    each(ROWS // TILE, body)


def turn_phase(src, dst):
    def body(i):
        here = rows_at(i, 256)
        dst[:, here] = src[here, :].T

    each(ROWS // 256, body)


def feed_phase(
    chunk, second, second_t, out_grad, out_grad_t, up, down, active, hidden_grad,
    result, second_grad, g_up, g_down,
):
    units = rows_at(chunk, CHUNK)

    def body(i):
        here = rows_at(i, TILE)
        hidden = dot_back(second[here, :], up[units, :])
        switch = 0.5 * jnp.tanh(0.851 * hidden) + 0.5
        act = (hidden * switch).astype(LOW)
        active[here, :] = act
        grad = dot_back(out_grad[here, :], down[units, :])
        back = (grad * (switch + 1.702 * hidden * switch * (1.0 - switch))).astype(LOW)
        hidden_grad[here, :] = back
        result[here, :] += dot(act, down[units, :])
        second_grad[here, :] += dot(back, up[units, :])

    each(ROWS // TILE, body)

    def grads(c):
        here = rows_at(c, 256)
        for turned, wide, out in ((out_grad_t, active, g_down), (second_t, hidden_grad, g_up)):
            grad = dot(turned[here, :], wide[...]).astype(LOW)
            for j in range(CHUNK // 128):
                out[chunk * 8 + j * 2 + c] = grad[:, j * 128 : j * 128 + 128]

    each(2, grads)


def middle_phase(
    params, middle, result, second_grad, out_grad, wout,
    layer_out, middle_grad, attended_low, context_grad, norms,
):
    gain = params[2:3, :]

    def body(i, sums):
        here = rows_at(i, TILE)
        value = middle[here, :]
        layer_out[here, :] = (value + result[here, :]).astype(LOW)
        _, plain, factor = normalize(value, gain, gain)
        upper = second_grad[here, :]
        lower, gains, shifts = normalize_back(upper, plain, factor, gain)
        total = out_grad[here, :].astype(F32) + lower
        middle_grad[here, :] = total
        low = total.astype(LOW)
        attended_low[here, :] = low
        context_grad[here, :] = dot_back(low, wout[...]).astype(LOW)
        return (sums[0] + gains[None], sums[1] + shifts[None])

    zero = jnp.zeros((1, 512), F32)
    sums = lax.fori_loop(0, ROWS // TILE, body, (zero, zero))
    norms[2:3, :] = sums[0]
    norms[3:4, :] = sums[1]


def out_phase(attended_t, context, g_attend):
    def body(i):
        here = rows_at(i, 256)
        grad = dot(attended_t[here, :], context[...]).astype(LOW)
        for p in range(PAIRS):
            g_attend[p, here, 384:512] = grad[:, p * 128 : p * 128 + 128]

    each(2, body)


def attend_back_phase(pair, seq, mixed, probs, context_grad, pair_grad):
    lane = lax.broadcasted_iota(jnp.int32, (1, 128), 1)
    left = (lane < HEAD_DIM).astype(LOW)
    scale = HEAD_DIM ** (-0.5)

    here = rows_at(seq, SEQ)
    query = mixed[pair, here, 0:128]
    keys = mixed[pair, here, 128:256]
    values = mixed[pair, here, 256:384]
    upper = context_grad[here, pl.ds(pl.multiple_of(pair * 128, 128), 128)]
    outs = []
    for half in range(2):
        mask = left if half == 0 else LOW(1.0) - left
        above = upper * mask
        prob_low = probs[pair * 4 + half * 2 + seq]
        prob = prob_low.astype(F32)
        prob_grad = dot_back(above, values)
        inner = jnp.sum(prob * prob_grad, axis=-1, keepdims=True)
        score_grad = (prob * (prob_grad - inner)).astype(LOW)
        outs.append(
            (
                dot(score_grad, keys),
                dot_rows(score_grad, query),
                dot_rows(prob_low, above),
            )
        )
    pick = lane < HEAD_DIM
    pair_grad[here, 0:128] = (jnp.where(pick, outs[0][0], outs[1][0]) * scale).astype(LOW)
    pair_grad[here, 128:256] = (jnp.where(pick, outs[0][1], outs[1][1]) * scale).astype(LOW)
    pair_grad[here, 256:384] = (outs[0][2] + outs[1][2]).astype(LOW)


def qkv_phase(pair, pair_grad, first_t, g_attend):
    def body(i):
        here = rows_at(i, 256)
        g_attend[pair, here, 0:384] = dot(first_t[here, :], pair_grad[...]).astype(LOW)

    each(2, body)


def first_grad_phase(pair, pair_grad, wqkv, first_grad):
    def body(i):
        here = rows_at(i, TILE)
        first_grad[here, :] += dot_back(pair_grad[here, :], wqkv[pair])

    each(ROWS // TILE, body)


def input_phase(params, tokens, first_grad, input_grad, norms):
    gain = params[0:1, :]

    def body(i, sums):
        here = rows_at(i, TILE)
        _, plain, factor = normalize(tokens[here, :].astype(F32), gain, gain)
        lower, gains, shifts = normalize_back(first_grad[here, :], plain, factor, gain)
        input_grad[here, :] += lower
        return (sums[0] + gains[None], sums[1] + shifts[None])

    zero = jnp.zeros((1, 512), F32)
    sums = lax.fori_loop(0, ROWS // TILE, body, (zero, zero))
    norms[0:1, :] = sums[0]
    norms[1:2, :] = sums[1]


def local_call(kernel, outs, scratch, args, name):
    vmem = pl.BlockSpec(memory_space=pltpu.VMEM)
    return pl.pallas_call(
        kernel,
        out_shape=tuple(jax.ShapeDtypeStruct(*o) for o in outs),
        in_specs=[vmem] * len(args),
        out_specs=(vmem,) * len(outs),
        scratch_shapes=[pltpu.VMEM(*v) for v in scratch],
        compiler_params=pltpu.CompilerParams(vmem_limit_bytes=60 << 20),
        name=name,
    )(*args)


STEP_DIMS = {"c": 1, "x": 2, "y": 4, "l": 8, "g": 16}
GATHER_UP = ("g", "l", "y", "x", "c")
GATHER_DOWN = ("l", "g", "x", "y", "c")
STARTS = (("g", "l", "y", "x", "c"), ("g", "x", "l", "y", "c"), ("g", "y", "x", "l", "c"))
ATTEND_ORDER = ("c", "x", "y", "l", "g")


def coordinates():
    dp = lax.axis_index("dp")
    head = lax.axis_index("head")
    bits = {
        "c": head % 2,
        "x": head // 2,
        "y": dp % 2,
        "l": (dp // 2) % 2,
        "g": dp // 4,
    }
    steps = {"c": (0, 1), "x": (0, 2), "y": (1, 0), "l": (2, 0), "g": (4, 0)}
    peers = {}
    for name, (along_dp, along_head) in steps.items():
        turn = 1 - 2 * bits[name]
        peers[name] = (dp + along_dp * turn, head + along_head * turn)
    return dp, head, bits, peers


def remote(src, dst, send_sem, recv_sem, peer):
    return pltpu.make_async_remote_copy(
        src_ref=src,
        dst_ref=dst,
        send_sem=send_sem,
        recv_sem=recv_sem,
        device_id=peer,
        device_id_type=pl.DeviceIdType.MESH,
    )


def tile_of(fixed, free, place):
    total = 0
    for name, bit in fixed.items():
        total = total + STEP_DIMS[name] * bit
    for i, name in enumerate(free):
        total = total + STEP_DIMS[name] * ((place // 2**i) % 2)
    return total


def scatter_start(acc, got, base, fixed, name, free, bits, peer, sems, slot):
    for place in range(2 ** len(free)):
        away = tile_of({**fixed, name: 1 - bits[name]}, free, place)
        remote(
            acc.at[away], got.at[base + place], sems[0].at[slot], sems[1].at[slot], peer
        ).start()


def scatter_end(acc, got, base, fixed, name, free, bits, peer, sems, slot):
    count = 2 ** len(free)
    span = got.at[pl.ds(base, count)]
    remote(span, span, sems[0].at[slot], sems[1].at[slot], peer).wait()
    rows = acc.shape[1]

    def body(i):
        here = tile_of({**fixed, name: bits[name]}, free, i)
        acc[here] = (acc[here].astype(F32) + got[base + i].astype(F32)).astype(LOW)

    each(count, body)


def gather_start(ref, rows, done, name, bits, peer, sems, slot):
    fixed = {d: bits[d] for d in STEP_DIMS if d not in done}
    for place in range(2 ** len(done)):
        tile = tile_of(fixed, done, place)
        if rows:
            part = ref.at[pl.ds(pl.multiple_of(tile * rows, rows), rows)]
        else:
            part = ref.at[tile]
        remote(part, part, sems[0].at[slot], sems[1].at[slot], peer).start()


def gather_end(ref, rows, done, peer, sems, slot):
    span = ref.at[pl.ds(0, 2 ** len(done) * (rows or 1))]
    remote(span, span, sems[0].at[slot], sems[1].at[slot], peer).wait()


def paired(block):
    parts = [block[:, i * 64 : i * 64 + 64] for i in (0, 3, 1, 4, 2, 5)]
    return jnp.concatenate(parts, axis=1)


def unpaired(block):
    parts = [block[:, i * 64 : i * 64 + 64] for i in (0, 2, 4, 1, 3, 5)]
    return jnp.concatenate(parts, axis=1)


class Slots:
    def __init__(self):
        self.used = 0

    def __call__(self, count):
        start = self.used
        self.used += count
        return start


def update_step(pool, now, later, count, blocks, lanes, gram, mix):
    def gram_body(i):
        rows = rows_at(i, TILE)
        total = dot_back(pool[now, rows, :], pool[now])
        for b in range(1, count):
            total = total + dot_back(pool[now + b, rows, :], pool[now + b])
        gram[rows, :] = total.astype(LOW)

    each(512 // TILE, gram_body)

    def mix_body(i):
        rows = rows_at(i, TILE)
        own = gram[rows, :]
        mix[rows, :] = (ns_b * own.astype(F32) + ns_c * dot(own, gram[...])).astype(LOW)

    each(512 // TILE, mix_body)

    def next_body(i):
        b = blocks[0] + i
        value = pool[now + b, :, lanes]
        pool[later + b, :, lanes] = (ns_a * value.astype(F32) + dot(mix[...], value)).astype(LOW)

    each(blocks[1], next_body)


def layer_kernel(
    tokens, segments, out_grad, params, w_qkv, m_qkv, w_out, m_out, w_up, m_up, w_down, m_down,
    layer_out, input_grad, start_a, start_u, start_d, ortho_q, ortho_o, ortho_u, ortho_d, norm_sum, scal,
    first, mixed, context, bias, wqkv, wout, wup, wdown, pool, middle, second, second_t, out_grad_t,
    active, hidden_grad, result, second_grad, pair_grad, acc_a, acc_u, acc_d, got_a, got_u, got_d,
    mom_full, mom_x, mom_u, mom_d, mom_a, norm_got, stat_got, gram, mix, send, recv,
):
    dp, head, bits, peers = coordinates()
    me = dp * 4 + head
    sibling = peers["c"]
    across = (dp, 3 - head)
    sems = (send, recv)
    slots = Slots()
    S_Q, S_O, S_M, S_MA = slots(4), slots(4), slots(2), slots(4)
    S_UP, S_DOWN, S_CHUNK, S_LG = slots(5), slots(5), slots(24), slots(4)
    S_A, S_NORM, S_STAT, S_START, S_SIDE, S_ORTHO = (
        slots(20), slots(1), slots(1), slots(15), slots(2), slots(8)
    )
    barrier = pltpu.get_barrier_semaphore()

    def greet(i):
        other = (me + 1 + i) % 32
        pl.semaphore_signal(
            barrier, inc=1, device_id=(other // 4, other % 4), device_id_type=pl.DeviceIdType.MESH
        )

    each(31, greet)
    wqkv[head] = paired(w_qkv[...].astype(LOW))
    wout[pl.ds(pl.multiple_of(head * 128, 128), 128), :] = w_out[...].astype(LOW)
    mine = pl.ds(pl.multiple_of(me * 64, 64), 64)
    wup[mine, :] = w_up[...].astype(LOW)
    wdown[mine, :] = w_down[...].astype(LOW)
    pl.semaphore_wait(barrier, 31)

    def block_q(who):
        return wqkv.at[who]

    def block_o(who):
        return wout.at[pl.ds(pl.multiple_of(who * 128, 128), 128)]

    def weight_copy(block, who, slot, peer):
        return remote(block(who), block(who), send.at[slot], recv.at[slot], peer)

    weight_copy(block_q, head, S_Q + 1, sibling).start()
    weight_copy(block_q, head, S_Q + 2, peers["x"]).start()
    gather_start(wup, 64, (), GATHER_UP[0], bits, peers[GATHER_UP[0]], sems, S_UP)
    gather_start(wdown, 64, (), GATHER_DOWN[0], bits, peers[GATHER_DOWN[0]], sems, S_DOWN)
    weight_copy(block_o, head, S_O + 1, sibling).start()
    weight_copy(block_o, head, S_O + 2, peers["x"]).start()
    other_half = pl.ds(pl.multiple_of((1 - bits["c"]) * 256, 256), 256)

    def moment_copy(i, ref):
        return remote(ref.at[:, other_half], mom_x.at[i], send.at[S_M + i], recv.at[S_M + i], sibling)

    moment_copy(0, m_up).start()
    moment_copy(1, m_down).start()

    def weight_step(k):
        for ref, order, slot in ((wup, GATHER_UP, S_UP), (wdown, GATHER_DOWN, S_DOWN)):
            gather_end(ref, 64, order[:k], peers[order[k]], sems, slot + k)
            if k < 4:
                gather_start(
                    ref, 64, order[: k + 1], order[k + 1], bits, peers[order[k + 1]], sems, slot + k + 1
                )

    first_phase(tokens, params, first)
    bias_phase(segments, head, bias)
    weight_step(0)
    turn_phase(out_grad, out_grad_t)
    mom_full[:, 0:384] = paired(m_qkv[...])
    mom_full[:, 384:512] = m_out[...].T

    def rank_of(c, x):
        return c * 16 + x * 8 + bits["y"] * 4 + bits["l"] * 2 + bits["g"]

    def rank_rows(who):
        return pl.ds(pl.multiple_of(rank_of(who % 2, who // 2) * 16, 16), 16)

    partners = (sibling, peers["x"], across)

    def rows_copy(j):
        who = partners[j][1]
        return remote(
            mom_full.at[rank_rows(who)], mom_a.at[head], send.at[S_MA + j], recv.at[S_MA + j], partners[j]
        )

    for j in range(3):
        rows_copy(j).start()
    mom_a[head] = mom_full[rank_rows(head), :]

    def pair_body(j):
        pair = (bits["c"] + j % 2) % 2 + 2 * ((bits["x"] + j // 2) % 2)
        mixed_phase(pair, first, wqkv, mixed)
        attend_phase(pair, mixed, bias, pool, context)

        @pl.when(j == 0)
        def _():
            weight_step(1)
            weight_copy(block_q, head, S_Q + 1, sibling).wait()
            weight_copy(block_o, head, S_O + 1, sibling).wait()
            weight_copy(block_q, head, S_Q + 2, peers["x"]).wait()
            weight_copy(block_q, peers["x"][1], S_Q + 3, sibling).start()
            weight_copy(block_o, head, S_O + 2, peers["x"]).wait()
            weight_copy(block_o, peers["x"][1], S_O + 3, sibling).start()

        @pl.when(j == 1)
        def _():
            weight_step(2)

        @pl.when(j == 2)
        def _():
            weight_copy(block_q, head, S_Q + 3, sibling).wait()
            weight_copy(block_o, head, S_O + 3, sibling).wait()

    each(PAIRS, pair_body)
    second_phase(tokens, context, wout, params, middle, second)
    weight_step(3)
    turn_phase(second, second_t)
    result[...] = jnp.zeros_like(result)
    second_grad[...] = jnp.zeros_like(second_grad)
    weight_step(4)

    chunk_orders = ((acc_u, got_u, ("c", "x", "y")), (acc_d, got_d, ("c", "y", "x")))

    def chunk_args(q, k, order):
        fixed = {"g": q // 2, "l": q % 2}
        for name in order[:k]:
            fixed[name] = bits[name]
        return fixed, order[k], order[k + 1 :]

    def chunk_start(q, k):
        for i, (acc, got, order) in enumerate(chunk_orders):
            fixed, name, free = chunk_args(q, k, order)
            scatter_start(
                acc, got, q * 7 + (0, 4, 6)[k], fixed, name, free, bits, peers[name], sems,
                S_CHUNK + q * 6 + i * 3 + k,
            )

    def chunk_end(q, k):
        for i, (acc, got, order) in enumerate(chunk_orders):
            fixed, name, free = chunk_args(q, k, order)
            scatter_end(
                acc, got, q * 7 + (0, 4, 6)[k], fixed, name, free, bits, peers[name], sems,
                S_CHUNK + q * 6 + i * 3 + k,
            )

    def feed_body(q):
        feed_phase(
            q, second, second_t, out_grad, out_grad_t, wup, wdown, active, hidden_grad,
            result, second_grad, acc_u, acc_d,
        )
        chunk_start(q, 0)

        @pl.when(q >= 1)
        def _():
            chunk_end(q - 1, 0)
            chunk_start(q - 1, 1)

        @pl.when(q >= 2)
        def _():
            chunk_end(q - 2, 1)
            chunk_start(q - 2, 2)

        @pl.when(q >= 3)
        def _():
            chunk_end(q - 3, 2)

    each(WIDE // CHUNK, feed_body)
    middle_phase(
        params, middle, result, second_grad, out_grad, wout,
        layer_out, input_grad, second, active, norm_got.at[me],
    )
    chunk_end(3, 0)
    chunk_start(3, 1)
    chunk_end(2, 1)
    chunk_start(2, 2)
    chunk_end(1, 2)
    turn_phase(second, second_t)
    out_phase(second_t, context, acc_a)
    turn_phase(first, second_t)
    result[...] = jnp.zeros_like(result)

    def last_args(k):
        fixed = {"c": bits["c"], "x": bits["x"], "y": bits["y"]}
        if k == 1:
            fixed["l"] = bits["l"]
            return fixed, "g", ()
        return fixed, "l", ("g",)

    def last_step(k, ending):
        for i, (acc, got, _) in enumerate(chunk_orders):
            fixed, name, free = last_args(k)
            (scatter_end if ending else scatter_start)(
                acc, got, 28 + 2 * k, fixed, name, free, bits, peers[name], sems, S_LG + 2 * k + i
            )

    spans = []
    low_row = 0
    for k, name in enumerate(ATTEND_ORDER):
        size = 256 >> k
        spans.append((name, size, low_row + bits[name] * size, low_row + (1 - bits[name]) * size))
        low_row = low_row + bits[name] * size

    def aligned(row, size):
        return pl.ds(pl.multiple_of(row, 16), size)

    def attend_copy(pair, k):
        name, size, _, give = spans[k]
        return remote(
            acc_a.at[pair, aligned(give, size)], got_a.at[pair, pl.ds(512 - 2 * size, size)],
            send.at[S_A + pair * 5 + k], recv.at[S_A + pair * 5 + k], peers[name],
        )

    def attend_start(pair, k):
        attend_copy(pair, k).start()

    def attend_next(pair, k, more=True):
        attend_copy(pair, k).wait()
        _, size, keep, _ = spans[k]
        step = min(size, 64)

        def body(i):
            here = aligned(keep + i * step, step)
            come = aligned(512 - 2 * size + i * step, step)
            acc_a[pair, here, :] = (
                acc_a[pair, here, :].astype(F32) + got_a[pair, come, :].astype(F32)
            ).astype(LOW)

        each(size // step, body)
        if k < 4:
            attend_start(pair, k + 1)

    def at(wanted, pair):
        return pl.when(pair == wanted)

    def back_body(pair):
        attend_back_phase(pair, 0, mixed, pool, active, pair_grad)

        @at(0, pair)
        def _():
            chunk_end(3, 1)
            chunk_start(3, 2)
            chunk_end(2, 2)

        @at(1, pair)
        def _():
            attend_next(0, 0)

        @at(2, pair)
        def _():
            attend_next(1, 0)
            attend_next(0, 1)

        @at(3, pair)
        def _():
            attend_next(2, 0)
            attend_next(1, 1)
            attend_next(0, 3)

        attend_back_phase(pair, 1, mixed, pool, active, pair_grad)
        qkv_phase(pair, pair_grad, second_t, acc_a)
        attend_start(pair, 0)

        @at(0, pair)
        def _():
            chunk_end(3, 2)
            last_step(0, False)

        @at(1, pair)
        def _():
            last_step(0, True)
            last_step(1, False)

        @at(2, pair)
        def _():
            last_step(1, True)
            attend_next(0, 2)

        first_grad_phase(pair, pair_grad, wqkv, result)

    each(PAIRS, back_body)
    attend_next(3, 0)
    attend_next(2, 1)
    attend_next(1, 2)
    attend_next(0, 4)
    input_phase(params, tokens, result, input_grad, norm_got.at[me])

    def tell_norm(i):
        other = (me + 1 + i) % 32
        remote(
            norm_got.at[me], norm_got.at[me], send.at[S_NORM], recv.at[S_NORM], (other // 4, other % 4)
        ).start()

    attend_next(3, 1)
    each(31, tell_norm)
    attend_next(2, 2)
    attend_next(1, 3)
    moment_copy(0, m_up).wait()
    moment_copy(1, m_down).wait()
    keep_half = pl.ds(pl.multiple_of(bits["c"] * 256, 256), 256)
    for i, (ref, out) in enumerate(((m_up, mom_u), (m_down, mom_d))):
        own = ref[:, keep_half]
        far = mom_x[i]
        low_half = jnp.where(bits["c"] == 0, own, far)
        high_half = jnp.where(bits["c"] == 0, far, own)
        out[...] = jnp.concatenate([low_half, high_half], axis=0).T
    for j in range(3):
        rows_copy(j).wait()

    def total_of(value):
        return jnp.sum(jnp.sum(value, axis=0, keepdims=True), axis=1, keepdims=True)

    lane = lax.broadcasted_iota(jnp.int32, (8, 128), 1)
    column = lax.broadcasted_iota(jnp.int32, (1, 512), 1)
    grad_u = acc_u[me].astype(F32)
    grad_d = acc_d[me].astype(F32)
    stats = jnp.zeros((8, 128), F32)
    for m, (moment, grad) in enumerate(((mom_u[...], grad_u), (mom_d[...], grad_d))):
        for i, product in enumerate((moment * moment, moment * grad, grad * grad)):
            stats = jnp.where(lane == 6 + 3 * m + i, total_of(product), stats)
    attend_next(3, 2)
    attend_next(2, 3)
    attend_next(1, 4)
    attend_next(3, 3)
    attend_next(2, 4)
    span = norm_got.at[pl.ds(0, 31)]
    remote(span, span, send.at[S_NORM], recv.at[S_NORM], sibling).wait()
    vector = norm_got[0]
    for i in range(1, 32):
        vector = vector + norm_got[i]
    norm_sum[...] = vector
    vector_total = total_of(vector * vector)
    attend_next(3, 4)
    my_rows = aligned(low_row, 16)
    for i in range(3):
        inside = jnp.zeros((1, 512), F32)
        for pair in range(PAIRS):
            moment = mom_a[pair]
            grad = acc_a[pair, my_rows, :].astype(F32)
            product = (moment * moment, moment * grad, grad * grad)[i]
            inside = inside + jnp.sum(product, axis=0, keepdims=True)
        stats = jnp.where(lane == i, total_of(jnp.where(column < 384, inside, 0.0)), stats)
        stats = jnp.where(lane == 3 + i, total_of(jnp.where(column < 384, 0.0, inside)), stats)
    stat_got[me] = stats

    def tell(i):
        other = (me + 1 + i) % 32
        remote(
            stat_got.at[me], stat_got.at[me], send.at[S_STAT], recv.at[S_STAT], (other // 4, other % 4)
        ).start()

    each(31, tell)
    span = stat_got.at[pl.ds(0, 31)]
    remote(span, span, send.at[S_STAT], recv.at[S_STAT], sibling).wait()
    stats = jnp.sum(stat_got[...], axis=0)

    def stat(i):
        return jnp.sum(jnp.where(lane == i, stats, 0.0), axis=1, keepdims=True)[0:1]

    norm = jnp.sqrt(stat(2) + stat(5) + stat(8) + stat(11) + vector_total)
    clip = jnp.minimum(1.0, 1.0 / (norm + 1e-06))
    sizes = []
    for m in range(4):
        square = (
            momentum_decay * momentum_decay * stat(3 * m)
            + 2.0 * momentum_decay * clip * stat(3 * m + 1)
            + clip * clip * stat(3 * m + 2)
        )
        sizes.append(jnp.sqrt(jnp.maximum(square, 0.0)) + 1e-07)
    told = jnp.where(lane == 0, norm, clip)
    for m in range(4):
        told = jnp.where(lane == 2 + m, sizes[m], told)
    scal[...] = told
    scale_a = jnp.where(column < 384, 1.0 / sizes[0], 1.0 / sizes[1])
    got_u[me] = ((momentum_decay * mom_u[...] + clip * grad_u) * (1.0 / sizes[2])).astype(LOW)
    got_d[me] = ((momentum_decay * mom_d[...] + clip * grad_d) * (1.0 / sizes[3])).astype(LOW)
    for pair in range(PAIRS):
        grad = acc_a[pair, my_rows, :].astype(F32)
        pool[pair, my_rows, :] = ((momentum_decay * mom_a[pair] + clip * grad) * scale_a).astype(LOW)

    mine_half = pl.ds(pl.multiple_of(bits["c"] * 256, 256), 256)

    def side_copy(i):
        src, dst = ((got_u, start_u), (got_d, start_d))[i]
        return remote(
            src.at[me], dst.at[mine_half], send.at[S_SIDE + i], recv.at[S_SIDE + i], sibling
        )

    side_copy(0).start()
    side_copy(1).start()
    start_u[mine_half, :] = got_u[me]
    start_d[mine_half, :] = got_d[me]

    def start_copy(k):
        name, size, keep, _ = spans[4 - k]
        part = pool.at[pl.ds(0, 4), aligned(keep, size)]
        return remote(part, part, send.at[S_START + 3 * k], recv.at[S_START + 3 * k], peers[name])

    tiles = ((got_u, STARTS[1]), (got_d, STARTS[2]))
    for k in range(4):
        start_copy(k).start()
        for m, (got, order) in enumerate(tiles):
            gather_start(
                got, 0, order[:k], order[k], bits, peers[order[k]], sems, S_START + 3 * k + 1 + m
            )
        start_copy(k).wait()
        for m, (got, order) in enumerate(tiles):
            gather_end(got, 0, order[:k], peers[order[k]], sems, S_START + 3 * k + 1 + m)
    half_rows = aligned(spans[0][2], 256)
    pair_part = pool.at[pl.ds(head + 1 - 2 * bits["c"], 1), half_rows]
    all_part = pool.at[pl.ds(0, 4), half_rows]

    def core_copy(part):
        return remote(part, part, send.at[S_START + 12], recv.at[S_START + 12], sibling)

    @pl.when(bits["c"] == 1)
    def _():
        core_copy(all_part).start()

        def slice_body(i):
            rows = rows_at(i, 256)
            start_a[rows, :] = pool[head, rows, :]

        for x, (got, order) in enumerate(tiles):
            @pl.when(bits["x"] == x)
            def _(got=got, order=order, x=x):
                span = got.at[pl.ds(0, 16)]
                remote(span, span, send.at[S_START + 13], recv.at[S_START + 13], sibling).wait_recv()

                def body(i):
                    for j in range(4):
                        for c in range(2):
                            pool[4 + i, c * 256 : c * 256 + 256, j * 128 : j * 128 + 128] = got[
                                i * 8 + j * 2 + c
                            ]

                each(4, body)

        core_copy(pair_part).wait_recv()
        core_copy(all_part).wait_send()
        each(2, slice_body)

    @pl.when(bits["c"] == 0)
    def _():
        for x, (got, order) in enumerate(tiles):
            @pl.when(bits["x"] == x)
            def _(got=got, order=order):
                gather_start(got, 0, order[:4], "c", bits, sibling, sems, S_START + 13)

        core_copy(pair_part).start()
        core_copy(all_part).wait_recv()

        def body(i):
            rows = rows_at(i, 256)
            start_a[rows, :] = pool[head, rows, :]
            for p in range(PAIRS):
                for r in range(3):
                    group = p * 3 + r
                    pool[4 + group // 4, rows, (group % 4) * 128 : (group % 4) * 128 + 128] = pool[
                        p, rows, r * 128 : r * 128 + 128
                    ]
                pool[7, rows, p * 128 : p * 128 + 128] = pool[p, rows, 384:512]

        each(2, body)
        core_copy(pair_part).wait_send()
        span = got_u.at[pl.ds(0, 16)]
        remote(span, span, send.at[S_START + 13], recv.at[S_START + 13], sibling).wait_send()

    side_copy(0).wait()
    side_copy(1).wait()

    every = pl.ds(0, 512)
    outs = (ortho_u, ortho_d)

    def out_copy(src, dst, i, peer):
        return remote(src, dst, send.at[S_ORTHO + i], recv.at[S_ORTHO + i], peer)

    def group_of(r):
        group = bits["x"] * 6 + r
        return pool.at[8 + group // 4, :, pl.ds(pl.multiple_of((group % 4) * 128, 128), 128)]

    def out_of(who):
        return pool.at[11, :, pl.ds(pl.multiple_of(who * 128, 128), 128)]

    @pl.when(bits["c"] == 0)
    def _():
        def turn_body(turn):
            now = 4 + (turn % 2) * 4
            later = 12 - now
            update_step(pool, now, later, 3, (0, 3), every, gram, mix)
            update_step(pool, now + 3, later + 3, 1, (0, 1), every, gram, mix)

        each(NS_STEPS - 1, turn_body)
        update_step(pool, 4, 8, 3, (bits["x"], 2), every, gram, mix)
        for r in range(3):
            out_copy(group_of(3 + r), ortho_q.at[:, pl.ds(r * 128, 128)], 0, sibling).start()
        for r in range(3):
            ortho_q[:, r * 128 : r * 128 + 128] = group_of(r)[...]
        columns = pl.ds(pl.multiple_of(bits["x"] * 256, 256), 256)
        update_step(pool, 7, 11, 1, (0, 1), columns, gram, mix)
        out_copy(out_of(head + 1), ortho_o, 1, sibling).start()
        ortho_o[...] = out_of(head)[...]
        out_copy(ortho_q, ortho_q, 0, sibling).wait_send()
        out_copy(ortho_o, ortho_o, 1, sibling).wait_send()

    @pl.when(bits["c"] == 1)
    def _():
        def turn_body(turn):
            now = 4 + (turn % 2) * 4
            update_step(pool, now, 12 - now, 4, (0, 4), every, gram, mix)

        each(NS_STEPS - 1, turn_body)
        wanted = dp // 2
        update_step(pool, 4, 8, 4, (wanted, 1), every, gram, mix)

        def block_of(x):
            block = dp * 2 + x
            return pool.at[8 + wanted, :, pl.ds(pl.multiple_of((block % 4) * 128, 128), 128)]

        for x in range(2):
            @pl.when(bits["x"] == x)
            def _(x=x):
                targets = ((across, 1 - x), (peers["x"], 1 - x), (sibling, x))
                for j, (peer, side) in enumerate(targets):
                    remote(
                        block_of(side), outs[x], send.at[S_ORTHO + 2 + j], recv.at[S_ORTHO + 2 + x], peer
                    ).start()
                outs[x][...] = block_of(x)[...]
                for j, (peer, side) in enumerate(targets):
                    remote(
                        block_of(side), outs[x], send.at[S_ORTHO + 2 + j], recv.at[S_ORTHO + 2 + x], peer
                    ).wait_send()

        out_copy(ortho_q, ortho_q, 0, sibling).wait_recv()
        out_copy(ortho_o, ortho_o, 1, sibling).wait_recv()

    for x in range(2):
        @pl.when(head != 2 * x + 1)
        def _(x=x):
            out_copy(outs[x], outs[x], 2 + x, sibling).wait_recv()


def layer_call(*args):
    shape = jax.ShapeDtypeStruct
    vmem = pl.BlockSpec(memory_space=pltpu.VMEM)
    outs = (
        shape((ROWS, 512), LOW), shape((ROWS, 512), F32),
        shape((512, 512), LOW), shape((512, 128), LOW), shape((512, 128), LOW),
        shape((512, 384), LOW), shape((512, 128), LOW), shape((512, 128), LOW), shape((512, 128), LOW),
        shape((4, 512), F32), shape((8, 128), F32),
    )
    scratch = [
        ((ROWS, 512), LOW),
        ((PAIRS, ROWS, 384), LOW),
        ((ROWS, 512), LOW),
        ((ROWS, SEQ), LOW),
        ((PAIRS, 512, 384), LOW),
        ((512, 512), LOW),
        ((WIDE, 512), LOW),
        ((WIDE, 512), LOW),
        ((16, 512, 512), LOW),
        ((ROWS, 512), F32),
        ((ROWS, 512), LOW),
        ((512, ROWS), LOW),
        ((512, ROWS), LOW),
        ((ROWS, CHUNK), LOW),
        ((ROWS, CHUNK), LOW),
        ((ROWS, 512), F32),
        ((ROWS, 512), F32),
        ((ROWS, 384), LOW),
        ((PAIRS, 512, 512), LOW),
        ((32, 256, 128), LOW),
        ((32, 256, 128), LOW),
        ((PAIRS, 512, 512), LOW),
        ((32, 256, 128), LOW),
        ((32, 256, 128), LOW),
        ((512, 512), F32),
        ((2, 64, 256), F32),
        ((256, 128), F32),
        ((256, 128), F32),
        ((PAIRS, 16, 512), F32),
        ((32, 4, 512), F32),
        ((32, 8, 128), F32),
        ((512, 512), LOW),
        ((512, 512), LOW),
    ]
    return pl.pallas_call(
        layer_kernel,
        out_shape=outs,
        in_specs=[vmem] * len(args),
        out_specs=(vmem,) * len(outs),
        scratch_shapes=[pltpu.VMEM(*v) for v in scratch]
        + [pltpu.SemaphoreType.DMA((104,)), pltpu.SemaphoreType.DMA((104,))],
        compiler_params=pltpu.CompilerParams(
            collective_id=1, has_side_effects=True, vmem_limit_bytes=VMEM_BYTES
        ),
        name="layer",
    )(*args)


def update_kernel(
    start_a, start_u, start_d, ortho_q, ortho_o, ortho_u, ortho_d, norm_sum, scal,
    w_qkv, w_out, w_up, w_down, norm_first, norm_second,
    new_q, mom_q, new_o, mom_o, new_u, mom_u, new_d, mom_d, clipped, first_new, second_new, norm,
):
    core = lax.axis_index("head") % 2
    clip = scal[0:1, 1:2]
    keep = 1.0 - muon_rate * muon_decay

    def fresh(weight, factor, ortho):
        return weight * keep - muon_rate * factor * ortho

    new_q[...] = fresh(w_qkv[...], math.sqrt(3.0), unpaired(ortho_q[...].astype(F32)))
    mom_q[...] = unpaired(start_a[:, 0:384].astype(F32)) * scal[0:1, 2:3]
    new_o[...] = fresh(w_out[...], math.sqrt(SEQ / 8.0), ortho_o[...].astype(F32).T)
    mom_o[...] = start_a[:, 384:512].astype(F32).T * scal[0:1, 3:4]
    for weight, ortho, start, new, mom, i in (
        (w_up, ortho_u, start_u, new_u, mom_u, 4),
        (w_down, ortho_d, start_d, new_d, mom_d, 5),
    ):
        turned = ortho[...].astype(F32).T
        turned = jnp.where(core == 0, turned[0:64], turned[64:128])
        new[...] = fresh(weight[...], math.sqrt(max(1.0, FF / 512)), turned)
        turned = start[...].astype(F32).T
        mom[...] = jnp.where(core == 0, turned[0:64], turned[64:128]) * scal[0:1, i : i + 1]
    norm[...] = scal[0:1, 0:1]
    clip_grad = clip * norm_sum[...]
    clipped[...] = clip_grad
    first_new[...] = beta_one * norm_first[...] + (1.0 - beta_one) * clip_grad
    second_new[...] = beta_two * norm_second[...] + (1.0 - beta_two) * clip_grad * clip_grad


def fast_shards(
    tokens,
    segments,
    out_grad,
    norm_params,
    norm_first,
    norm_second,
    qkv_weight,
    qkv_moment,
    out_weight,
    out_moment,
    up_weight,
    up_moment,
    down_weight,
    down_moment,
):
    (
        layer_out, input_grad, start_a, start_u, start_d, ortho_q, ortho_o, ortho_u, ortho_d, norm_sum, scal
    ) = layer_call(
        tokens, segments.reshape(segments.shape[0] // SEQ, SEQ), out_grad, norm_params,
        qkv_weight, qkv_moment, out_weight, out_moment,
        up_weight.T, up_moment.T, down_weight.T, down_moment.T,
    )
    tall = ((64, 512), F32)
    new_q, mom_q, new_o, mom_o, new_u, mom_u, new_d, mom_d, clipped, first_new, second_new, norm = local_call(
        update_kernel,
        [((512, 384), F32)] * 2 + [((128, 512), F32)] * 2 + [tall] * 4 + [((4, 512), F32)] * 3 + [((1, 1), F32)],
        [],
        (
            start_a, start_u, start_d, ortho_q, ortho_o, ortho_u, ortho_d, norm_sum, scal,
            qkv_weight, out_weight, up_weight.T, down_weight.T, norm_first, norm_second,
        ),
        "update",
    )
    return (
        layer_out, input_grad, norm.reshape(()), clipped, first_new, second_new,
        new_q, mom_q, new_o, mom_o, new_u.T, mom_u.T, new_d.T, mom_d.T,
    )


def general_update(
    whole_qkv, whole_out, up_grad, down_grad, vector_part,
    qkv_moment, out_moment, up_moment, down_moment,
):
    everywhere = ("dp", "head")
    narrow = out_moment.shape[0]
    up_part, down_part = (
        lax.psum_scatter(
            up_grad.astype(jnp.bfloat16), everywhere, scatter_dimension=1, tiled=True
        ).astype(jnp.float32),
        lax.psum_scatter(
            down_grad.astype(jnp.bfloat16), everywhere, scatter_dimension=1, tiled=True
        ).astype(jnp.float32),
    )
    qkv_part = lax.psum_scatter(
        whole_qkv.astype(jnp.bfloat16), "head", scatter_dimension=1, tiled=True
    )
    out_part = lax.psum_scatter(
        whole_out.astype(jnp.bfloat16), "head", scatter_dimension=0, tiled=True
    )
    qkv_sum, out_sum = (
        lax.psum(qkv_part, "dp").astype(jnp.float32),
        lax.psum(out_part, "dp").astype(jnp.float32),
    )
    leading = (lax.axis_index("dp") == 0).astype(jnp.float32)
    moments = [qkv_moment, out_moment, up_moment, down_moment]
    grads = [qkv_sum, out_sum, up_part, down_part]
    stats = jnp.stack(
        [
            squares_of(qkv_moment, qkv_sum, leading),
            squares_of(out_moment, out_sum, leading),
            squares_of(up_moment, up_part, 1.0),
            squares_of(down_moment, down_part, 1.0),
        ]
    )
    vector_sum, stat_sum = lax.psum((vector_part, stats), everywhere)
    grad_norm = jnp.sqrt(jnp.sum(stat_sum[:, 2]) + jnp.sum(vector_sum * vector_sum))
    clip = jnp.minimum(1.0, 1.0 / (grad_norm + 1e-06))
    sizes = jnp.sqrt(
        momentum_decay * momentum_decay * stat_sum[:, 0]
        + 2.0 * momentum_decay * clip * stat_sum[:, 1]
        + clip * clip * stat_sum[:, 2]
    )
    new_moments = [momentum_decay * moments[index] + clip * grads[index] for index in range(4)]
    starts = [
        (new_moments[index] / (sizes[index] + 1e-07)).astype(jnp.bfloat16) for index in range(4)
    ]
    blocks = [
        lax.all_gather(starts[0], "head", axis=1, tiled=True),
        lax.all_gather(starts[1], "head", axis=0, tiled=True),
        lax.all_gather(starts[2], everywhere, axis=1, tiled=True),
        lax.all_gather(starts[3], everywhere, axis=1, tiled=True),
    ]
    for turn in range(NS_STEPS):
        updated = []
        for index in range(4):
            form = gram_right if index == 1 else gram_left
            gram = form(blocks[index]).astype(jnp.bfloat16)
            mix = (
                ns_b * gram.astype(jnp.float32)
                + ns_c * jnp.dot(gram, gram, preferred_element_type=jnp.float32)
            ).astype(jnp.bfloat16)
            if index == 1:
                product = jnp.dot(blocks[index], mix, preferred_element_type=jnp.float32)
            else:
                product = jnp.dot(mix, blocks[index], preferred_element_type=jnp.float32)
            updated.append(
                (ns_a * blocks[index].astype(jnp.float32) + product).astype(jnp.bfloat16)
            )
        blocks = updated
    share = up_moment.shape[1]
    along = lax.axis_index("head")
    offset = (lax.axis_index("dp") * lax.axis_size("head") + along) * share
    owned = [
        lax.dynamic_slice_in_dim(blocks[0], along * qkv_moment.shape[1], qkv_moment.shape[1], 1),
        lax.dynamic_slice_in_dim(blocks[1], along * narrow, narrow, 0),
        lax.dynamic_slice_in_dim(blocks[2], offset, share, 1),
        lax.dynamic_slice_in_dim(blocks[3], offset, share, 1),
    ]
    return (owned, new_moments, vector_sum, grad_norm, clip)


def general_shards(
    tokens,
    segments,
    out_grad,
    norm_params,
    norm_first,
    norm_second,
    qkv_weight,
    qkv_moment,
    out_weight,
    out_moment,
    up_weight,
    up_moment,
    down_weight,
    down_moment,
):
    width = tokens.shape[1]
    rows = tokens.shape[0]
    narrow = out_weight.shape[0]
    sequences = rows // SEQ
    heads = width // HEAD_DIM
    everywhere = ("dp", "head")
    inputs = tokens.astype(jnp.float32)
    first, first_plain, first_factor = normalize(inputs, norm_params[0], norm_params[1])
    first_low = first.astype(jnp.bfloat16)
    qkv_full = lax.all_gather(qkv_weight.astype(jnp.bfloat16), "head", axis=1, tiled=True)
    out_full = lax.all_gather(out_weight.astype(jnp.bfloat16), "head", axis=0, tiled=True)
    up_all = lax.all_gather(up_weight.astype(jnp.bfloat16), everywhere, axis=1, tiled=True)
    down_all = lax.all_gather(down_weight.astype(jnp.bfloat16), everywhere, axis=1, tiled=True)
    mixed = jnp.dot(first_low, qkv_full, preferred_element_type=jnp.float32).astype(jnp.bfloat16)
    mixed = mixed.reshape(sequences, SEQ, heads, 3, HEAD_DIM)
    segment_rows = lax.dynamic_slice_in_dim(segments, lax.axis_index("head") * rows, rows, 0)
    segment_rows = segment_rows.reshape(sequences, SEQ)
    query = mixed[:, :, :, 0]
    keys = mixed[:, :, :, 1]
    values = mixed[:, :, :, 2]
    context, lse = lax.map(attend_forward, (query, keys, values, segment_rows))
    context = context.reshape(rows, width)
    attended = jnp.dot(context, out_full, preferred_element_type=jnp.float32)
    middle = inputs + attended
    second, second_plain, second_factor = normalize(middle, norm_params[2], norm_params[3])
    second_low = second.astype(jnp.bfloat16)
    hidden = jnp.dot(second_low, up_all, preferred_element_type=jnp.float32)
    switch = jax.nn.sigmoid(1.702 * hidden)
    active = (hidden * switch).astype(jnp.bfloat16)
    result = middle + lax.dot_general(
        active, down_all, (((1,), (1,)), ((), ())), preferred_element_type=jnp.float32
    )
    layer_out = result.astype(jnp.bfloat16)
    down_grad = lax.dot_general(
        out_grad, active, (((0,), (0,)), ((), ())), preferred_element_type=jnp.float32
    )
    active_grad = jnp.dot(out_grad, down_all, preferred_element_type=jnp.float32)
    hidden_grad = (active_grad * (switch + 1.702 * hidden * switch * (1.0 - switch))).astype(
        jnp.bfloat16
    )
    up_grad = lax.dot_general(
        second_low, hidden_grad, (((0,), (0,)), ((), ())), preferred_element_type=jnp.float32
    )
    second_grad = lax.dot_general(
        hidden_grad, up_all, (((1,), (1,)), ((), ())), preferred_element_type=jnp.float32
    )
    middle_lower, gain_two, shift_two = normalize_back(
        second_grad, second_plain, second_factor, norm_params[2]
    )
    middle_grad = out_grad.astype(jnp.float32) + middle_lower
    attended_low = middle_grad.astype(jnp.bfloat16)
    context_grad = lax.dot_general(
        attended_low, out_full, (((1,), (1,)), ((), ())), preferred_element_type=jnp.float32
    ).astype(jnp.bfloat16)
    whole_out = lax.dot_general(
        context, attended_low, (((0,), (0,)), ((), ())), preferred_element_type=jnp.float32
    )
    context_grad = context_grad.reshape(sequences, SEQ, heads, HEAD_DIM)
    mixed_grad = lax.map(attend_backward, (query, keys, values, segment_rows, context_grad, lse))
    mixed_grad = mixed_grad.reshape(rows, 3 * width)
    whole_qkv = lax.dot_general(
        first_low, mixed_grad, (((0,), (0,)), ((), ())), preferred_element_type=jnp.float32
    )
    first_grad = lax.dot_general(
        mixed_grad, qkv_full, (((1,), (1,)), ((), ())), preferred_element_type=jnp.float32
    )
    input_lower, gain_one, shift_one = normalize_back(
        first_grad, first_plain, first_factor, norm_params[0]
    )
    input_grad = middle_grad + input_lower
    vector_part = jnp.stack([gain_one, shift_one, gain_two, shift_two])
    (owned, new_moments, vector_sum, grad_norm, clip) = general_update(
        whole_qkv, whole_out, up_grad, down_grad, vector_part,
        qkv_moment, out_moment, up_moment, down_moment,
    )
    weights = [qkv_weight, out_weight, up_weight, down_weight]
    factors = [
        math.sqrt(3.0),
        math.sqrt(SEQ / 8.0),
        math.sqrt(max(1.0, FF / width)),
        math.sqrt(max(1.0, FF / width)),
    ]
    new_weights = [
        weights[index] * (1.0 - muon_rate * muon_decay)
        - muon_rate * factors[index] * owned[index].astype(jnp.float32)
        for index in range(4)
    ]
    clipped = clip * vector_sum
    first_new = beta_one * norm_first + (1.0 - beta_one) * clipped
    second_new = beta_two * norm_second + (1.0 - beta_two) * clipped * clipped
    return (
        layer_out,
        input_grad,
        grad_norm,
        clipped,
        first_new,
        second_new,
        new_weights[0],
        new_moments[0],
        new_weights[1],
        new_moments[1],
        new_weights[2],
        new_moments[2],
        new_weights[3],
        new_moments[3],
    )


def solution(mesh):
    placed = (
        P(("dp", "head"), None),
        P("dp"),
        P(("dp", "head"), None),
        P(),
        P(),
        P(),
        P(None, "head"),
        P(None, "head"),
        P("head", None),
        P("head", None),
        P(None, ("dp", "head")),
        P(None, ("dp", "head")),
        P(None, ("dp", "head")),
        P(None, ("dp", "head")),
    )
    fast = mesh.shape["dp"] == 8 and mesh.shape["head"] == 4
    return jax.shard_map(
        fast_shards if fast else general_shards,
        mesh=mesh,
        in_specs=placed,
        out_specs=(
            P(("dp", "head"), None),
            P(("dp", "head"), None),
            P(),
            P(),
            P(),
            P(),
            P(None, "head"),
            P(None, "head"),
            P("head", None),
            P("head", None),
            P(None, ("dp", "head")),
            P(None, ("dp", "head")),
            P(None, ("dp", "head")),
            P(None, ("dp", "head")),
        ),
        check_vma=False,
    )
```

```python
import math

import jax
import jax.numpy as jnp
from jax import lax
from jax.experimental import pallas as pl
from jax.experimental.pallas import tpu as pltpu
from jax.sharding import PartitionSpec as P

HEAD_DIM = 64
FF = 2048
SEQ = 512
NS_STEPS = 5


neg_fill = -1000000000.0
norm_eps = 1e-05
ns_a = 3.4445
ns_b = -4.775
ns_c = 2.0315
momentum_decay = 0.95
muon_rate = 0.5
muon_decay = 0.01
beta_one = 0.9
beta_two = 0.95


def normalize(values, gain, shift):
    mean = jnp.mean(values, axis=-1, keepdims=True)
    centered = values - mean
    factor = lax.rsqrt(jnp.mean(centered * centered, axis=-1, keepdims=True) + norm_eps)
    plain = centered * factor
    return (plain * gain + shift, plain, factor)


def normalize_back(upper, plain, factor, gain):
    inner = upper * gain
    lower = factor * (
        inner
        - jnp.mean(inner, axis=-1, keepdims=True)
        - plain * jnp.mean(inner * plain, axis=-1, keepdims=True)
    )
    return (lower, jnp.sum(upper * plain, axis=0), jnp.sum(upper, axis=0))


def masked_scores(query, keys, segment):
    scores = jnp.einsum(
        "qhd,khd->hqk", query, keys, preferred_element_type=jnp.float32
    ) * HEAD_DIM ** (-0.5)
    same = segment[:, None] == segment[None, :]
    return jnp.where(same[None], scores, neg_fill)


def attend_forward(block):
    query, keys, values, segment = block
    scores = masked_scores(query, keys, segment)
    top = jnp.max(scores, axis=-1, keepdims=True)
    weights = jnp.exp(scores - top)
    total = jnp.sum(weights, axis=-1, keepdims=True)
    probs = (weights / total).astype(jnp.bfloat16)
    context = jnp.einsum("hqk,khd->qhd", probs, values, preferred_element_type=jnp.float32)
    return (context.astype(jnp.bfloat16), top + jnp.log(total))


def attend_backward(block):
    query, keys, values, segment, context_grad, lse = block
    scores = masked_scores(query, keys, segment)
    probs = jnp.exp(scores - lse)
    probs_low = probs.astype(jnp.bfloat16)
    probs_grad = jnp.einsum(
        "qhd,khd->hqk", context_grad, values, preferred_element_type=jnp.float32
    )
    inner = jnp.sum(probs * probs_grad, axis=-1, keepdims=True)
    score_grad = (probs * (probs_grad - inner)).astype(jnp.bfloat16)
    query_grad = jnp.einsum(
        "hqk,khd->qhd", score_grad, keys, preferred_element_type=jnp.float32
    ) * HEAD_DIM ** (-0.5)
    key_grad = jnp.einsum(
        "hqk,qhd->khd", score_grad, query, preferred_element_type=jnp.float32
    ) * HEAD_DIM ** (-0.5)
    value_grad = jnp.einsum(
        "hqk,qhd->khd", probs_low, context_grad, preferred_element_type=jnp.float32
    )
    return jnp.stack([query_grad, key_grad, value_grad], axis=2).astype(jnp.bfloat16)


def gram_left(block):
    return lax.dot_general(
        block, block, (((1,), (1,)), ((), ())), preferred_element_type=jnp.float32
    )


def gram_right(block):
    return lax.dot_general(
        block, block, (((0,), (0,)), ((), ())), preferred_element_type=jnp.float32
    )


def squares_of(moment, grad, weight):
    return (
        jnp.stack([jnp.sum(moment * moment), jnp.sum(moment * grad), jnp.sum(grad * grad)]) * weight
    )


ROWS = 1024
TILE = 512
PAIRS = 4
WIDE = 2048
CHUNK = 512
VMEM_BYTES = 62 << 20
LOW = jnp.bfloat16
F32 = jnp.float32


def dot(one, two):
    return jnp.dot(one, two, preferred_element_type=F32)


def dot_back(one, two):
    return lax.dot_general(one, two, (((1,), (1,)), ((), ())), preferred_element_type=F32)


def dot_rows(one, two):
    return lax.dot_general(one, two, (((0,), (0,)), ((), ())), preferred_element_type=F32)


def each(count, body):
    def step(i, carry):
        body(i)
        return carry

    lax.fori_loop(0, count, step, 0)


def rows_at(i, size):
    return pl.ds(pl.multiple_of(i * size, size), size)


def first_phase(tokens, params, first):
    gain = params[0:1, :]
    shift = params[1:2, :]

    def body(i):
        here = rows_at(i, 128)
        plain_gain, _, _ = normalize(tokens[here, :].astype(F32), gain, shift)
        first[here, :] = plain_gain.astype(LOW)

    each(ROWS // 128, body)


def mixed_phase(pair, first, wqkv, mixed):
    def body(i):
        mixed[pair] = dot(first[...], wqkv[pair]).astype(LOW)

    body(0)


def bias_phase(segments, head, bias):
    turned = segments[...].astype(F32).T
    lane = lax.broadcasted_iota(jnp.int32, (1, segments.shape[0]), 1)

    for seq in range(ROWS // SEQ):
        which = head * (ROWS // SEQ) + seq
        row = segments[pl.ds(which, 1), :].astype(F32)
        column = jnp.sum(jnp.where(lane == which, turned, 0.0), axis=1, keepdims=True)
        bias[seq * SEQ : seq * SEQ + SEQ, :] = jnp.where(column == row, 0.0, neg_fill).astype(LOW)


def attend_phase(pair, mixed, bias, probs, context):
    lane = lax.broadcasted_iota(jnp.int32, (1, 128), 1)
    left = (lane < HEAD_DIM).astype(LOW)

    def body(seq):
        here = rows_at(seq, SEQ)
        query = mixed[pair, here, 0:128] * LOW(HEAD_DIM ** (-0.5))
        keys = mixed[pair, here, 128:256]
        values = mixed[pair, here, 256:384]
        allowed = bias[here, :].astype(F32)
        outs = []
        for half in range(2):
            mask = left if half == 0 else LOW(1.0) - left
            scores = dot_back(keys, query * mask) + allowed
            top = jnp.max(scores, axis=0, keepdims=True)
            weights = jnp.exp(scores - top)
            total = jnp.sum(weights, axis=0, keepdims=True)
            prob = (weights * (1.0 / total)).astype(LOW)
            probs[pair * 4 + half * 2 + seq] = prob
            outs.append(dot_rows(prob, values))
        context[here, pl.ds(pl.multiple_of(pair * 128, 128), 128)] = jnp.where(
            lane < HEAD_DIM, outs[0], outs[1]
        ).astype(LOW)

    each(ROWS // SEQ, body)


def second_phase(tokens, context, wout, params, middle, second):
    gain = params[2:3, :]
    shift = params[3:4, :]

    def body(i):
        here = rows_at(i, TILE)
        value = tokens[here, :].astype(F32) + dot(context[here, :], wout[...])
        middle[here, :] = value
        normal, _, _ = normalize(value, gain, shift)
        second[here, :] = normal.astype(LOW)

    each(ROWS // TILE, body)


def turn_phase(src, dst):
    def body(i):
        here = rows_at(i, 256)
        dst[:, here] = src[here, :].T

    each(ROWS // 256, body)


def feed_phase(
    chunk, second, second_t, out_grad, out_grad_t, up, down, active, hidden_grad,
    result, second_grad, g_up, g_down,
):
    units = rows_at(chunk, CHUNK)

    def body(i):
        here = rows_at(i, TILE)
        hidden = dot_back(second[here, :], up[units, :])
        switch = 0.5 * jnp.tanh(0.851 * hidden) + 0.5
        act = (hidden * switch).astype(LOW)
        active[here, :] = act
        grad = dot_back(out_grad[here, :], down[units, :])
        back = (grad * (switch + 1.702 * hidden * switch * (1.0 - switch))).astype(LOW)
        hidden_grad[here, :] = back
        result[here, :] += dot(act, down[units, :])
        second_grad[here, :] += dot(back, up[units, :])

    each(ROWS // TILE, body)

    for turned, wide, out in ((out_grad_t, active, g_down), (second_t, hidden_grad, g_up)):
        grad = dot(turned[...], wide[...]).astype(LOW)
        for j in range(CHUNK // 128):
            for c in range(2):
                out[chunk * 8 + j * 2 + c] = grad[c * 256 : c * 256 + 256, j * 128 : j * 128 + 128]


def middle_phase(
    params, middle, result, second_grad, out_grad, wout,
    layer_out, middle_grad, attended_low, context_grad, norms,
):
    gain = params[2:3, :]

    def body(i, sums):
        here = rows_at(i, TILE)
        value = middle[here, :]
        layer_out[here, :] = (value + result[here, :]).astype(LOW)
        _, plain, factor = normalize(value, gain, gain)
        upper = second_grad[here, :]
        lower, gains, shifts = normalize_back(upper, plain, factor, gain)
        total = out_grad[here, :].astype(F32) + lower
        middle_grad[here, :] = total
        low = total.astype(LOW)
        attended_low[here, :] = low
        context_grad[here, :] = dot_back(low, wout[...]).astype(LOW)
        return (sums[0] + gains[None], sums[1] + shifts[None])

    zero = jnp.zeros((1, 512), F32)
    sums = lax.fori_loop(0, ROWS // TILE, body, (zero, zero))
    norms[2:3, :] = sums[0]
    norms[3:4, :] = sums[1]


def out_phase(attended_t, context, g_attend):
    def body(i):
        here = rows_at(i, 512)
        grad = dot(attended_t[here, :], context[...]).astype(LOW)
        for p in range(PAIRS):
            g_attend[p, here, 384:512] = grad[:, p * 128 : p * 128 + 128]

    body(0)


def attend_back_phase(pair, seq, mixed, probs, context, context_grad):
    lane = lax.broadcasted_iota(jnp.int32, (1, 128), 1)
    left = (lane < HEAD_DIM).astype(LOW)
    scale = HEAD_DIM ** (-0.5)
    here = rows_at(seq, SEQ)
    query = mixed[pair, here, 0:128]
    keys = mixed[pair, here, 128:256]
    values = mixed[pair, here, 256:384]
    upper = context_grad[here, pl.ds(pl.multiple_of(pair * 128, 128), 128)]
    product = upper.astype(F32) * context[
        here, pl.ds(pl.multiple_of(pair * 128, 128), 128)
    ].astype(F32)
    product_high = product.astype(LOW)
    product_low = (product - product_high.astype(F32)).astype(LOW)
    marks = lax.broadcasted_iota(jnp.int32, (8, 128), 1) // HEAD_DIM
    marks = (marks == lax.broadcasted_iota(jnp.int32, (8, 128), 0)).astype(LOW)
    inners = dot_back(marks, product_high) + dot_back(marks, product_low)
    outs = []
    for half in range(2):
        mask = left if half == 0 else LOW(1.0) - left
        above = upper * mask
        prob_low = probs[pair * 4 + half * 2 + seq]
        prob = prob_low.astype(F32)
        prob_grad = dot_back(values, above)
        inner = inners[half : half + 1, :]
        score_grad = (prob * (prob_grad - inner)).astype(LOW)
        outs.append((dot_rows(score_grad, keys), dot(score_grad, query), dot(prob_low, above)))
    pick = lane < HEAD_DIM
    mixed[pair, here, 0:128] = (jnp.where(pick, outs[0][0], outs[1][0]) * scale).astype(LOW)
    mixed[pair, here, 128:256] = (jnp.where(pick, outs[0][1], outs[1][1]) * scale).astype(LOW)
    mixed[pair, here, 256:384] = (outs[0][2] + outs[1][2]).astype(LOW)


def qkv_phase(pair, mixed, first_t, g_attend):
    g_attend[pair, :, 0:384] = dot(first_t[...], mixed[pair]).astype(LOW)


def input_phase(params, tokens, mixed, wqkv, input_grad, norms):
    gain = params[0:1, :]

    def body(i, sums):
        here = rows_at(i, TILE)
        _, plain, factor = normalize(tokens[here, :].astype(F32), gain, gain)
        first_grad = dot_back(mixed[0, here, :], wqkv[0])
        for pair in range(1, PAIRS):
            first_grad = first_grad + dot_back(mixed[pair, here, :], wqkv[pair])
        lower, gains, shifts = normalize_back(first_grad, plain, factor, gain)
        input_grad[here, :] += lower
        return (sums[0] + gains[None], sums[1] + shifts[None])

    zero = jnp.zeros((1, 512), F32)
    sums = lax.fori_loop(0, ROWS // TILE, body, (zero, zero))
    norms[0:1, :] = sums[0]
    norms[1:2, :] = sums[1]


def local_call(kernel, outs, scratch, args, name):
    vmem = pl.BlockSpec(memory_space=pltpu.VMEM)
    return pl.pallas_call(
        kernel,
        out_shape=tuple(jax.ShapeDtypeStruct(*o) for o in outs),
        in_specs=[vmem] * len(args),
        out_specs=(vmem,) * len(outs),
        scratch_shapes=[pltpu.VMEM(*v) for v in scratch],
        compiler_params=pltpu.CompilerParams(vmem_limit_bytes=60 << 20),
        name=name,
    )(*args)


STEP_DIMS = {"c": 1, "x": 2, "y": 4, "l": 8, "g": 16}
GATHERS = (
    (0, 0, 256, ("g", "l", "y", "x")),
    (0, 256, 256, ("g", "x", "l", "y")),
    (1, 0, 128, ("g", "x", "l", "y")),
    (1, 128, 384, ("g", "y", "x", "l")),
)
STARTS = (("g", "l", "y", "x", "c"), ("g", "x", "l", "y", "c"), ("g", "y", "x", "l", "c"))
ATTEND_ORDER = ("c", "x", "y", "l", "g")


def coordinates():
    dp = lax.axis_index("dp")
    head = lax.axis_index("head")
    bits = {
        "c": head % 2,
        "x": head // 2,
        "y": dp % 2,
        "l": (dp // 2) % 2,
        "g": dp // 4,
    }
    steps = {"c": (0, 1), "x": (0, 2), "y": (1, 0), "l": (2, 0), "g": (4, 0)}
    peers = {}
    for name, (along_dp, along_head) in steps.items():
        turn = 1 - 2 * bits[name]
        peers[name] = (dp + along_dp * turn, head + along_head * turn)
    return dp, head, bits, peers


def remote(src, dst, send_sem, recv_sem, peer):
    return pltpu.make_async_remote_copy(
        src_ref=src,
        dst_ref=dst,
        send_sem=send_sem,
        recv_sem=recv_sem,
        device_id=peer,
        device_id_type=pl.DeviceIdType.MESH,
    )


def tile_of(fixed, free, place):
    total = 0
    for name, bit in fixed.items():
        total = total + STEP_DIMS[name] * bit
    for i, name in enumerate(free):
        total = total + STEP_DIMS[name] * ((place // 2**i) % 2)
    return total


def scatter_start(acc, got, base, fixed, name, free, bits, peer, sems, slot):
    for place in range(2 ** len(free)):
        away = tile_of({**fixed, name: 1 - bits[name]}, free, place)
        remote(
            acc.at[away], got.at[base + place], sems[0].at[slot], sems[1].at[slot], peer
        ).start()


def scatter_end(acc, got, base, fixed, name, free, bits, peer, sems, slot):
    count = 2 ** len(free)
    span = got.at[pl.ds(base, count)]
    remote(span, span, sems[0].at[slot], sems[1].at[slot], peer).wait()
    rows = acc.shape[1]

    def body(i):
        here = tile_of({**fixed, name: bits[name]}, free, i)
        acc[here] = (acc[here].astype(F32) + got[base + i].astype(F32)).astype(LOW)

    each(count, body)


def gather_start(ref, done, name, bits, peer, sems, slot):
    fixed = {d: bits[d] for d in STEP_DIMS if d not in done}
    for place in range(2 ** len(done)):
        part = ref.at[tile_of(fixed, done, place)]
        remote(part, part, sems[0].at[slot], sems[1].at[slot], peer).start()


def gather_end(ref, done, peer, sems, slot):
    span = ref.at[pl.ds(0, 2 ** len(done))]
    remote(span, span, sems[0].at[slot], sems[1].at[slot], peer).wait()


def paired(block):
    parts = [block[:, i * 64 : i * 64 + 64] for i in (0, 3, 1, 4, 2, 5)]
    return jnp.concatenate(parts, axis=1)


def unpaired(block):
    parts = [block[:, i * 64 : i * 64 + 64] for i in (0, 2, 4, 1, 3, 5)]
    return jnp.concatenate(parts, axis=1)


class Slots:
    def __init__(self):
        self.used = 0

    def __call__(self, count):
        start = self.used
        self.used += count
        return start


def update_step(pool, now, later, count, blocks, lanes, gram, mix):
    def gram_body(i):
        rows = rows_at(i, TILE)
        total = dot_back(pool[now, rows, :], pool[now])
        for b in range(1, count):
            total = total + dot_back(pool[now + b, rows, :], pool[now + b])
        gram[rows, :] = total.astype(LOW)

    each(512 // TILE, gram_body)

    def mix_body(i):
        rows = rows_at(i, TILE)
        own = gram[rows, :]
        mix[rows, :] = (ns_b * own.astype(F32) + ns_c * dot(own, gram[...])).astype(LOW)

    each(512 // TILE, mix_body)

    def next_body(i):
        b = blocks[0] + i
        value = pool[now + b, :, lanes]
        pool[later + b, :, lanes] = (ns_a * value.astype(F32) + dot(mix[...], value)).astype(LOW)

    each(blocks[1], next_body)


def layer_kernel(
    tokens, segments, out_grad, params, w_qkv, m_qkv, w_out, m_out, w_up, m_up, w_down, m_down,
    layer_out, input_grad, start_a, start_u, start_d, ortho_q, ortho_o, ortho_u, ortho_d, norm_sum, scal,
    first, mixed, context, bias, wqkv, wout, wup, wdown, pool, middle, second, second_t, out_grad_t,
    active, hidden_grad, result, second_grad, acc_a, acc_u, acc_d, got_a, got_u, got_d,
    mom_full, mom_x, mom_u, mom_d, mom_a, norm_got, stat_got, gram, mix, send, recv,
):
    dp, head, bits, peers = coordinates()
    me = dp * 4 + head
    sibling = peers["c"]
    across = (dp, 3 - head)
    sems = (send, recv)
    slots = Slots()
    S_Q, S_O, S_M, S_MA = slots(4), slots(4), slots(2), slots(4)
    S_W, S_CORE, S_CHUNK, S_LG = slots(16), slots(20), slots(24), slots(16)
    S_A, S_NORM, S_STAT, S_START, S_SIDE, S_ORTHO = (
        slots(12), slots(1), slots(1), slots(15), slots(2), slots(8)
    )
    barrier = pltpu.get_barrier_semaphore()

    def greet(i):
        other = (me + 1 + i) % 32
        pl.semaphore_signal(
            barrier, inc=1, device_id=(other // 4, other % 4), device_id_type=pl.DeviceIdType.MESH
        )

    each(31, greet)
    wqkv[head] = paired(w_qkv[...].astype(LOW))
    wout[pl.ds(pl.multiple_of(head * 128, 128), 128), :] = w_out[...].astype(LOW)
    mine = pl.ds(pl.multiple_of(me * 64, 64), 64)
    wup[mine, :] = w_up[...].astype(LOW)
    wdown[mine, :] = w_down[...].astype(LOW)
    pl.semaphore_wait(barrier, 31)

    def block_q(who):
        return wqkv.at[who]

    def block_o(who):
        return wout.at[pl.ds(pl.multiple_of(who * 128, 128), 128)]

    def weight_copy(block, who, slot, peer):
        return remote(block(who), block(who), send.at[slot], recv.at[slot], peer)

    weight_copy(block_q, head, S_Q + 1, sibling).start()
    weight_copy(block_q, head, S_Q + 2, peers["x"]).start()
    other_half = pl.ds(pl.multiple_of((1 - bits["c"]) * 256, 256), 256)

    def moment_copy(i, ref):
        return remote(ref.at[:, other_half], mom_x.at[i], send.at[S_M + i], recv.at[S_M + i], sibling)

    moment_copy(0, m_up).start()
    moment_copy(1, m_down).start()

    def weight_tiles(k, far):
        for i, (matrix, start, count, order) in enumerate(GATHERS):
            done = order[: max(k, 0)]
            fixed = {d: bits[d] for d in STEP_DIMS if d not in done}
            if far and k >= 0:
                fixed[order[k]] = 1 - bits[order[k]]
            name = "c" if far else order[k]
            slot = S_CORE + i * 5 + k + 1 if far else S_W + i * 4 + k
            for place in range(2 ** len(done)):
                row = pl.multiple_of(tile_of(fixed, done, place) * 64, 64)
                part = (wup, wdown)[matrix].at[pl.ds(row, 64), pl.ds(start, count)]
                remote(part, part, send.at[slot], recv.at[slot], peers[name]).start()

    def weight_wait(k, far):
        for i, (matrix, start, count, order) in enumerate(GATHERS):
            slot = S_CORE + i * 5 + k + 1 if far else S_W + i * 4 + k
            span = (wup, wdown)[matrix].at[pl.ds(0, 64 * 2 ** max(k, 0)), pl.ds(start, count)]
            remote(span, span, send.at[slot], recv.at[slot], sibling).wait()

    def weight_step(k):
        weight_wait(k, False)
        if k < 3:
            weight_tiles(k + 1, False)
        weight_tiles(k, True)

    weight_tiles(0, False)
    weight_tiles(-1, True)
    weight_copy(block_o, head, S_O + 1, sibling).start()
    weight_copy(block_o, head, S_O + 2, peers["x"]).start()
    first_phase(tokens, params, first)
    bias_phase(segments, head, bias)
    mom_full[:, 0:384] = paired(m_qkv[...])
    mom_full[:, 384:512] = m_out[...].T

    def rank_of(c, x):
        return c * 16 + x * 8 + bits["y"] * 4 + bits["l"] * 2 + bits["g"]

    def rank_rows(who):
        return pl.ds(pl.multiple_of(rank_of(who % 2, who // 2) * 16, 16), 16)

    partners = (sibling, peers["x"], across)

    def rows_copy(j):
        who = partners[j][1]
        return remote(
            mom_full.at[rank_rows(who)], mom_a.at[head], send.at[S_MA + j], recv.at[S_MA + j], partners[j]
        )

    for j in range(3):
        rows_copy(j).start()
    mom_a[head] = mom_full[rank_rows(head), :]

    def pair_body(j):
        pair = (bits["c"] + j % 2) % 2 + 2 * ((bits["x"] + j // 2) % 2)
        mixed_phase(pair, first, wqkv, mixed)
        attend_phase(pair, mixed, bias, pool, context)

        @pl.when(j == 0)
        def _():
            weight_step(0)
            turn_phase(out_grad, out_grad_t)
            weight_copy(block_q, head, S_Q + 1, sibling).wait()
            weight_copy(block_o, head, S_O + 1, sibling).wait()

        @pl.when(j == 1)
        def _():
            weight_copy(block_q, head, S_Q + 2, peers["x"]).wait()
            weight_copy(block_q, peers["x"][1], S_Q + 3, sibling).start()
            weight_step(1)
            weight_copy(block_o, head, S_O + 2, peers["x"]).wait()
            weight_copy(block_o, peers["x"][1], S_O + 3, sibling).start()

        @pl.when(j == 2)
        def _():
            weight_copy(block_q, head, S_Q + 3, sibling).wait()
            weight_copy(block_o, head, S_O + 3, sibling).wait()

    each(PAIRS, pair_body)
    weight_step(2)
    second_phase(tokens, context, wout, params, middle, second)
    turn_phase(second, second_t)
    result[...] = jnp.zeros_like(result)
    second_grad[...] = jnp.zeros_like(second_grad)
    weight_step(3)
    for k in range(-1, 4):
        weight_wait(k, True)

    chunk_orders = ((acc_u, got_u, ("c", "x", "y")), (acc_d, got_d, ("c", "y", "x")))

    def chunk_args(q, k, order):
        fixed = {"g": q // 2, "l": q % 2}
        for name in order[:k]:
            fixed[name] = bits[name]
        return fixed, order[k], order[k + 1 :]

    def chunk_start(q, k):
        for i, (acc, got, order) in enumerate(chunk_orders):
            fixed, name, free = chunk_args(q, k, order)
            scatter_start(
                acc, got, q * 7 + (0, 4, 6)[k], fixed, name, free, bits, peers[name], sems,
                S_CHUNK + q * 6 + i * 3 + k,
            )

    def chunk_end(q, k):
        for i, (acc, got, order) in enumerate(chunk_orders):
            fixed, name, free = chunk_args(q, k, order)
            scatter_end(
                acc, got, q * 7 + (0, 4, 6)[k], fixed, name, free, bits, peers[name], sems,
                S_CHUNK + q * 6 + i * 3 + k,
            )

    def feed_body(q):
        feed_phase(
            q, second, second_t, out_grad, out_grad_t, wup, wdown, active, hidden_grad,
            result, second_grad, acc_u, acc_d,
        )
        chunk_start(q, 0)

        @pl.when(q >= 1)
        def _():
            chunk_end(q - 1, 0)
            chunk_start(q - 1, 1)

        @pl.when(q >= 3)
        def _():
            chunk_end(q - 3, 1)
            chunk_start(q - 3, 2)

    each(WIDE // CHUNK, feed_body)
    middle_phase(
        params, middle, result, second_grad, out_grad, wout,
        layer_out, input_grad, second, active, norm_got.at[me],
    )
    chunk_end(3, 0)
    chunk_start(3, 1)
    chunk_end(1, 1)
    chunk_start(1, 2)
    turn_phase(second, second_t)
    out_phase(second_t, context, acc_a)
    turn_phase(first, second_t)

    depth = dp // 2

    def owner_copy(i, acc, got, q):
        tile = tile_of({"g": q // 2, "l": q % 2, "c": bits["c"], "x": bits["x"], "y": bits["y"]}, (), 0)
        other = (2 * q + bits["y"], head)
        return remote(
            acc.at[tile], got.at[28 + (depth - q + 3) % 4], send.at[S_LG + 2 * q + i],
            recv.at[S_LG + 8 + 3 * i + (depth - q + 3) % 4], other,
        )

    def owner_start(q):
        @pl.when(depth != q)
        def _():
            for i, (acc, got, _) in enumerate(chunk_orders):
                owner_copy(i, acc, got, q).start()

    def owner_sent(q):
        @pl.when(depth != q)
        def _():
            for i, (acc, got, _) in enumerate(chunk_orders):
                owner_copy(i, acc, got, q).wait_send()

    def owner_end():
        for i, (acc, got, _) in enumerate(chunk_orders):
            for way in range(3):
                remote(
                    got.at[28 + way], got.at[28 + way], send.at[S_LG], recv.at[S_LG + 8 + 3 * i + way], sibling
                ).wait_recv()
            total = acc[me].astype(F32)
            for way in range(3):
                total = total + got[28 + way].astype(F32)
            acc[me] = total.astype(LOW)

    spans = []
    low_row = 0
    for k, name in enumerate(ATTEND_ORDER):
        size = 256 >> k
        spans.append((name, size, low_row + bits[name] * size, low_row + (1 - bits[name]) * size))
        low_row = low_row + bits[name] * size

    def aligned(row, size):
        return pl.ds(pl.multiple_of(row, 16), size)

    def attend_copy(pair, k):
        name, size, _, give = spans[k]
        return remote(
            acc_a.at[pair, aligned(give, size)], got_a.at[pair, pl.ds(512 - 2 * size, size)],
            send.at[S_A + pair * 3 + k], recv.at[S_A + pair * 3 + k], peers[name],
        )

    quarter = spans[1][2]

    def place_of(group):
        return (group % 2) * 4 + ((group // 2) % 2) * 2 + group // 4

    def attend_start(pair, k):
        if k < 2:
            attend_copy(pair, k).start()
            return

        def body(i):
            other = (dp + 1 + i) % 8
            remote(
                acc_a.at[pair, aligned(quarter + place_of(other) * 16, 16)],
                got_a.at[pair, aligned(384 + (6 - i) * 16, 16)],
                send.at[S_A + pair * 3 + 2], recv.at[S_A + pair * 3 + 2], (other, head),
            ).start()

        each(7, body)

    def attend_next(pair, k):
        if k == 2:
            span = got_a.at[pair, pl.ds(384, 112)]
            remote(span, span, send.at[S_A + pair * 3 + 2], recv.at[S_A + pair * 3 + 2], sibling).wait()
            here = aligned(low_row, 16)
            total = acc_a[pair, here, :].astype(F32)
            for i in range(1, 8):
                total = total + got_a[pair, 368 + i * 16 : 384 + i * 16, :].astype(F32)
            acc_a[pair, here, :] = total.astype(LOW)
            return
        attend_copy(pair, k).wait()
        _, size, keep, _ = spans[k]

        def body(i):
            here = aligned(keep + i * 64, 64)
            come = aligned(512 - 2 * size + i * 64, 64)
            acc_a[pair, here, :] = (
                acc_a[pair, here, :].astype(F32) + got_a[pair, come, :].astype(F32)
            ).astype(LOW)

        each(size // 64, body)
        attend_start(pair, k + 1)

    def at(wanted, pair):
        return pl.when(pair == wanted)

    def back_body(pair):
        attend_back_phase(pair, 0, mixed, pool, context, active)

        @at(0, pair)
        def _():
            chunk_end(0, 2)
            owner_start(0)
            chunk_end(2, 1)
            chunk_start(2, 2)

        @at(1, pair)
        def _():
            attend_next(0, 0)
            chunk_end(3, 1)
            chunk_start(3, 2)

        @at(2, pair)
        def _():
            attend_next(1, 0)
            attend_next(0, 1)

        @at(3, pair)
        def _():
            attend_next(2, 0)
            attend_next(1, 1)

        attend_back_phase(pair, 1, mixed, pool, context, active)
        qkv_phase(pair, mixed, second_t, acc_a)
        attend_start(pair, 0)

        @at(0, pair)
        def _():
            chunk_end(1, 2)
            owner_start(1)

        @at(1, pair)
        def _():
            chunk_end(2, 2)
            owner_start(2)

        @at(2, pair)
        def _():
            chunk_end(3, 2)
            owner_start(3)

    each(PAIRS, back_body)
    attend_next(3, 0)
    attend_next(2, 1)
    attend_next(0, 2)
    input_phase(params, tokens, mixed, wqkv, input_grad, norm_got.at[me])

    def tell_norm(i):
        other = (me + 1 + i) % 32
        remote(
            norm_got.at[me], norm_got.at[me], send.at[S_NORM], recv.at[S_NORM], (other // 4, other % 4)
        ).start()

    attend_next(3, 1)
    each(31, tell_norm)
    attend_next(1, 2)
    for q in range(4):
        owner_sent(q)
    owner_end()
    moment_copy(0, m_up).wait()
    moment_copy(1, m_down).wait()
    keep_half = pl.ds(pl.multiple_of(bits["c"] * 256, 256), 256)
    for i, (ref, out) in enumerate(((m_up, mom_u), (m_down, mom_d))):
        own = ref[:, keep_half]
        far = mom_x[i]
        low_half = jnp.where(bits["c"] == 0, own, far)
        high_half = jnp.where(bits["c"] == 0, far, own)
        out[...] = jnp.concatenate([low_half, high_half], axis=0).T
    for j in range(3):
        rows_copy(j).wait()

    def total_of(value):
        return jnp.sum(jnp.sum(value, axis=0, keepdims=True), axis=1, keepdims=True)

    lane = lax.broadcasted_iota(jnp.int32, (8, 128), 1)
    column = lax.broadcasted_iota(jnp.int32, (1, 512), 1)
    grad_u = acc_u[me].astype(F32)
    grad_d = acc_d[me].astype(F32)
    stats = jnp.zeros((8, 128), F32)
    for m, (moment, grad) in enumerate(((mom_u[...], grad_u), (mom_d[...], grad_d))):
        for i, product in enumerate((moment * moment, moment * grad, grad * grad)):
            stats = jnp.where(lane == 6 + 3 * m + i, total_of(product), stats)
    attend_next(2, 2)
    attend_next(3, 2)
    span = norm_got.at[pl.ds(0, 31)]
    remote(span, span, send.at[S_NORM], recv.at[S_NORM], sibling).wait()
    vector = norm_got[0]
    for i in range(1, 32):
        vector = vector + norm_got[i]
    norm_sum[...] = vector
    vector_total = total_of(vector * vector)
    my_rows = aligned(low_row, 16)
    for i in range(3):
        inside = jnp.zeros((1, 512), F32)
        for pair in range(PAIRS):
            moment = mom_a[pair]
            grad = acc_a[pair, my_rows, :].astype(F32)
            product = (moment * moment, moment * grad, grad * grad)[i]
            inside = inside + jnp.sum(product, axis=0, keepdims=True)
        stats = jnp.where(lane == i, total_of(jnp.where(column < 384, inside, 0.0)), stats)
        stats = jnp.where(lane == 3 + i, total_of(jnp.where(column < 384, 0.0, inside)), stats)
    stat_got[me] = stats

    def tell(i):
        other = (me + 1 + i) % 32
        remote(
            stat_got.at[me], stat_got.at[me], send.at[S_STAT], recv.at[S_STAT], (other // 4, other % 4)
        ).start()

    each(31, tell)
    span = stat_got.at[pl.ds(0, 31)]
    remote(span, span, send.at[S_STAT], recv.at[S_STAT], sibling).wait()
    stats = jnp.sum(stat_got[...], axis=0)

    def stat(i):
        return jnp.sum(jnp.where(lane == i, stats, 0.0), axis=1, keepdims=True)[0:1]

    norm = jnp.sqrt(stat(2) + stat(5) + stat(8) + stat(11) + vector_total)
    clip = jnp.minimum(1.0, 1.0 / (norm + 1e-06))
    sizes = []
    for m in range(4):
        square = (
            momentum_decay * momentum_decay * stat(3 * m)
            + 2.0 * momentum_decay * clip * stat(3 * m + 1)
            + clip * clip * stat(3 * m + 2)
        )
        sizes.append(jnp.sqrt(jnp.maximum(square, 0.0)) + 1e-07)
    told = jnp.where(lane == 0, norm, clip)
    for m in range(4):
        told = jnp.where(lane == 2 + m, sizes[m], told)
    scal[...] = told
    scale_a = jnp.where(column < 384, 1.0 / sizes[0], 1.0 / sizes[1])
    got_u[me] = ((momentum_decay * mom_u[...] + clip * grad_u) * (1.0 / sizes[2])).astype(LOW)
    got_d[me] = ((momentum_decay * mom_d[...] + clip * grad_d) * (1.0 / sizes[3])).astype(LOW)
    for pair in range(PAIRS):
        grad = acc_a[pair, my_rows, :].astype(F32)
        pool[pair, my_rows, :] = ((momentum_decay * mom_a[pair] + clip * grad) * scale_a).astype(LOW)

    mine_half = pl.ds(pl.multiple_of(bits["c"] * 256, 256), 256)

    def side_copy(i):
        src, dst = ((got_u, start_u), (got_d, start_d))[i]
        return remote(
            src.at[me], dst.at[mine_half], send.at[S_SIDE + i], recv.at[S_SIDE + i], sibling
        )

    side_copy(0).start()
    side_copy(1).start()
    start_u[mine_half, :] = got_u[me]
    start_d[mine_half, :] = got_d[me]

    def start_copy(k):
        name, size, keep, _ = spans[4 - k]
        part = pool.at[pl.ds(0, 4), aligned(keep, size)]
        return remote(part, part, send.at[S_START + 3 * k], recv.at[S_START + 3 * k], peers[name])

    tiles = ((got_u, STARTS[1]), (got_d, STARTS[2]))
    for k in range(5):
        if k > 0:
            start_copy(k - 1).wait()
        if k < 4:
            start_copy(k).start()
        for m, (got, order) in enumerate(tiles):
            if k > 0:
                gather_end(got, order[: k - 1], peers[order[k - 1]], sems, S_START + 3 * k - 2 + m)
            if k < 4:
                gather_start(
                    got, order[:k], order[k], bits, peers[order[k]], sems, S_START + 3 * k + 1 + m
                )
    half_rows = aligned(spans[0][2], 256)
    pair_part = pool.at[pl.ds(head + 1 - 2 * bits["c"], 1), half_rows]
    all_part = pool.at[pl.ds(0, 4), half_rows]

    def core_copy(part):
        return remote(part, part, send.at[S_START + 12], recv.at[S_START + 12], sibling)

    @pl.when(bits["c"] == 1)
    def _():
        core_copy(all_part).start()

        def slice_body(i):
            rows = rows_at(i, 256)
            start_a[rows, :] = pool[head, rows, :]

        for x, (got, order) in enumerate(tiles):
            @pl.when(bits["x"] == x)
            def _(got=got, order=order, x=x):
                span = got.at[pl.ds(0, 16)]
                remote(span, span, send.at[S_START + 13], recv.at[S_START + 13], sibling).wait_recv()

                def body(i):
                    for j in range(4):
                        for c in range(2):
                            pool[4 + i, c * 256 : c * 256 + 256, j * 128 : j * 128 + 128] = got[
                                i * 8 + j * 2 + c
                            ]

                each(4, body)

        core_copy(pair_part).wait_recv()
        core_copy(all_part).wait_send()
        each(2, slice_body)

    @pl.when(bits["c"] == 0)
    def _():
        for x, (got, order) in enumerate(tiles):
            @pl.when(bits["x"] == x)
            def _(got=got, order=order):
                gather_start(got, order[:4], "c", bits, sibling, sems, S_START + 13)

        core_copy(pair_part).start()
        core_copy(all_part).wait_recv()

        def body(i):
            rows = rows_at(i, 256)
            start_a[rows, :] = pool[head, rows, :]
            for p in range(PAIRS):
                for r in range(3):
                    group = p * 3 + r
                    pool[4 + group // 4, rows, (group % 4) * 128 : (group % 4) * 128 + 128] = pool[
                        p, rows, r * 128 : r * 128 + 128
                    ]
                pool[7, rows, p * 128 : p * 128 + 128] = pool[p, rows, 384:512]

        each(2, body)
        core_copy(pair_part).wait_send()
        span = got_u.at[pl.ds(0, 16)]
        remote(span, span, send.at[S_START + 13], recv.at[S_START + 13], sibling).wait_send()

    side_copy(0).wait()
    side_copy(1).wait()

    every = pl.ds(0, 512)
    outs = (ortho_u, ortho_d)

    def out_copy(src, dst, i, peer):
        return remote(src, dst, send.at[S_ORTHO + i], recv.at[S_ORTHO + i], peer)

    def group_of(r):
        group = bits["x"] * 6 + r
        return pool.at[8 + group // 4, :, pl.ds(pl.multiple_of((group % 4) * 128, 128), 128)]

    def out_of(who):
        return pool.at[11, :, pl.ds(pl.multiple_of(who * 128, 128), 128)]

    @pl.when(bits["c"] == 0)
    def _():
        def turn_body(turn):
            now = 4 + (turn % 2) * 4
            later = 12 - now
            update_step(pool, now, later, 3, (0, 3), every, gram, mix)
            update_step(pool, now + 3, later + 3, 1, (0, 1), every, gram, mix)

        each(NS_STEPS - 1, turn_body)
        update_step(pool, 4, 8, 3, (bits["x"], 2), every, gram, mix)
        for r in range(3):
            out_copy(group_of(3 + r), ortho_q.at[:, pl.ds(r * 128, 128)], 0, sibling).start()
        for r in range(3):
            ortho_q[:, r * 128 : r * 128 + 128] = group_of(r)[...]
        columns = pl.ds(pl.multiple_of(bits["x"] * 256, 256), 256)
        update_step(pool, 7, 11, 1, (0, 1), columns, gram, mix)
        out_copy(out_of(head + 1), ortho_o, 1, sibling).start()
        ortho_o[...] = out_of(head)[...]
        out_copy(ortho_q, ortho_q, 0, sibling).wait_send()
        out_copy(ortho_o, ortho_o, 1, sibling).wait_send()

    @pl.when(bits["c"] == 1)
    def _():
        def turn_body(turn):
            now = 4 + (turn % 2) * 4
            update_step(pool, now, 12 - now, 4, (0, 4), every, gram, mix)

        each(NS_STEPS - 1, turn_body)
        wanted = dp // 2
        update_step(pool, 4, 8, 4, (wanted, 1), every, gram, mix)

        def block_of(x):
            block = dp * 2 + x
            return pool.at[8 + wanted, :, pl.ds(pl.multiple_of((block % 4) * 128, 128), 128)]

        for x in range(2):
            @pl.when(bits["x"] == x)
            def _(x=x):
                targets = ((across, 1 - x), (peers["x"], 1 - x), (sibling, x))
                for j, (peer, side) in enumerate(targets):
                    remote(
                        block_of(side), outs[x], send.at[S_ORTHO + 2 + j], recv.at[S_ORTHO + 2 + x], peer
                    ).start()
                outs[x][...] = block_of(x)[...]
                for j, (peer, side) in enumerate(targets):
                    remote(
                        block_of(side), outs[x], send.at[S_ORTHO + 2 + j], recv.at[S_ORTHO + 2 + x], peer
                    ).wait_send()

        out_copy(ortho_q, ortho_q, 0, sibling).wait_recv()
        out_copy(ortho_o, ortho_o, 1, sibling).wait_recv()

    for x in range(2):
        @pl.when(head != 2 * x + 1)
        def _(x=x):
            out_copy(outs[x], outs[x], 2 + x, sibling).wait_recv()


def layer_call(*args):
    shape = jax.ShapeDtypeStruct
    vmem = pl.BlockSpec(memory_space=pltpu.VMEM)
    outs = (
        shape((ROWS, 512), LOW), shape((ROWS, 512), F32),
        shape((512, 512), LOW), shape((512, 128), LOW), shape((512, 128), LOW),
        shape((512, 384), LOW), shape((512, 128), LOW), shape((512, 128), LOW), shape((512, 128), LOW),
        shape((4, 512), F32), shape((8, 128), F32),
    )
    scratch = [
        ((ROWS, 512), LOW),
        ((PAIRS, ROWS, 384), LOW),
        ((ROWS, 512), LOW),
        ((ROWS, SEQ), LOW),
        ((PAIRS, 512, 384), LOW),
        ((512, 512), LOW),
        ((WIDE, 512), LOW),
        ((WIDE, 512), LOW),
        ((16, 512, 512), LOW),
        ((ROWS, 512), F32),
        ((ROWS, 512), LOW),
        ((512, ROWS), LOW),
        ((512, ROWS), LOW),
        ((ROWS, CHUNK), LOW),
        ((ROWS, CHUNK), LOW),
        ((ROWS, 512), F32),
        ((ROWS, 512), F32),
        ((PAIRS, 512, 512), LOW),
        ((32, 256, 128), LOW),
        ((32, 256, 128), LOW),
        ((PAIRS, 512, 512), LOW),
        ((32, 256, 128), LOW),
        ((32, 256, 128), LOW),
        ((512, 512), F32),
        ((2, 64, 256), F32),
        ((256, 128), F32),
        ((256, 128), F32),
        ((PAIRS, 16, 512), F32),
        ((32, 4, 512), F32),
        ((32, 8, 128), F32),
        ((512, 512), LOW),
        ((512, 512), LOW),
    ]
    return pl.pallas_call(
        layer_kernel,
        out_shape=outs,
        in_specs=[vmem] * len(args),
        out_specs=(vmem,) * len(outs),
        scratch_shapes=[pltpu.VMEM(*v) for v in scratch]
        + [pltpu.SemaphoreType.DMA((128,)), pltpu.SemaphoreType.DMA((128,))],
        compiler_params=pltpu.CompilerParams(
            collective_id=1, has_side_effects=True, vmem_limit_bytes=VMEM_BYTES
        ),
        name="layer",
    )(*args)


def update_kernel(
    start_a, start_u, start_d, ortho_q, ortho_o, ortho_u, ortho_d, norm_sum, scal,
    w_qkv, w_out, w_up, w_down, norm_first, norm_second,
    new_q, mom_q, new_o, mom_o, new_u, mom_u, new_d, mom_d, clipped, first_new, second_new, norm,
):
    core = lax.axis_index("head") % 2
    clip = scal[0:1, 1:2]
    keep = 1.0 - muon_rate * muon_decay

    def fresh(weight, factor, ortho):
        return weight * keep - muon_rate * factor * ortho

    new_q[...] = fresh(w_qkv[...], math.sqrt(3.0), unpaired(ortho_q[...].astype(F32)))
    mom_q[...] = unpaired(start_a[:, 0:384].astype(F32)) * scal[0:1, 2:3]
    new_o[...] = fresh(w_out[...], math.sqrt(SEQ / 8.0), ortho_o[...].astype(F32).T)
    mom_o[...] = start_a[:, 384:512].astype(F32).T * scal[0:1, 3:4]
    for weight, ortho, start, new, mom, i in (
        (w_up, ortho_u, start_u, new_u, mom_u, 4),
        (w_down, ortho_d, start_d, new_d, mom_d, 5),
    ):
        turned = ortho[...].astype(F32).T
        turned = jnp.where(core == 0, turned[0:64], turned[64:128])
        new[...] = fresh(weight[...], math.sqrt(max(1.0, FF / 512)), turned)
        turned = start[...].astype(F32).T
        mom[...] = jnp.where(core == 0, turned[0:64], turned[64:128]) * scal[0:1, i : i + 1]
    norm[...] = scal[0:1, 0:1]
    clip_grad = clip * norm_sum[...]
    clipped[...] = clip_grad
    first_new[...] = beta_one * norm_first[...] + (1.0 - beta_one) * clip_grad
    second_new[...] = beta_two * norm_second[...] + (1.0 - beta_two) * clip_grad * clip_grad


def fast_shards(
    tokens,
    segments,
    out_grad,
    norm_params,
    norm_first,
    norm_second,
    qkv_weight,
    qkv_moment,
    out_weight,
    out_moment,
    up_weight,
    up_moment,
    down_weight,
    down_moment,
):
    (
        layer_out, input_grad, start_a, start_u, start_d, ortho_q, ortho_o, ortho_u, ortho_d, norm_sum, scal
    ) = layer_call(
        tokens, segments.reshape(segments.shape[0] // SEQ, SEQ), out_grad, norm_params,
        qkv_weight, qkv_moment, out_weight, out_moment,
        up_weight.T, up_moment.T, down_weight.T, down_moment.T,
    )
    tall = ((64, 512), F32)
    new_q, mom_q, new_o, mom_o, new_u, mom_u, new_d, mom_d, clipped, first_new, second_new, norm = local_call(
        update_kernel,
        [((512, 384), F32)] * 2 + [((128, 512), F32)] * 2 + [tall] * 4 + [((4, 512), F32)] * 3 + [((1, 1), F32)],
        [],
        (
            start_a, start_u, start_d, ortho_q, ortho_o, ortho_u, ortho_d, norm_sum, scal,
            qkv_weight, out_weight, up_weight.T, down_weight.T, norm_first, norm_second,
        ),
        "update",
    )
    return (
        layer_out, input_grad, norm.reshape(()), clipped, first_new, second_new,
        new_q, mom_q, new_o, mom_o, new_u.T, mom_u.T, new_d.T, mom_d.T,
    )


def general_update(
    whole_qkv, whole_out, up_grad, down_grad, vector_part,
    qkv_moment, out_moment, up_moment, down_moment,
):
    everywhere = ("dp", "head")
    narrow = out_moment.shape[0]
    up_part, down_part = (
        lax.psum_scatter(
            up_grad.astype(jnp.bfloat16), everywhere, scatter_dimension=1, tiled=True
        ).astype(jnp.float32),
        lax.psum_scatter(
            down_grad.astype(jnp.bfloat16), everywhere, scatter_dimension=1, tiled=True
        ).astype(jnp.float32),
    )
    qkv_part = lax.psum_scatter(
        whole_qkv.astype(jnp.bfloat16), "head", scatter_dimension=1, tiled=True
    )
    out_part = lax.psum_scatter(
        whole_out.astype(jnp.bfloat16), "head", scatter_dimension=0, tiled=True
    )
    qkv_sum, out_sum = (
        lax.psum(qkv_part, "dp").astype(jnp.float32),
        lax.psum(out_part, "dp").astype(jnp.float32),
    )
    leading = (lax.axis_index("dp") == 0).astype(jnp.float32)
    moments = [qkv_moment, out_moment, up_moment, down_moment]
    grads = [qkv_sum, out_sum, up_part, down_part]
    stats = jnp.stack(
        [
            squares_of(qkv_moment, qkv_sum, leading),
            squares_of(out_moment, out_sum, leading),
            squares_of(up_moment, up_part, 1.0),
            squares_of(down_moment, down_part, 1.0),
        ]
    )
    vector_sum, stat_sum = lax.psum((vector_part, stats), everywhere)
    grad_norm = jnp.sqrt(jnp.sum(stat_sum[:, 2]) + jnp.sum(vector_sum * vector_sum))
    clip = jnp.minimum(1.0, 1.0 / (grad_norm + 1e-06))
    sizes = jnp.sqrt(
        momentum_decay * momentum_decay * stat_sum[:, 0]
        + 2.0 * momentum_decay * clip * stat_sum[:, 1]
        + clip * clip * stat_sum[:, 2]
    )
    new_moments = [momentum_decay * moments[index] + clip * grads[index] for index in range(4)]
    starts = [
        (new_moments[index] / (sizes[index] + 1e-07)).astype(jnp.bfloat16) for index in range(4)
    ]
    blocks = [
        lax.all_gather(starts[0], "head", axis=1, tiled=True),
        lax.all_gather(starts[1], "head", axis=0, tiled=True),
        lax.all_gather(starts[2], everywhere, axis=1, tiled=True),
        lax.all_gather(starts[3], everywhere, axis=1, tiled=True),
    ]
    for turn in range(NS_STEPS):
        updated = []
        for index in range(4):
            form = gram_right if index == 1 else gram_left
            gram = form(blocks[index]).astype(jnp.bfloat16)
            mix = (
                ns_b * gram.astype(jnp.float32)
                + ns_c * jnp.dot(gram, gram, preferred_element_type=jnp.float32)
            ).astype(jnp.bfloat16)
            if index == 1:
                product = jnp.dot(blocks[index], mix, preferred_element_type=jnp.float32)
            else:
                product = jnp.dot(mix, blocks[index], preferred_element_type=jnp.float32)
            updated.append(
                (ns_a * blocks[index].astype(jnp.float32) + product).astype(jnp.bfloat16)
            )
        blocks = updated
    share = up_moment.shape[1]
    along = lax.axis_index("head")
    offset = (lax.axis_index("dp") * lax.axis_size("head") + along) * share
    owned = [
        lax.dynamic_slice_in_dim(blocks[0], along * qkv_moment.shape[1], qkv_moment.shape[1], 1),
        lax.dynamic_slice_in_dim(blocks[1], along * narrow, narrow, 0),
        lax.dynamic_slice_in_dim(blocks[2], offset, share, 1),
        lax.dynamic_slice_in_dim(blocks[3], offset, share, 1),
    ]
    return (owned, new_moments, vector_sum, grad_norm, clip)


def general_shards(
    tokens,
    segments,
    out_grad,
    norm_params,
    norm_first,
    norm_second,
    qkv_weight,
    qkv_moment,
    out_weight,
    out_moment,
    up_weight,
    up_moment,
    down_weight,
    down_moment,
):
    width = tokens.shape[1]
    rows = tokens.shape[0]
    narrow = out_weight.shape[0]
    sequences = rows // SEQ
    heads = width // HEAD_DIM
    everywhere = ("dp", "head")
    inputs = tokens.astype(jnp.float32)
    first, first_plain, first_factor = normalize(inputs, norm_params[0], norm_params[1])
    first_low = first.astype(jnp.bfloat16)
    qkv_full = lax.all_gather(qkv_weight.astype(jnp.bfloat16), "head", axis=1, tiled=True)
    out_full = lax.all_gather(out_weight.astype(jnp.bfloat16), "head", axis=0, tiled=True)
    up_all = lax.all_gather(up_weight.astype(jnp.bfloat16), everywhere, axis=1, tiled=True)
    down_all = lax.all_gather(down_weight.astype(jnp.bfloat16), everywhere, axis=1, tiled=True)
    mixed = jnp.dot(first_low, qkv_full, preferred_element_type=jnp.float32).astype(jnp.bfloat16)
    mixed = mixed.reshape(sequences, SEQ, heads, 3, HEAD_DIM)
    segment_rows = lax.dynamic_slice_in_dim(segments, lax.axis_index("head") * rows, rows, 0)
    segment_rows = segment_rows.reshape(sequences, SEQ)
    query = mixed[:, :, :, 0]
    keys = mixed[:, :, :, 1]
    values = mixed[:, :, :, 2]
    context, lse = lax.map(attend_forward, (query, keys, values, segment_rows))
    context = context.reshape(rows, width)
    attended = jnp.dot(context, out_full, preferred_element_type=jnp.float32)
    middle = inputs + attended
    second, second_plain, second_factor = normalize(middle, norm_params[2], norm_params[3])
    second_low = second.astype(jnp.bfloat16)
    hidden = jnp.dot(second_low, up_all, preferred_element_type=jnp.float32)
    switch = jax.nn.sigmoid(1.702 * hidden)
    active = (hidden * switch).astype(jnp.bfloat16)
    result = middle + lax.dot_general(
        active, down_all, (((1,), (1,)), ((), ())), preferred_element_type=jnp.float32
    )
    layer_out = result.astype(jnp.bfloat16)
    down_grad = lax.dot_general(
        out_grad, active, (((0,), (0,)), ((), ())), preferred_element_type=jnp.float32
    )
    active_grad = jnp.dot(out_grad, down_all, preferred_element_type=jnp.float32)
    hidden_grad = (active_grad * (switch + 1.702 * hidden * switch * (1.0 - switch))).astype(
        jnp.bfloat16
    )
    up_grad = lax.dot_general(
        second_low, hidden_grad, (((0,), (0,)), ((), ())), preferred_element_type=jnp.float32
    )
    second_grad = lax.dot_general(
        hidden_grad, up_all, (((1,), (1,)), ((), ())), preferred_element_type=jnp.float32
    )
    middle_lower, gain_two, shift_two = normalize_back(
        second_grad, second_plain, second_factor, norm_params[2]
    )
    middle_grad = out_grad.astype(jnp.float32) + middle_lower
    attended_low = middle_grad.astype(jnp.bfloat16)
    context_grad = lax.dot_general(
        attended_low, out_full, (((1,), (1,)), ((), ())), preferred_element_type=jnp.float32
    ).astype(jnp.bfloat16)
    whole_out = lax.dot_general(
        context, attended_low, (((0,), (0,)), ((), ())), preferred_element_type=jnp.float32
    )
    context_grad = context_grad.reshape(sequences, SEQ, heads, HEAD_DIM)
    mixed_grad = lax.map(attend_backward, (query, keys, values, segment_rows, context_grad, lse))
    mixed_grad = mixed_grad.reshape(rows, 3 * width)
    whole_qkv = lax.dot_general(
        first_low, mixed_grad, (((0,), (0,)), ((), ())), preferred_element_type=jnp.float32
    )
    first_grad = lax.dot_general(
        mixed_grad, qkv_full, (((1,), (1,)), ((), ())), preferred_element_type=jnp.float32
    )
    input_lower, gain_one, shift_one = normalize_back(
        first_grad, first_plain, first_factor, norm_params[0]
    )
    input_grad = middle_grad + input_lower
    vector_part = jnp.stack([gain_one, shift_one, gain_two, shift_two])
    (owned, new_moments, vector_sum, grad_norm, clip) = general_update(
        whole_qkv, whole_out, up_grad, down_grad, vector_part,
        qkv_moment, out_moment, up_moment, down_moment,
    )
    weights = [qkv_weight, out_weight, up_weight, down_weight]
    factors = [
        math.sqrt(3.0),
        math.sqrt(SEQ / 8.0),
        math.sqrt(max(1.0, FF / width)),
        math.sqrt(max(1.0, FF / width)),
    ]
    new_weights = [
        weights[index] * (1.0 - muon_rate * muon_decay)
        - muon_rate * factors[index] * owned[index].astype(jnp.float32)
        for index in range(4)
    ]
    clipped = clip * vector_sum
    first_new = beta_one * norm_first + (1.0 - beta_one) * clipped
    second_new = beta_two * norm_second + (1.0 - beta_two) * clipped * clipped
    return (
        layer_out,
        input_grad,
        grad_norm,
        clipped,
        first_new,
        second_new,
        new_weights[0],
        new_moments[0],
        new_weights[1],
        new_moments[1],
        new_weights[2],
        new_moments[2],
        new_weights[3],
        new_moments[3],
    )


def solution(mesh):
    placed = (
        P(("dp", "head"), None),
        P("dp"),
        P(("dp", "head"), None),
        P(),
        P(),
        P(),
        P(None, "head"),
        P(None, "head"),
        P("head", None),
        P("head", None),
        P(None, ("dp", "head")),
        P(None, ("dp", "head")),
        P(None, ("dp", "head")),
        P(None, ("dp", "head")),
    )
    fast = mesh.shape["dp"] == 8 and mesh.shape["head"] == 4
    return jax.shard_map(
        fast_shards if fast else general_shards,
        mesh=mesh,
        in_specs=placed,
        out_specs=(
            P(("dp", "head"), None),
            P(("dp", "head"), None),
            P(),
            P(),
            P(),
            P(),
            P(None, "head"),
            P(None, "head"),
            P("head", None),
            P("head", None),
            P(None, ("dp", "head")),
            P(None, ("dp", "head")),
            P(None, ("dp", "head")),
            P(None, ("dp", "head")),
        ),
        check_vma=False,
    )
```

```python
import math

import jax
import jax.numpy as jnp
from jax import lax
from jax.experimental import pallas as pl
from jax.experimental.pallas import tpu as pltpu
from jax.sharding import PartitionSpec as P

HEAD_DIM = 64
FF = 2048
SEQ = 512
NS_STEPS = 5


neg_fill = -1000000000.0
norm_eps = 1e-05
ns_a = 3.4445
ns_b = -4.775
ns_c = 2.0315
momentum_decay = 0.95
muon_rate = 0.5
muon_decay = 0.01
beta_one = 0.9
beta_two = 0.95


def normalize(values, gain, shift):
    mean = jnp.mean(values, axis=-1, keepdims=True)
    centered = values - mean
    factor = lax.rsqrt(jnp.mean(centered * centered, axis=-1, keepdims=True) + norm_eps)
    plain = centered * factor
    return (plain * gain + shift, plain, factor)


def normalize_back(upper, plain, factor, gain):
    inner = upper * gain
    lower = factor * (
        inner
        - jnp.mean(inner, axis=-1, keepdims=True)
        - plain * jnp.mean(inner * plain, axis=-1, keepdims=True)
    )
    return (lower, jnp.sum(upper * plain, axis=0), jnp.sum(upper, axis=0))


def masked_scores(query, keys, segment):
    scores = jnp.einsum(
        "qhd,khd->hqk", query, keys, preferred_element_type=jnp.float32
    ) * HEAD_DIM ** (-0.5)
    same = segment[:, None] == segment[None, :]
    return jnp.where(same[None], scores, neg_fill)


def attend_forward(block):
    query, keys, values, segment = block
    scores = masked_scores(query, keys, segment)
    top = jnp.max(scores, axis=-1, keepdims=True)
    weights = jnp.exp(scores - top)
    total = jnp.sum(weights, axis=-1, keepdims=True)
    probs = (weights / total).astype(jnp.bfloat16)
    context = jnp.einsum("hqk,khd->qhd", probs, values, preferred_element_type=jnp.float32)
    return (context.astype(jnp.bfloat16), top + jnp.log(total))


def attend_backward(block):
    query, keys, values, segment, context_grad, lse = block
    scores = masked_scores(query, keys, segment)
    probs = jnp.exp(scores - lse)
    probs_low = probs.astype(jnp.bfloat16)
    probs_grad = jnp.einsum(
        "qhd,khd->hqk", context_grad, values, preferred_element_type=jnp.float32
    )
    inner = jnp.sum(probs * probs_grad, axis=-1, keepdims=True)
    score_grad = (probs * (probs_grad - inner)).astype(jnp.bfloat16)
    query_grad = jnp.einsum(
        "hqk,khd->qhd", score_grad, keys, preferred_element_type=jnp.float32
    ) * HEAD_DIM ** (-0.5)
    key_grad = jnp.einsum(
        "hqk,qhd->khd", score_grad, query, preferred_element_type=jnp.float32
    ) * HEAD_DIM ** (-0.5)
    value_grad = jnp.einsum(
        "hqk,qhd->khd", probs_low, context_grad, preferred_element_type=jnp.float32
    )
    return jnp.stack([query_grad, key_grad, value_grad], axis=2).astype(jnp.bfloat16)


def gram_left(block):
    return lax.dot_general(
        block, block, (((1,), (1,)), ((), ())), preferred_element_type=jnp.float32
    )


def gram_right(block):
    return lax.dot_general(
        block, block, (((0,), (0,)), ((), ())), preferred_element_type=jnp.float32
    )


def squares_of(moment, grad, weight):
    return (
        jnp.stack([jnp.sum(moment * moment), jnp.sum(moment * grad), jnp.sum(grad * grad)]) * weight
    )


ROWS = 1024
TILE = 512
PAIRS = 4
WIDE = 2048
CHUNK = 512
VMEM_BYTES = 62 << 20
LOW = jnp.bfloat16
F32 = jnp.float32


def dot(one, two):
    return jnp.dot(one, two, preferred_element_type=F32)


def dot_back(one, two):
    return lax.dot_general(one, two, (((1,), (1,)), ((), ())), preferred_element_type=F32)


def dot_rows(one, two):
    return lax.dot_general(one, two, (((0,), (0,)), ((), ())), preferred_element_type=F32)


def each(count, body):
    def step(i, carry):
        body(i)
        return carry

    lax.fori_loop(0, count, step, 0)


def rows_at(i, size):
    return pl.ds(pl.multiple_of(i * size, size), size)


def first_phase(tokens, params, first):
    gain = params[0:1, :]
    shift = params[1:2, :]

    def body(i):
        here = rows_at(i, 128)
        plain_gain, _, _ = normalize(tokens[here, :].astype(F32), gain, shift)
        first[here, :] = plain_gain.astype(LOW)

    each(ROWS // 128, body)


def mixed_phase(pair, first, wqkv, mixed):
    def body(i):
        mixed[pair] = dot(first[...], wqkv[pair]).astype(LOW)

    body(0)


def bias_phase(segments, head, bias):
    turned = segments[...].astype(F32).T
    lane = lax.broadcasted_iota(jnp.int32, (1, segments.shape[0]), 1)

    for seq in range(ROWS // SEQ):
        which = head * (ROWS // SEQ) + seq
        row = segments[pl.ds(which, 1), :].astype(F32)
        column = jnp.sum(jnp.where(lane == which, turned, 0.0), axis=1, keepdims=True)
        bias[seq * SEQ : seq * SEQ + SEQ, :] = jnp.where(column == row, 0.0, neg_fill).astype(LOW)


def attend_phase(pair, mixed, bias, probs, context):
    lane = lax.broadcasted_iota(jnp.int32, (1, 128), 1)
    left = (lane < HEAD_DIM).astype(LOW)

    def body(seq):
        here = rows_at(seq, SEQ)
        query = mixed[pair, here, 0:128] * LOW(HEAD_DIM ** (-0.5))
        keys = mixed[pair, here, 128:256]
        values = mixed[pair, here, 256:384]
        allowed = bias[here, :].astype(F32)
        outs = []
        for half in range(2):
            mask = left if half == 0 else LOW(1.0) - left
            scores = dot_back(keys, query * mask) + allowed
            top = jnp.max(scores, axis=0, keepdims=True)
            weights = jnp.exp(scores - top)
            total = jnp.sum(weights, axis=0, keepdims=True)
            prob = (weights * (1.0 / total)).astype(LOW)
            probs[pair * 4 + half * 2 + seq] = prob
            outs.append(dot_rows(prob, values))
        context[here, pl.ds(pl.multiple_of(pair * 128, 128), 128)] = jnp.where(
            lane < HEAD_DIM, outs[0], outs[1]
        ).astype(LOW)

    each(ROWS // SEQ, body)


def second_phase(tokens, context, wout, params, middle, second):
    gain = params[2:3, :]
    shift = params[3:4, :]

    def body(i):
        here = rows_at(i, TILE)
        value = tokens[here, :].astype(F32) + dot(context[here, :], wout[...])
        middle[here, :] = value
        normal, _, _ = normalize(value, gain, shift)
        second[here, :] = normal.astype(LOW)

    each(ROWS // TILE, body)


def turn_phase(src, dst):
    def body(i):
        here = rows_at(i, 256)
        dst[:, here] = src[here, :].T

    each(ROWS // 256, body)


def feed_phase(
    chunk, second, second_t, out_grad, out_grad_t, up, down, active, hidden_grad,
    result, second_grad, g_up, g_down,
):
    units = rows_at(chunk, CHUNK)

    def body(i):
        here = rows_at(i, TILE)
        hidden = dot_back(second[here, :], up[units, :])
        switch = 0.5 * jnp.tanh(0.851 * hidden) + 0.5
        act = (hidden * switch).astype(LOW)
        active[here, :] = act
        grad = dot_back(out_grad[here, :], down[units, :])
        back = (grad * (switch + 1.702 * hidden * switch * (1.0 - switch))).astype(LOW)
        hidden_grad[here, :] = back
        result[here, :] += dot(act, down[units, :])
        second_grad[here, :] += dot(back, up[units, :])

    each(ROWS // TILE, body)

    for turned, wide, out in ((out_grad_t, active, g_down), (second_t, hidden_grad, g_up)):
        grad = dot(turned[...], wide[...]).astype(LOW)
        for j in range(CHUNK // 128):
            for c in range(2):
                out[chunk * 8 + j * 2 + c] = grad[c * 256 : c * 256 + 256, j * 128 : j * 128 + 128]


def middle_phase(
    params, middle, result, second_grad, out_grad, wout,
    layer_out, middle_grad, attended_low, context_grad, norms,
):
    gain = params[2:3, :]

    def body(i, sums):
        here = rows_at(i, TILE)
        value = middle[here, :]
        layer_out[here, :] = (value + result[here, :]).astype(LOW)
        _, plain, factor = normalize(value, gain, gain)
        upper = second_grad[here, :]
        lower, gains, shifts = normalize_back(upper, plain, factor, gain)
        total = out_grad[here, :].astype(F32) + lower
        middle_grad[here, :] = total
        low = total.astype(LOW)
        attended_low[here, :] = low
        context_grad[here, :] = dot_back(low, wout[...]).astype(LOW)
        return (sums[0] + gains[None], sums[1] + shifts[None])

    zero = jnp.zeros((1, 512), F32)
    sums = lax.fori_loop(0, ROWS // TILE, body, (zero, zero))
    norms[2:3, :] = sums[0]
    norms[3:4, :] = sums[1]


def out_phase(attended_t, context, g_attend):
    def body(i):
        here = rows_at(i, 512)
        grad = dot(attended_t[here, :], context[...]).astype(LOW)
        for p in range(PAIRS):
            g_attend[p, here, 384:512] = grad[:, p * 128 : p * 128 + 128]

    body(0)


def attend_back_phase(pair, seq, mixed, probs, context, context_grad):
    lane = lax.broadcasted_iota(jnp.int32, (1, 128), 1)
    left = (lane < HEAD_DIM).astype(LOW)
    scale = HEAD_DIM ** (-0.5)
    here = rows_at(seq, SEQ)
    query = mixed[pair, here, 0:128]
    keys = mixed[pair, here, 128:256]
    values = mixed[pair, here, 256:384]
    upper = context_grad[here, pl.ds(pl.multiple_of(pair * 128, 128), 128)]
    product = upper.astype(F32) * context[
        here, pl.ds(pl.multiple_of(pair * 128, 128), 128)
    ].astype(F32)
    product_high = product.astype(LOW)
    product_low = (product - product_high.astype(F32)).astype(LOW)
    marks = lax.broadcasted_iota(jnp.int32, (8, 128), 1) // HEAD_DIM
    marks = (marks == lax.broadcasted_iota(jnp.int32, (8, 128), 0)).astype(LOW)
    inners = dot_back(marks, product_high) + dot_back(marks, product_low)
    outs = []
    for half in range(2):
        mask = left if half == 0 else LOW(1.0) - left
        above = upper * mask
        prob_low = probs[pair * 4 + half * 2 + seq]
        prob = prob_low.astype(F32)
        prob_grad = dot_back(values, above)
        inner = inners[half : half + 1, :]
        score_grad = (prob * (prob_grad - inner)).astype(LOW)
        outs.append((dot_rows(score_grad, keys), dot(score_grad, query), dot(prob_low, above)))
    pick = lane < HEAD_DIM
    mixed[pair, here, 0:128] = (jnp.where(pick, outs[0][0], outs[1][0]) * scale).astype(LOW)
    mixed[pair, here, 128:256] = (jnp.where(pick, outs[0][1], outs[1][1]) * scale).astype(LOW)
    mixed[pair, here, 256:384] = (outs[0][2] + outs[1][2]).astype(LOW)


def qkv_phase(pair, mixed, first_t, g_attend):
    g_attend[pair, :, 0:384] = dot(first_t[...], mixed[pair]).astype(LOW)


def input_phase(params, tokens, mixed, wqkv, input_grad, norms):
    gain = params[0:1, :]

    def body(i, sums):
        here = rows_at(i, TILE)
        _, plain, factor = normalize(tokens[here, :].astype(F32), gain, gain)
        first_grad = dot_back(mixed[0, here, :], wqkv[0])
        for pair in range(1, PAIRS):
            first_grad = first_grad + dot_back(mixed[pair, here, :], wqkv[pair])
        lower, gains, shifts = normalize_back(first_grad, plain, factor, gain)
        input_grad[here, :] += lower
        return (sums[0] + gains[None], sums[1] + shifts[None])

    zero = jnp.zeros((1, 512), F32)
    sums = lax.fori_loop(0, ROWS // TILE, body, (zero, zero))
    norms[0:1, :] = sums[0]
    norms[1:2, :] = sums[1]


def local_call(kernel, outs, scratch, args, name):
    vmem = pl.BlockSpec(memory_space=pltpu.VMEM)
    return pl.pallas_call(
        kernel,
        out_shape=tuple(jax.ShapeDtypeStruct(*o) for o in outs),
        in_specs=[vmem] * len(args),
        out_specs=(vmem,) * len(outs),
        scratch_shapes=[pltpu.VMEM(*v) for v in scratch],
        compiler_params=pltpu.CompilerParams(vmem_limit_bytes=60 << 20),
        name=name,
    )(*args)


STEP_DIMS = {"c": 1, "x": 2, "y": 4, "l": 8, "g": 16}
GATHERS = (
    (0, 0, 256, ("g", "l", "y", "x")),
    (0, 256, 256, ("g", "x", "l", "y")),
    (1, 0, 128, ("g", "x", "l", "y")),
    (1, 128, 384, ("g", "y", "x", "l")),
)
STARTS = (("g", "l", "y", "x", "c"), ("g", "x", "l", "y", "c"), ("g", "y", "x", "l", "c"))
ATTEND_ORDER = ("c", "x", "y", "l", "g")


def coordinates():
    dp = lax.axis_index("dp")
    head = lax.axis_index("head")
    bits = {
        "c": head % 2,
        "x": head // 2,
        "y": dp % 2,
        "l": (dp // 2) % 2,
        "g": dp // 4,
    }
    steps = {"c": (0, 1), "x": (0, 2), "y": (1, 0), "l": (2, 0), "g": (4, 0)}
    peers = {}
    for name, (along_dp, along_head) in steps.items():
        turn = 1 - 2 * bits[name]
        peers[name] = (dp + along_dp * turn, head + along_head * turn)
    return dp, head, bits, peers


def remote(src, dst, send_sem, recv_sem, peer):
    return pltpu.make_async_remote_copy(
        src_ref=src,
        dst_ref=dst,
        send_sem=send_sem,
        recv_sem=recv_sem,
        device_id=peer,
        device_id_type=pl.DeviceIdType.MESH,
    )


def tile_of(fixed, free, place):
    total = 0
    for name, bit in fixed.items():
        total = total + STEP_DIMS[name] * bit
    for i, name in enumerate(free):
        total = total + STEP_DIMS[name] * ((place // 2**i) % 2)
    return total


def scatter_start(acc, got, base, fixed, name, free, bits, peer, sems, slot):
    for place in range(2 ** len(free)):
        away = tile_of({**fixed, name: 1 - bits[name]}, free, place)
        remote(
            acc.at[away], got.at[base + place], sems[0].at[slot], sems[1].at[slot], peer
        ).start()


def scatter_end(acc, got, base, fixed, name, free, bits, peer, sems, slot):
    count = 2 ** len(free)
    span = got.at[pl.ds(base, count)]
    remote(span, span, sems[0].at[slot], sems[1].at[slot], peer).wait()
    rows = acc.shape[1]

    def body(i):
        here = tile_of({**fixed, name: bits[name]}, free, i)
        acc[here] = (acc[here].astype(F32) + got[base + i].astype(F32)).astype(LOW)

    each(count, body)


def gather_start(ref, done, name, bits, peer, sems, slot):
    fixed = {d: bits[d] for d in STEP_DIMS if d not in done}
    for place in range(2 ** len(done)):
        part = ref.at[tile_of(fixed, done, place)]
        remote(part, part, sems[0].at[slot], sems[1].at[slot], peer).start()


def gather_end(ref, done, peer, sems, slot):
    span = ref.at[pl.ds(0, 2 ** len(done))]
    remote(span, span, sems[0].at[slot], sems[1].at[slot], peer).wait()


def paired(block):
    parts = [block[:, i * 64 : i * 64 + 64] for i in (0, 3, 1, 4, 2, 5)]
    return jnp.concatenate(parts, axis=1)


def unpaired(block):
    parts = [block[:, i * 64 : i * 64 + 64] for i in (0, 2, 4, 1, 3, 5)]
    return jnp.concatenate(parts, axis=1)


class Slots:
    def __init__(self):
        self.used = 0

    def __call__(self, count):
        start = self.used
        self.used += count
        return start


def update_step(pool, now, later, count, blocks, lanes, gram, mix):
    for low, high in ((0, 512), (256, 512)):
        rows = slice(low, low + 256)
        cols = slice(low, high)
        total = dot_back(pool[now, rows, :], pool[now, cols, :])
        for b in range(1, count):
            total = total + dot_back(pool[now + b, rows, :], pool[now + b, cols, :])
        made = total.astype(LOW)
        gram[rows, cols] = made
        if low == 0:
            gram[256:512, 0:256] = made[:, 256:512].T
    for low, high in ((0, 512), (256, 512)):
        rows = slice(low, low + 256)
        cols = slice(low, high)
        made = (
            ns_b * gram[rows, cols].astype(F32) + ns_c * dot(gram[rows, :], gram[:, cols])
        ).astype(LOW)
        mix[rows, cols] = made
        if low == 0:
            mix[256:512, 0:256] = made[:, 256:512].T

    def next_body(i):
        b = blocks[0] + i
        value = pool[now + b, :, lanes]
        pool[later + b, :, lanes] = (ns_a * value.astype(F32) + dot(mix[...], value)).astype(LOW)

    each(blocks[1], next_body)


def layer_kernel(
    tokens, segments, out_grad, params, w_qkv, m_qkv, w_out, m_out, w_up, m_up, w_down, m_down,
    layer_out, input_grad, start_a, start_u, start_d, ortho_q, ortho_o, ortho_u, ortho_d, norm_sum, scal,
    first, mixed, context, bias, wqkv, wout, wup, wdown, pool, middle, second, second_t, out_grad_t,
    active, hidden_grad, result, second_grad, acc_a, acc_u, acc_d, got_a, got_u, got_d,
    mom_full, mom_x, mom_u, mom_d, mom_a, norm_got, norm_far, stat_got, stat_far, gram, mix, send, recv,
):
    dp, head, bits, peers = coordinates()
    me = dp * 4 + head
    sibling = peers["c"]
    across = (dp, 3 - head)
    sems = (send, recv)
    slots = Slots()
    S_Q, S_O, S_M, S_MA = slots(4), slots(4), slots(2), slots(4)
    S_W, S_CORE, S_CHUNK, S_LG = slots(16), slots(20), slots(24), slots(16)
    S_A, S_NORM, S_STAT, S_START, S_SIDE, S_ORTHO = (
        slots(12), slots(2), slots(2), slots(15), slots(2), slots(8)
    )
    barrier = pltpu.get_barrier_semaphore()

    partners = (sibling, peers["x"], across)

    def along(i):
        return ((dp + 1 + i) % 8, head)

    def greet(peer):
        pl.semaphore_signal(barrier, inc=1, device_id=peer, device_id_type=pl.DeviceIdType.MESH)

    for peer in partners:
        greet(peer)
    each(7, lambda i: greet(along(i)))
    wqkv[head] = paired(w_qkv[...].astype(LOW))
    wout[pl.ds(pl.multiple_of(head * 128, 128), 128), :] = w_out[...].astype(LOW)
    mine = pl.ds(pl.multiple_of(me * 64, 64), 64)
    wup[mine, :] = w_up[...].astype(LOW)
    wdown[mine, :] = w_down[...].astype(LOW)
    pl.semaphore_wait(barrier, 10)

    def block_q(who):
        return wqkv.at[who]

    def block_o(who):
        return wout.at[pl.ds(pl.multiple_of(who * 128, 128), 128)]

    def weight_copy(block, who, slot, peer):
        return remote(block(who), block(who), send.at[slot], recv.at[slot], peer)

    def weight_tiles(i, k, far):
        matrix, start, count, order = GATHERS[i]
        done = order[: max(k, 0)]
        fixed = {d: bits[d] for d in STEP_DIMS if d not in done}
        if far and k >= 0:
            fixed[order[k]] = 1 - bits[order[k]]
        name = "c" if far else order[k]
        slot = S_CORE + i * 5 + k + 1 if far else S_W + i * 4 + k
        for place in range(2 ** len(done)):
            row = pl.multiple_of(tile_of(fixed, done, place) * 64, 64)
            part = (wup, wdown)[matrix].at[pl.ds(row, 64), pl.ds(start, count)]
            remote(part, part, send.at[slot], recv.at[slot], peers[name]).start()

    def weight_wait(i, k, far):
        matrix, start, count, _ = GATHERS[i]
        slot = S_CORE + i * 5 + k + 1 if far else S_W + i * 4 + k
        span = (wup, wdown)[matrix].at[pl.ds(0, 64 * 2 ** max(k, 0)), pl.ds(start, count)]
        remote(span, span, send.at[slot], recv.at[slot], sibling).wait()

    for i in range(len(GATHERS)):
        weight_tiles(i, 0, False)
    weight_copy(block_q, head, S_Q + 1, sibling).start()
    weight_copy(block_q, head, S_Q + 2, peers["x"]).start()
    other_half = pl.ds(pl.multiple_of((1 - bits["c"]) * 256, 256), 256)

    def moment_copy(i, ref):
        return remote(ref.at[:, other_half], mom_x.at[i], send.at[S_M + i], recv.at[S_M + i], sibling)

    moment_copy(0, m_up).start()
    moment_copy(1, m_down).start()

    parts = range(len(GATHERS))

    def weight_step(k):
        for i in parts:
            weight_wait(i, k, False)
            if k < 3:
                weight_tiles(i, k + 1, False)
        for i in parts:
            weight_tiles(i, k, True)

    weight_copy(block_o, head, S_O + 1, sibling).start()
    weight_copy(block_o, head, S_O + 2, peers["x"]).start()
    for i in parts:
        weight_tiles(i, -1, True)
    first_phase(tokens, params, first)
    bias_phase(segments, head, bias)
    mom_full[:, 0:384] = paired(m_qkv[...])
    mom_full[:, 384:512] = m_out[...].T

    def rank_of(c, x):
        return c * 16 + x * 8 + bits["y"] * 4 + bits["l"] * 2 + bits["g"]

    def rank_rows(who):
        return pl.ds(pl.multiple_of(rank_of(who % 2, who // 2) * 16, 16), 16)

    def rows_copy(j):
        who = partners[j][1]
        return remote(
            mom_full.at[rank_rows(who)], mom_a.at[head], send.at[S_MA + j], recv.at[S_MA + j], partners[j]
        )

    for j in range(3):
        rows_copy(j).start()
    mom_a[head] = mom_full[rank_rows(head), :]

    def pair_body(j):
        pair = (bits["c"] + j % 2) % 2 + 2 * ((bits["x"] + j // 2) % 2)
        mixed_phase(pair, first, wqkv, mixed)
        attend_phase(pair, mixed, bias, pool, context)

        @pl.when(j == 0)
        def _():
            weight_step(0)
            turn_phase(out_grad, out_grad_t)
            weight_copy(block_q, head, S_Q + 1, sibling).wait()
            weight_copy(block_o, head, S_O + 1, sibling).wait()

        @pl.when(j == 1)
        def _():
            weight_copy(block_q, head, S_Q + 2, peers["x"]).wait()
            weight_copy(block_q, peers["x"][1], S_Q + 3, sibling).start()
            weight_step(1)
            weight_copy(block_o, head, S_O + 2, peers["x"]).wait()
            weight_copy(block_o, peers["x"][1], S_O + 3, sibling).start()

        @pl.when(j == 2)
        def _():
            weight_copy(block_q, head, S_Q + 3, sibling).wait()
            weight_copy(block_o, head, S_O + 3, sibling).wait()

    each(PAIRS, pair_body)
    weight_step(2)
    second_phase(tokens, context, wout, params, middle, second)
    turn_phase(second, second_t)
    result[...] = jnp.zeros_like(result)
    second_grad[...] = jnp.zeros_like(second_grad)
    weight_step(3)
    for k in range(-1, 4):
        for i in parts:
            weight_wait(i, k, True)

    chunk_orders = ((acc_u, got_u, ("c", "x", "y")), (acc_d, got_d, ("c", "y", "x")))

    def chunk_args(q, k, order):
        fixed = {"g": q // 2, "l": q % 2}
        for name in order[:k]:
            fixed[name] = bits[name]
        return fixed, order[k], order[k + 1 :]

    def chunk_start(q, k):
        for i, (acc, got, order) in enumerate(chunk_orders):
            fixed, name, free = chunk_args(q, k, order)
            scatter_start(
                acc, got, q * 7 + (0, 4, 6)[k], fixed, name, free, bits, peers[name], sems,
                S_CHUNK + q * 6 + i * 3 + k,
            )

    def chunk_end(q, k):
        for i, (acc, got, order) in enumerate(chunk_orders):
            fixed, name, free = chunk_args(q, k, order)
            scatter_end(
                acc, got, q * 7 + (0, 4, 6)[k], fixed, name, free, bits, peers[name], sems,
                S_CHUNK + q * 6 + i * 3 + k,
            )

    def feed_body(q):
        feed_phase(
            q, second, second_t, out_grad, out_grad_t, wup, wdown, active, hidden_grad,
            result, second_grad, acc_u, acc_d,
        )
        chunk_start(q, 0)

        @pl.when(q >= 1)
        def _():
            chunk_end(q - 1, 0)
            chunk_start(q - 1, 1)

        @pl.when(q >= 3)
        def _():
            chunk_end(q - 3, 1)
            chunk_start(q - 3, 2)

    each(WIDE // CHUNK, feed_body)
    middle_phase(
        params, middle, result, second_grad, out_grad, wout,
        layer_out, input_grad, second, active, norm_got.at[head],
    )
    chunk_end(3, 0)
    chunk_start(3, 1)
    chunk_end(1, 1)
    chunk_start(1, 2)
    turn_phase(second, second_t)
    out_phase(second_t, context, acc_a)
    turn_phase(first, second_t)

    depth = dp // 2

    def owner_copy(i, acc, got, q):
        tile = tile_of({"g": q // 2, "l": q % 2, "c": bits["c"], "x": bits["x"], "y": bits["y"]}, (), 0)
        other = (2 * q + bits["y"], head)
        return remote(
            acc.at[tile], got.at[28 + (depth - q + 3) % 4], send.at[S_LG + 2 * q + i],
            recv.at[S_LG + 8 + 3 * i + (depth - q + 3) % 4], other,
        )

    def owner_start(q):
        @pl.when(depth != q)
        def _():
            for i, (acc, got, _) in enumerate(chunk_orders):
                owner_copy(i, acc, got, q).start()

    def owner_sent(q):
        @pl.when(depth != q)
        def _():
            for i, (acc, got, _) in enumerate(chunk_orders):
                owner_copy(i, acc, got, q).wait_send()

    def owner_end():
        for i, (acc, got, _) in enumerate(chunk_orders):
            for way in range(3):
                remote(
                    got.at[28 + way], got.at[28 + way], send.at[S_LG], recv.at[S_LG + 8 + 3 * i + way], sibling
                ).wait_recv()
            total = acc[me].astype(F32)
            for way in range(3):
                total = total + got[28 + way].astype(F32)
            acc[me] = total.astype(LOW)

    spans = []
    low_row = 0
    for k, name in enumerate(ATTEND_ORDER):
        size = 256 >> k
        spans.append((name, size, low_row + bits[name] * size, low_row + (1 - bits[name]) * size))
        low_row = low_row + bits[name] * size

    def aligned(row, size):
        return pl.ds(pl.multiple_of(row, 16), size)

    def attend_copy(pair, k):
        name, size, _, give = spans[k]
        return remote(
            acc_a.at[pair, aligned(give, size)], got_a.at[pair, pl.ds(512 - 2 * size, size)],
            send.at[S_A + pair * 3 + k], recv.at[S_A + pair * 3 + k], peers[name],
        )

    quarter = spans[1][2]

    def place_of(group):
        return (group % 2) * 4 + ((group // 2) % 2) * 2 + group // 4

    def attend_start(pair, k):
        if k < 2:
            attend_copy(pair, k).start()
            return

        def body(i):
            other = (dp + 1 + i) % 8
            remote(
                acc_a.at[pair, aligned(quarter + place_of(other) * 16, 16)],
                got_a.at[pair, aligned(384 + (6 - i) * 16, 16)],
                send.at[S_A + pair * 3 + 2], recv.at[S_A + pair * 3 + 2], (other, head),
            ).start()

        each(7, body)

    def attend_next(pair, k):
        if k == 2:
            span = got_a.at[pair, pl.ds(384, 112)]
            remote(span, span, send.at[S_A + pair * 3 + 2], recv.at[S_A + pair * 3 + 2], sibling).wait()
            here = aligned(low_row, 16)
            total = acc_a[pair, here, :].astype(F32)
            for i in range(1, 8):
                total = total + got_a[pair, 368 + i * 16 : 384 + i * 16, :].astype(F32)
            acc_a[pair, here, :] = total.astype(LOW)
            return
        attend_copy(pair, k).wait()
        _, size, keep, _ = spans[k]

        def body(i):
            here = aligned(keep + i * 64, 64)
            come = aligned(512 - 2 * size + i * 64, 64)
            acc_a[pair, here, :] = (
                acc_a[pair, here, :].astype(F32) + got_a[pair, come, :].astype(F32)
            ).astype(LOW)

        each(size // 64, body)
        attend_start(pair, k + 1)

    def at(wanted, pair):
        return pl.when(pair == wanted)

    def back_body(pair):
        attend_back_phase(pair, 0, mixed, pool, context, active)

        @at(0, pair)
        def _():
            chunk_end(0, 2)
            owner_start(0)
            chunk_end(2, 1)
            chunk_start(2, 2)

        @at(1, pair)
        def _():
            attend_next(0, 0)
            chunk_end(3, 1)
            chunk_start(3, 2)

        @at(2, pair)
        def _():
            attend_next(1, 0)
            attend_next(0, 1)

        @at(3, pair)
        def _():
            attend_next(2, 0)
            attend_next(1, 1)

        attend_back_phase(pair, 1, mixed, pool, context, active)
        qkv_phase(pair, mixed, second_t, acc_a)
        attend_start(pair, 0)

        @at(0, pair)
        def _():
            chunk_end(1, 2)
            owner_start(1)

        @at(1, pair)
        def _():
            chunk_end(2, 2)
            owner_start(2)

        @at(2, pair)
        def _():
            chunk_end(3, 2)
            owner_start(3)

    each(PAIRS, back_body)
    attend_next(3, 0)
    attend_next(2, 1)
    attend_next(0, 2)
    input_phase(params, tokens, mixed, wqkv, input_grad, norm_got.at[head])

    def tell(ref, slot):
        for peer in partners:
            remote(ref.at[head], ref.at[head], send.at[slot], recv.at[slot], peer).start()

    def tell_on(ref, far, slot):
        span = ref.at[pl.ds(0, 3)]
        remote(span, span, send.at[slot], recv.at[slot], sibling).wait()
        far[dp] = (ref[0] + ref[1]) + (ref[2] + ref[3])

        def body(i):
            remote(
                far.at[dp], far.at[dp], send.at[slot + 1], recv.at[slot + 1], along(i)
            ).start()

        each(7, body)

    def told_of(far, slot):
        span = far.at[pl.ds(0, 7)]
        remote(span, span, send.at[slot + 1], recv.at[slot + 1], sibling).wait()
        return jnp.sum(far[...], axis=0)

    tell(norm_got, S_NORM)
    attend_next(3, 1)
    attend_next(1, 2)
    tell_on(norm_got, norm_far, S_NORM)
    for q in range(4):
        owner_sent(q)
    owner_end()
    moment_copy(0, m_up).wait()
    moment_copy(1, m_down).wait()
    keep_half = pl.ds(pl.multiple_of(bits["c"] * 256, 256), 256)
    for i, (ref, out) in enumerate(((m_up, mom_u), (m_down, mom_d))):
        own = ref[:, keep_half]
        far = mom_x[i]
        low_half = jnp.where(bits["c"] == 0, own, far)
        high_half = jnp.where(bits["c"] == 0, far, own)
        out[...] = jnp.concatenate([low_half, high_half], axis=0).T
    for j in range(3):
        rows_copy(j).wait()

    def total_of(value):
        return jnp.sum(jnp.sum(value, axis=0, keepdims=True), axis=1, keepdims=True)

    lane = lax.broadcasted_iota(jnp.int32, (8, 128), 1)
    column = lax.broadcasted_iota(jnp.int32, (1, 512), 1)
    grad_u = acc_u[me].astype(F32)
    grad_d = acc_d[me].astype(F32)
    stats = jnp.zeros((8, 128), F32)
    for m, (moment, grad) in enumerate(((mom_u[...], grad_u), (mom_d[...], grad_d))):
        for i, product in enumerate((moment * moment, moment * grad, grad * grad)):
            stats = jnp.where(lane == 6 + 3 * m + i, total_of(product), stats)
    attend_next(2, 2)
    attend_next(3, 2)
    vector = told_of(norm_far, S_NORM)
    norm_sum[...] = vector
    vector_total = total_of(vector * vector)
    my_rows = aligned(low_row, 16)
    for i in range(3):
        inside = jnp.zeros((1, 512), F32)
        for pair in range(PAIRS):
            moment = mom_a[pair]
            grad = acc_a[pair, my_rows, :].astype(F32)
            product = (moment * moment, moment * grad, grad * grad)[i]
            inside = inside + jnp.sum(product, axis=0, keepdims=True)
        stats = jnp.where(lane == i, total_of(jnp.where(column < 384, inside, 0.0)), stats)
        stats = jnp.where(lane == 3 + i, total_of(jnp.where(column < 384, 0.0, inside)), stats)
    stat_got[head] = stats
    tell(stat_got, S_STAT)
    tell_on(stat_got, stat_far, S_STAT)
    stats = told_of(stat_far, S_STAT)

    def stat(i):
        return jnp.sum(jnp.where(lane == i, stats, 0.0), axis=1, keepdims=True)[0:1]

    norm = jnp.sqrt(stat(2) + stat(5) + stat(8) + stat(11) + vector_total)
    clip = jnp.minimum(1.0, 1.0 / (norm + 1e-06))
    sizes = []
    for m in range(4):
        square = (
            momentum_decay * momentum_decay * stat(3 * m)
            + 2.0 * momentum_decay * clip * stat(3 * m + 1)
            + clip * clip * stat(3 * m + 2)
        )
        sizes.append(jnp.sqrt(jnp.maximum(square, 0.0)) + 1e-07)
    told = jnp.where(lane == 0, norm, clip)
    for m in range(4):
        told = jnp.where(lane == 2 + m, sizes[m], told)
    scal[...] = told
    scale_a = jnp.where(column < 384, 1.0 / sizes[0], 1.0 / sizes[1])
    got_u[me] = ((momentum_decay * mom_u[...] + clip * grad_u) * (1.0 / sizes[2])).astype(LOW)
    got_d[me] = ((momentum_decay * mom_d[...] + clip * grad_d) * (1.0 / sizes[3])).astype(LOW)
    for pair in range(PAIRS):
        grad = acc_a[pair, my_rows, :].astype(F32)
        pool[pair, my_rows, :] = ((momentum_decay * mom_a[pair] + clip * grad) * scale_a).astype(LOW)

    mine_half = pl.ds(pl.multiple_of(bits["c"] * 256, 256), 256)

    def side_copy(i):
        src, dst = ((got_u, start_u), (got_d, start_d))[i]
        return remote(
            src.at[me], dst.at[mine_half], send.at[S_SIDE + i], recv.at[S_SIDE + i], sibling
        )

    side_copy(0).start()
    side_copy(1).start()
    start_u[mine_half, :] = got_u[me]
    start_d[mine_half, :] = got_d[me]

    def start_copy(k):
        name, size, keep, _ = spans[4 - k]
        part = pool.at[pl.ds(0, 4), aligned(keep, size)]
        return remote(part, part, send.at[S_START + 3 * k], recv.at[S_START + 3 * k], peers[name])

    tiles = ((got_u, STARTS[1]), (got_d, STARTS[2]))
    for k in range(5):
        if k > 0:
            start_copy(k - 1).wait()
        if k < 4:
            start_copy(k).start()
        for m, (got, order) in enumerate(tiles):
            if k > 0:
                gather_end(got, order[: k - 1], peers[order[k - 1]], sems, S_START + 3 * k - 2 + m)
            if k < 4:
                gather_start(
                    got, order[:k], order[k], bits, peers[order[k]], sems, S_START + 3 * k + 1 + m
                )
    half_rows = aligned(spans[0][2], 256)
    pair_part = pool.at[pl.ds(head + 1 - 2 * bits["c"], 1), half_rows]
    all_part = pool.at[pl.ds(0, 4), half_rows]

    def core_copy(part):
        return remote(part, part, send.at[S_START + 12], recv.at[S_START + 12], sibling)

    @pl.when(bits["c"] == 1)
    def _():
        core_copy(all_part).start()

        def slice_body(i):
            rows = rows_at(i, 256)
            start_a[rows, :] = pool[head, rows, :]

        for x, (got, order) in enumerate(tiles):
            @pl.when(bits["x"] == x)
            def _(got=got, order=order, x=x):
                span = got.at[pl.ds(0, 16)]
                remote(span, span, send.at[S_START + 13], recv.at[S_START + 13], sibling).wait_recv()

                def body(i):
                    for j in range(4):
                        for c in range(2):
                            pool[4 + i, c * 256 : c * 256 + 256, j * 128 : j * 128 + 128] = got[
                                i * 8 + j * 2 + c
                            ]

                each(4, body)

        core_copy(pair_part).wait_recv()
        core_copy(all_part).wait_send()
        each(2, slice_body)

    @pl.when(bits["c"] == 0)
    def _():
        for x, (got, order) in enumerate(tiles):
            @pl.when(bits["x"] == x)
            def _(got=got, order=order):
                gather_start(got, order[:4], "c", bits, sibling, sems, S_START + 13)

        core_copy(pair_part).start()
        core_copy(all_part).wait_recv()

        def body(i):
            rows = rows_at(i, 256)
            start_a[rows, :] = pool[head, rows, :]
            for p in range(PAIRS):
                for r in range(3):
                    group = p * 3 + r
                    pool[4 + group // 4, rows, (group % 4) * 128 : (group % 4) * 128 + 128] = pool[
                        p, rows, r * 128 : r * 128 + 128
                    ]
                pool[7, rows, p * 128 : p * 128 + 128] = pool[p, rows, 384:512]

        each(2, body)
        core_copy(pair_part).wait_send()
        span = got_u.at[pl.ds(0, 16)]
        remote(span, span, send.at[S_START + 13], recv.at[S_START + 13], sibling).wait_send()

    side_copy(0).wait()
    side_copy(1).wait()

    every = pl.ds(0, 512)
    outs = (ortho_u, ortho_d)

    def out_copy(src, dst, i, peer):
        return remote(src, dst, send.at[S_ORTHO + i], recv.at[S_ORTHO + i], peer)

    def group_of(r):
        group = bits["x"] * 6 + r
        return pool.at[8 + group // 4, :, pl.ds(pl.multiple_of((group % 4) * 128, 128), 128)]

    def out_of(who):
        return pool.at[11, :, pl.ds(pl.multiple_of(who * 128, 128), 128)]

    @pl.when(bits["c"] == 0)
    def _():
        def turn_body(turn):
            now = 4 + (turn % 2) * 4
            later = 12 - now
            update_step(pool, now, later, 3, (0, 3), every, gram, mix)
            update_step(pool, now + 3, later + 3, 1, (0, 1), every, gram, mix)

        each(NS_STEPS - 1, turn_body)
        update_step(pool, 4, 8, 3, (bits["x"], 2), every, gram, mix)
        for r in range(3):
            out_copy(group_of(3 + r), ortho_q.at[:, pl.ds(r * 128, 128)], 0, sibling).start()
        for r in range(3):
            ortho_q[:, r * 128 : r * 128 + 128] = group_of(r)[...]
        columns = pl.ds(pl.multiple_of(bits["x"] * 256, 256), 256)
        update_step(pool, 7, 11, 1, (0, 1), columns, gram, mix)
        out_copy(out_of(head + 1), ortho_o, 1, sibling).start()
        ortho_o[...] = out_of(head)[...]
        out_copy(ortho_q, ortho_q, 0, sibling).wait_send()
        out_copy(ortho_o, ortho_o, 1, sibling).wait_send()

    @pl.when(bits["c"] == 1)
    def _():
        def turn_body(turn):
            now = 4 + (turn % 2) * 4
            update_step(pool, now, 12 - now, 4, (0, 4), every, gram, mix)

        each(NS_STEPS - 1, turn_body)
        wanted = dp // 2
        update_step(pool, 4, 8, 4, (wanted, 1), every, gram, mix)

        def block_of(x):
            block = dp * 2 + x
            return pool.at[8 + wanted, :, pl.ds(pl.multiple_of((block % 4) * 128, 128), 128)]

        for x in range(2):
            @pl.when(bits["x"] == x)
            def _(x=x):
                targets = ((across, 1 - x), (peers["x"], 1 - x), (sibling, x))
                for j, (peer, side) in enumerate(targets):
                    remote(
                        block_of(side), outs[x], send.at[S_ORTHO + 2 + j], recv.at[S_ORTHO + 2 + x], peer
                    ).start()
                outs[x][...] = block_of(x)[...]
                for j, (peer, side) in enumerate(targets):
                    remote(
                        block_of(side), outs[x], send.at[S_ORTHO + 2 + j], recv.at[S_ORTHO + 2 + x], peer
                    ).wait_send()

        out_copy(ortho_q, ortho_q, 0, sibling).wait_recv()
        out_copy(ortho_o, ortho_o, 1, sibling).wait_recv()

    for x in range(2):
        @pl.when(head != 2 * x + 1)
        def _(x=x):
            out_copy(outs[x], outs[x], 2 + x, sibling).wait_recv()


def layer_call(*args):
    shape = jax.ShapeDtypeStruct
    vmem = pl.BlockSpec(memory_space=pltpu.VMEM)
    outs = (
        shape((ROWS, 512), LOW), shape((ROWS, 512), F32),
        shape((512, 512), LOW), shape((512, 128), LOW), shape((512, 128), LOW),
        shape((512, 384), LOW), shape((512, 128), LOW), shape((512, 128), LOW), shape((512, 128), LOW),
        shape((4, 512), F32), shape((8, 128), F32),
    )
    scratch = [
        ((ROWS, 512), LOW),
        ((PAIRS, ROWS, 384), LOW),
        ((ROWS, 512), LOW),
        ((ROWS, SEQ), LOW),
        ((PAIRS, 512, 384), LOW),
        ((512, 512), LOW),
        ((WIDE, 512), LOW),
        ((WIDE, 512), LOW),
        ((16, 512, 512), LOW),
        ((ROWS, 512), F32),
        ((ROWS, 512), LOW),
        ((512, ROWS), LOW),
        ((512, ROWS), LOW),
        ((ROWS, CHUNK), LOW),
        ((ROWS, CHUNK), LOW),
        ((ROWS, 512), F32),
        ((ROWS, 512), F32),
        ((PAIRS, 512, 512), LOW),
        ((32, 256, 128), LOW),
        ((32, 256, 128), LOW),
        ((PAIRS, 512, 512), LOW),
        ((32, 256, 128), LOW),
        ((32, 256, 128), LOW),
        ((512, 512), F32),
        ((2, 64, 256), F32),
        ((256, 128), F32),
        ((256, 128), F32),
        ((PAIRS, 16, 512), F32),
        ((4, 4, 512), F32),
        ((8, 4, 512), F32),
        ((4, 8, 128), F32),
        ((8, 8, 128), F32),
        ((512, 512), LOW),
        ((512, 512), LOW),
    ]
    return pl.pallas_call(
        layer_kernel,
        out_shape=outs,
        in_specs=[vmem] * len(args),
        out_specs=(vmem,) * len(outs),
        scratch_shapes=[pltpu.VMEM(*v) for v in scratch]
        + [pltpu.SemaphoreType.DMA((128,)), pltpu.SemaphoreType.DMA((128,))],
        compiler_params=pltpu.CompilerParams(
            collective_id=1, has_side_effects=True, vmem_limit_bytes=VMEM_BYTES
        ),
        name="layer",
    )(*args)


def update_kernel(
    start_a, start_u, start_d, ortho_q, ortho_o, ortho_u, ortho_d, norm_sum, scal,
    w_qkv, w_out, w_up, w_down, norm_first, norm_second,
    new_q, mom_q, new_o, mom_o, new_u, mom_u, new_d, mom_d, clipped, first_new, second_new, norm,
):
    core = lax.axis_index("head") % 2
    clip = scal[0:1, 1:2]
    keep = 1.0 - muon_rate * muon_decay

    def fresh(weight, factor, ortho):
        return weight * keep - muon_rate * factor * ortho

    new_q[...] = fresh(w_qkv[...], math.sqrt(3.0), unpaired(ortho_q[...].astype(F32)))
    mom_q[...] = unpaired(start_a[:, 0:384].astype(F32)) * scal[0:1, 2:3]
    new_o[...] = fresh(w_out[...], math.sqrt(SEQ / 8.0), ortho_o[...].astype(F32).T)
    mom_o[...] = start_a[:, 384:512].astype(F32).T * scal[0:1, 3:4]
    for weight, ortho, start, new, mom, i in (
        (w_up, ortho_u, start_u, new_u, mom_u, 4),
        (w_down, ortho_d, start_d, new_d, mom_d, 5),
    ):
        turned = ortho[...].astype(F32).T
        turned = jnp.where(core == 0, turned[0:64], turned[64:128])
        new[...] = fresh(weight[...], math.sqrt(max(1.0, FF / 512)), turned)
        turned = start[...].astype(F32).T
        mom[...] = jnp.where(core == 0, turned[0:64], turned[64:128]) * scal[0:1, i : i + 1]
    norm[...] = scal[0:1, 0:1]
    clip_grad = clip * norm_sum[...]
    clipped[...] = clip_grad
    first_new[...] = beta_one * norm_first[...] + (1.0 - beta_one) * clip_grad
    second_new[...] = beta_two * norm_second[...] + (1.0 - beta_two) * clip_grad * clip_grad


def fast_shards(
    tokens,
    segments,
    out_grad,
    norm_params,
    norm_first,
    norm_second,
    qkv_weight,
    qkv_moment,
    out_weight,
    out_moment,
    up_weight,
    up_moment,
    down_weight,
    down_moment,
):
    (
        layer_out, input_grad, start_a, start_u, start_d, ortho_q, ortho_o, ortho_u, ortho_d, norm_sum, scal
    ) = layer_call(
        tokens, segments.reshape(segments.shape[0] // SEQ, SEQ), out_grad, norm_params,
        qkv_weight, qkv_moment, out_weight, out_moment,
        up_weight.T, up_moment.T, down_weight.T, down_moment.T,
    )
    tall = ((64, 512), F32)
    new_q, mom_q, new_o, mom_o, new_u, mom_u, new_d, mom_d, clipped, first_new, second_new, norm = local_call(
        update_kernel,
        [((512, 384), F32)] * 2 + [((128, 512), F32)] * 2 + [tall] * 4 + [((4, 512), F32)] * 3 + [((1, 1), F32)],
        [],
        (
            start_a, start_u, start_d, ortho_q, ortho_o, ortho_u, ortho_d, norm_sum, scal,
            qkv_weight, out_weight, up_weight.T, down_weight.T, norm_first, norm_second,
        ),
        "update",
    )
    return (
        layer_out, input_grad, norm.reshape(()), clipped, first_new, second_new,
        new_q, mom_q, new_o, mom_o, new_u.T, mom_u.T, new_d.T, mom_d.T,
    )


def general_update(
    whole_qkv, whole_out, up_grad, down_grad, vector_part,
    qkv_moment, out_moment, up_moment, down_moment,
):
    everywhere = ("dp", "head")
    narrow = out_moment.shape[0]
    up_part, down_part = (
        lax.psum_scatter(
            up_grad.astype(jnp.bfloat16), everywhere, scatter_dimension=1, tiled=True
        ).astype(jnp.float32),
        lax.psum_scatter(
            down_grad.astype(jnp.bfloat16), everywhere, scatter_dimension=1, tiled=True
        ).astype(jnp.float32),
    )
    qkv_part = lax.psum_scatter(
        whole_qkv.astype(jnp.bfloat16), "head", scatter_dimension=1, tiled=True
    )
    out_part = lax.psum_scatter(
        whole_out.astype(jnp.bfloat16), "head", scatter_dimension=0, tiled=True
    )
    qkv_sum, out_sum = (
        lax.psum(qkv_part, "dp").astype(jnp.float32),
        lax.psum(out_part, "dp").astype(jnp.float32),
    )
    leading = (lax.axis_index("dp") == 0).astype(jnp.float32)
    moments = [qkv_moment, out_moment, up_moment, down_moment]
    grads = [qkv_sum, out_sum, up_part, down_part]
    stats = jnp.stack(
        [
            squares_of(qkv_moment, qkv_sum, leading),
            squares_of(out_moment, out_sum, leading),
            squares_of(up_moment, up_part, 1.0),
            squares_of(down_moment, down_part, 1.0),
        ]
    )
    vector_sum, stat_sum = lax.psum((vector_part, stats), everywhere)
    grad_norm = jnp.sqrt(jnp.sum(stat_sum[:, 2]) + jnp.sum(vector_sum * vector_sum))
    clip = jnp.minimum(1.0, 1.0 / (grad_norm + 1e-06))
    sizes = jnp.sqrt(
        momentum_decay * momentum_decay * stat_sum[:, 0]
        + 2.0 * momentum_decay * clip * stat_sum[:, 1]
        + clip * clip * stat_sum[:, 2]
    )
    new_moments = [momentum_decay * moments[index] + clip * grads[index] for index in range(4)]
    starts = [
        (new_moments[index] / (sizes[index] + 1e-07)).astype(jnp.bfloat16) for index in range(4)
    ]
    blocks = [
        lax.all_gather(starts[0], "head", axis=1, tiled=True),
        lax.all_gather(starts[1], "head", axis=0, tiled=True),
        lax.all_gather(starts[2], everywhere, axis=1, tiled=True),
        lax.all_gather(starts[3], everywhere, axis=1, tiled=True),
    ]
    for turn in range(NS_STEPS):
        updated = []
        for index in range(4):
            form = gram_right if index == 1 else gram_left
            gram = form(blocks[index]).astype(jnp.bfloat16)
            mix = (
                ns_b * gram.astype(jnp.float32)
                + ns_c * jnp.dot(gram, gram, preferred_element_type=jnp.float32)
            ).astype(jnp.bfloat16)
            if index == 1:
                product = jnp.dot(blocks[index], mix, preferred_element_type=jnp.float32)
            else:
                product = jnp.dot(mix, blocks[index], preferred_element_type=jnp.float32)
            updated.append(
                (ns_a * blocks[index].astype(jnp.float32) + product).astype(jnp.bfloat16)
            )
        blocks = updated
    share = up_moment.shape[1]
    along = lax.axis_index("head")
    offset = (lax.axis_index("dp") * lax.axis_size("head") + along) * share
    owned = [
        lax.dynamic_slice_in_dim(blocks[0], along * qkv_moment.shape[1], qkv_moment.shape[1], 1),
        lax.dynamic_slice_in_dim(blocks[1], along * narrow, narrow, 0),
        lax.dynamic_slice_in_dim(blocks[2], offset, share, 1),
        lax.dynamic_slice_in_dim(blocks[3], offset, share, 1),
    ]
    return (owned, new_moments, vector_sum, grad_norm, clip)


def general_shards(
    tokens,
    segments,
    out_grad,
    norm_params,
    norm_first,
    norm_second,
    qkv_weight,
    qkv_moment,
    out_weight,
    out_moment,
    up_weight,
    up_moment,
    down_weight,
    down_moment,
):
    width = tokens.shape[1]
    rows = tokens.shape[0]
    narrow = out_weight.shape[0]
    sequences = rows // SEQ
    heads = width // HEAD_DIM
    everywhere = ("dp", "head")
    inputs = tokens.astype(jnp.float32)
    first, first_plain, first_factor = normalize(inputs, norm_params[0], norm_params[1])
    first_low = first.astype(jnp.bfloat16)
    qkv_full = lax.all_gather(qkv_weight.astype(jnp.bfloat16), "head", axis=1, tiled=True)
    out_full = lax.all_gather(out_weight.astype(jnp.bfloat16), "head", axis=0, tiled=True)
    up_all = lax.all_gather(up_weight.astype(jnp.bfloat16), everywhere, axis=1, tiled=True)
    down_all = lax.all_gather(down_weight.astype(jnp.bfloat16), everywhere, axis=1, tiled=True)
    mixed = jnp.dot(first_low, qkv_full, preferred_element_type=jnp.float32).astype(jnp.bfloat16)
    mixed = mixed.reshape(sequences, SEQ, heads, 3, HEAD_DIM)
    segment_rows = lax.dynamic_slice_in_dim(segments, lax.axis_index("head") * rows, rows, 0)
    segment_rows = segment_rows.reshape(sequences, SEQ)
    query = mixed[:, :, :, 0]
    keys = mixed[:, :, :, 1]
    values = mixed[:, :, :, 2]
    context, lse = lax.map(attend_forward, (query, keys, values, segment_rows))
    context = context.reshape(rows, width)
    attended = jnp.dot(context, out_full, preferred_element_type=jnp.float32)
    middle = inputs + attended
    second, second_plain, second_factor = normalize(middle, norm_params[2], norm_params[3])
    second_low = second.astype(jnp.bfloat16)
    hidden = jnp.dot(second_low, up_all, preferred_element_type=jnp.float32)
    switch = jax.nn.sigmoid(1.702 * hidden)
    active = (hidden * switch).astype(jnp.bfloat16)
    result = middle + lax.dot_general(
        active, down_all, (((1,), (1,)), ((), ())), preferred_element_type=jnp.float32
    )
    layer_out = result.astype(jnp.bfloat16)
    down_grad = lax.dot_general(
        out_grad, active, (((0,), (0,)), ((), ())), preferred_element_type=jnp.float32
    )
    active_grad = jnp.dot(out_grad, down_all, preferred_element_type=jnp.float32)
    hidden_grad = (active_grad * (switch + 1.702 * hidden * switch * (1.0 - switch))).astype(
        jnp.bfloat16
    )
    up_grad = lax.dot_general(
        second_low, hidden_grad, (((0,), (0,)), ((), ())), preferred_element_type=jnp.float32
    )
    second_grad = lax.dot_general(
        hidden_grad, up_all, (((1,), (1,)), ((), ())), preferred_element_type=jnp.float32
    )
    middle_lower, gain_two, shift_two = normalize_back(
        second_grad, second_plain, second_factor, norm_params[2]
    )
    middle_grad = out_grad.astype(jnp.float32) + middle_lower
    attended_low = middle_grad.astype(jnp.bfloat16)
    context_grad = lax.dot_general(
        attended_low, out_full, (((1,), (1,)), ((), ())), preferred_element_type=jnp.float32
    ).astype(jnp.bfloat16)
    whole_out = lax.dot_general(
        context, attended_low, (((0,), (0,)), ((), ())), preferred_element_type=jnp.float32
    )
    context_grad = context_grad.reshape(sequences, SEQ, heads, HEAD_DIM)
    mixed_grad = lax.map(attend_backward, (query, keys, values, segment_rows, context_grad, lse))
    mixed_grad = mixed_grad.reshape(rows, 3 * width)
    whole_qkv = lax.dot_general(
        first_low, mixed_grad, (((0,), (0,)), ((), ())), preferred_element_type=jnp.float32
    )
    first_grad = lax.dot_general(
        mixed_grad, qkv_full, (((1,), (1,)), ((), ())), preferred_element_type=jnp.float32
    )
    input_lower, gain_one, shift_one = normalize_back(
        first_grad, first_plain, first_factor, norm_params[0]
    )
    input_grad = middle_grad + input_lower
    vector_part = jnp.stack([gain_one, shift_one, gain_two, shift_two])
    (owned, new_moments, vector_sum, grad_norm, clip) = general_update(
        whole_qkv, whole_out, up_grad, down_grad, vector_part,
        qkv_moment, out_moment, up_moment, down_moment,
    )
    weights = [qkv_weight, out_weight, up_weight, down_weight]
    factors = [
        math.sqrt(3.0),
        math.sqrt(SEQ / 8.0),
        math.sqrt(max(1.0, FF / width)),
        math.sqrt(max(1.0, FF / width)),
    ]
    new_weights = [
        weights[index] * (1.0 - muon_rate * muon_decay)
        - muon_rate * factors[index] * owned[index].astype(jnp.float32)
        for index in range(4)
    ]
    clipped = clip * vector_sum
    first_new = beta_one * norm_first + (1.0 - beta_one) * clipped
    second_new = beta_two * norm_second + (1.0 - beta_two) * clipped * clipped
    return (
        layer_out,
        input_grad,
        grad_norm,
        clipped,
        first_new,
        second_new,
        new_weights[0],
        new_moments[0],
        new_weights[1],
        new_moments[1],
        new_weights[2],
        new_moments[2],
        new_weights[3],
        new_moments[3],
    )


def solution(mesh):
    placed = (
        P(("dp", "head"), None),
        P("dp"),
        P(("dp", "head"), None),
        P(),
        P(),
        P(),
        P(None, "head"),
        P(None, "head"),
        P("head", None),
        P("head", None),
        P(None, ("dp", "head")),
        P(None, ("dp", "head")),
        P(None, ("dp", "head")),
        P(None, ("dp", "head")),
    )
    fast = mesh.shape["dp"] == 8 and mesh.shape["head"] == 4
    return jax.shard_map(
        fast_shards if fast else general_shards,
        mesh=mesh,
        in_specs=placed,
        out_specs=(
            P(("dp", "head"), None),
            P(("dp", "head"), None),
            P(),
            P(),
            P(),
            P(),
            P(None, "head"),
            P(None, "head"),
            P("head", None),
            P("head", None),
            P(None, ("dp", "head")),
            P(None, ("dp", "head")),
            P(None, ("dp", "head")),
            P(None, ("dp", "head")),
        ),
        check_vma=False,
    )
```

```python
import math

import jax
import jax.numpy as jnp
from jax import lax
from jax.experimental import pallas as pl
from jax.experimental.pallas import tpu as pltpu
from jax.sharding import PartitionSpec as P

HEAD_DIM = 64
FF = 2048
SEQ = 512
NS_STEPS = 5


neg_fill = -1000000000.0
norm_eps = 1e-05
ns_a = 3.4445
ns_b = -4.775
ns_c = 2.0315
momentum_decay = 0.95
muon_rate = 0.5
muon_decay = 0.01
beta_one = 0.9
beta_two = 0.95


def normalize(values, gain, shift):
    mean = jnp.mean(values, axis=-1, keepdims=True)
    centered = values - mean
    factor = lax.rsqrt(jnp.mean(centered * centered, axis=-1, keepdims=True) + norm_eps)
    plain = centered * factor
    return (plain * gain + shift, plain, factor)


def normalize_back(upper, plain, factor, gain):
    inner = upper * gain
    lower = factor * (
        inner
        - jnp.mean(inner, axis=-1, keepdims=True)
        - plain * jnp.mean(inner * plain, axis=-1, keepdims=True)
    )
    return (lower, jnp.sum(upper * plain, axis=0), jnp.sum(upper, axis=0))


def masked_scores(query, keys, segment):
    scores = jnp.einsum(
        "qhd,khd->hqk", query, keys, preferred_element_type=jnp.float32
    ) * HEAD_DIM ** (-0.5)
    same = segment[:, None] == segment[None, :]
    return jnp.where(same[None], scores, neg_fill)


def attend_forward(block):
    query, keys, values, segment = block
    scores = masked_scores(query, keys, segment)
    top = jnp.max(scores, axis=-1, keepdims=True)
    weights = jnp.exp(scores - top)
    total = jnp.sum(weights, axis=-1, keepdims=True)
    probs = (weights / total).astype(jnp.bfloat16)
    context = jnp.einsum("hqk,khd->qhd", probs, values, preferred_element_type=jnp.float32)
    return (context.astype(jnp.bfloat16), top + jnp.log(total))


def attend_backward(block):
    query, keys, values, segment, context_grad, lse = block
    scores = masked_scores(query, keys, segment)
    probs = jnp.exp(scores - lse)
    probs_low = probs.astype(jnp.bfloat16)
    probs_grad = jnp.einsum(
        "qhd,khd->hqk", context_grad, values, preferred_element_type=jnp.float32
    )
    inner = jnp.sum(probs * probs_grad, axis=-1, keepdims=True)
    score_grad = (probs * (probs_grad - inner)).astype(jnp.bfloat16)
    query_grad = jnp.einsum(
        "hqk,khd->qhd", score_grad, keys, preferred_element_type=jnp.float32
    ) * HEAD_DIM ** (-0.5)
    key_grad = jnp.einsum(
        "hqk,qhd->khd", score_grad, query, preferred_element_type=jnp.float32
    ) * HEAD_DIM ** (-0.5)
    value_grad = jnp.einsum(
        "hqk,qhd->khd", probs_low, context_grad, preferred_element_type=jnp.float32
    )
    return jnp.stack([query_grad, key_grad, value_grad], axis=2).astype(jnp.bfloat16)


def gram_left(block):
    return lax.dot_general(
        block, block, (((1,), (1,)), ((), ())), preferred_element_type=jnp.float32
    )


def gram_right(block):
    return lax.dot_general(
        block, block, (((0,), (0,)), ((), ())), preferred_element_type=jnp.float32
    )


def squares_of(moment, grad, weight):
    return (
        jnp.stack([jnp.sum(moment * moment), jnp.sum(moment * grad), jnp.sum(grad * grad)]) * weight
    )


ROWS = 1024
TILE = 512
PAIRS = 4
WIDE = 2048
CHUNK = 512
VMEM_BYTES = 62 << 20
LOW = jnp.bfloat16
F32 = jnp.float32


def dot(one, two):
    return jnp.dot(one, two, preferred_element_type=F32)


def dot_back(one, two):
    return lax.dot_general(one, two, (((1,), (1,)), ((), ())), preferred_element_type=F32)


def dot_rows(one, two):
    return lax.dot_general(one, two, (((0,), (0,)), ((), ())), preferred_element_type=F32)


def each(count, body):
    def step(i, carry):
        body(i)
        return carry

    lax.fori_loop(0, count, step, 0)


def rows_at(i, size):
    return pl.ds(pl.multiple_of(i * size, size), size)


def first_phase(tokens, params, first):
    gain = params[0:1, :]
    shift = params[1:2, :]

    def body(i):
        here = rows_at(i, 128)
        plain_gain, _, _ = normalize(tokens[here, :].astype(F32), gain, shift)
        first[here, :] = plain_gain.astype(LOW)

    each(ROWS // 128, body)


def mixed_phase(pair, first, wqkv, mixed):
    def body(i):
        mixed[pair] = dot(first[...], wqkv[pair]).astype(LOW)

    body(0)


def bias_phase(segments, head, bias):
    for seq in range(ROWS // SEQ):
        start = (head * (ROWS // SEQ) + seq) * (SEQ // 128)
        row = jnp.concatenate(
            [segments[pl.ds(start + i, 1), :] for i in range(SEQ // 128)], axis=1
        ).astype(F32)
        column = jnp.broadcast_to(row, (8, SEQ)).T[:, 0:1]
        bias[seq * SEQ : seq * SEQ + SEQ, :] = jnp.where(column == row, 0.0, neg_fill).astype(LOW)


def attend_phase(pair, mixed, bias, probs, context):
    lane = lax.broadcasted_iota(jnp.int32, (1, 128), 1)
    left = (lane < HEAD_DIM).astype(LOW)

    def body(seq):
        here = rows_at(seq, SEQ)
        query = mixed[pair, here, 0:128] * LOW(HEAD_DIM ** (-0.5))
        keys = mixed[pair, here, 128:256]
        values = mixed[pair, here, 256:384]
        allowed = bias[here, :].astype(F32)
        outs = []
        for half in range(2):
            mask = left if half == 0 else LOW(1.0) - left
            scores = dot_back(keys, query * mask) + allowed
            top = jnp.max(scores, axis=0, keepdims=True)
            weights = jnp.exp(scores - top)
            total = jnp.sum(weights, axis=0, keepdims=True)
            prob = (weights * (1.0 / total)).astype(LOW)
            probs[pair * 4 + half * 2 + seq] = prob
            outs.append(dot_rows(prob, values))
        context[here, pl.ds(pl.multiple_of(pair * 128, 128), 128)] = jnp.where(
            lane < HEAD_DIM, outs[0], outs[1]
        ).astype(LOW)

    each(ROWS // SEQ, body)


def second_phase(tokens, context, wout, params, middle, second):
    gain = params[2:3, :]
    shift = params[3:4, :]

    def body(i):
        here = rows_at(i, TILE)
        value = tokens[here, :].astype(F32) + dot(context[here, :], wout[...])
        middle[here, :] = value
        normal, _, _ = normalize(value, gain, shift)
        second[here, :] = normal.astype(LOW)

    each(ROWS // TILE, body)


def turn_phase(src, dst):
    def body(i):
        here = rows_at(i, 256)
        dst[:, here] = src[here, :].T

    each(ROWS // 256, body)


def feed_phase(
    chunk, second, second_t, out_grad, out_grad_t, up, down, active, hidden_grad,
    result, second_grad, g_up, g_down,
):
    units = rows_at(chunk, CHUNK)

    def body(i):
        here = rows_at(i, TILE)
        hidden = dot_back(second[here, :], up[units, :])
        switch = 0.5 * jnp.tanh(0.851 * hidden) + 0.5
        act = (hidden * switch).astype(LOW)
        active[here, :] = act
        grad = dot_back(out_grad[here, :], down[units, :])
        back = (grad * (switch + 1.702 * hidden * switch * (1.0 - switch))).astype(LOW)
        hidden_grad[here, :] = back
        result[here, :] += dot(act, down[units, :])
        second_grad[here, :] += dot(back, up[units, :])

    each(ROWS // TILE, body)

    for turned, wide, out in ((out_grad_t, active, g_down), (second_t, hidden_grad, g_up)):
        grad = dot(turned[...], wide[...]).astype(LOW)
        for j in range(CHUNK // 128):
            for c in range(2):
                out[chunk * 8 + j * 2 + c] = grad[c * 256 : c * 256 + 256, j * 128 : j * 128 + 128]


def middle_phase(
    params, middle, result, second_grad, out_grad, wout,
    layer_out, middle_grad, attended_low, context_grad, norms,
):
    gain = params[2:3, :]

    def body(i, sums):
        here = rows_at(i, TILE)
        value = middle[here, :]
        layer_out[here, :] = (value + result[here, :]).astype(LOW)
        _, plain, factor = normalize(value, gain, gain)
        upper = second_grad[here, :]
        lower, gains, shifts = normalize_back(upper, plain, factor, gain)
        total = out_grad[here, :].astype(F32) + lower
        middle_grad[here, :] = total
        low = total.astype(LOW)
        attended_low[here, :] = low
        context_grad[here, :] = dot_back(low, wout[...]).astype(LOW)
        return (sums[0] + gains[None], sums[1] + shifts[None])

    zero = jnp.zeros((1, 512), F32)
    sums = lax.fori_loop(0, ROWS // TILE, body, (zero, zero))
    norms[2:3, :] = sums[0]
    norms[3:4, :] = sums[1]


def out_phase(attended_t, context, g_attend):
    def body(i):
        here = rows_at(i, 512)
        grad = dot(attended_t[here, :], context[...]).astype(LOW)
        for p in range(PAIRS):
            g_attend[p, here, 384:512] = grad[:, p * 128 : p * 128 + 128]

    body(0)


def attend_back_phase(pair, seq, mixed, probs, context, context_grad):
    lane = lax.broadcasted_iota(jnp.int32, (1, 128), 1)
    left = (lane < HEAD_DIM).astype(LOW)
    scale = HEAD_DIM ** (-0.5)
    here = rows_at(seq, SEQ)
    query = mixed[pair, here, 0:128]
    keys = mixed[pair, here, 128:256]
    values = mixed[pair, here, 256:384]
    upper = context_grad[here, pl.ds(pl.multiple_of(pair * 128, 128), 128)]
    product = upper.astype(F32) * context[
        here, pl.ds(pl.multiple_of(pair * 128, 128), 128)
    ].astype(F32)
    product_high = product.astype(LOW)
    product_low = (product - product_high.astype(F32)).astype(LOW)
    marks = lax.broadcasted_iota(jnp.int32, (8, 128), 1) // HEAD_DIM
    marks = (marks == lax.broadcasted_iota(jnp.int32, (8, 128), 0)).astype(LOW)
    inners = dot_back(marks, product_high) + dot_back(marks, product_low)
    outs = []
    for half in range(2):
        mask = left if half == 0 else LOW(1.0) - left
        above = upper * mask
        prob_low = probs[pair * 4 + half * 2 + seq]
        prob = prob_low.astype(F32)
        prob_grad = dot_back(values, above)
        inner = inners[half : half + 1, :]
        score_grad = (prob * (prob_grad - inner)).astype(LOW)
        outs.append((dot_rows(score_grad, keys), dot(score_grad, query), dot(prob_low, above)))
    pick = lane < HEAD_DIM
    mixed[pair, here, 0:128] = (jnp.where(pick, outs[0][0], outs[1][0]) * scale).astype(LOW)
    mixed[pair, here, 128:256] = (jnp.where(pick, outs[0][1], outs[1][1]) * scale).astype(LOW)
    mixed[pair, here, 256:384] = (outs[0][2] + outs[1][2]).astype(LOW)


def qkv_phase(pair, mixed, first_t, g_attend):
    g_attend[pair, :, 0:384] = dot(first_t[...], mixed[pair]).astype(LOW)


def input_phase(params, tokens, mixed, wqkv, input_grad, norms):
    gain = params[0:1, :]

    def body(i, sums):
        here = rows_at(i, TILE)
        _, plain, factor = normalize(tokens[here, :].astype(F32), gain, gain)
        first_grad = dot_back(mixed[0, here, :], wqkv[0])
        for pair in range(1, PAIRS):
            first_grad = first_grad + dot_back(mixed[pair, here, :], wqkv[pair])
        lower, gains, shifts = normalize_back(first_grad, plain, factor, gain)
        input_grad[here, :] += lower
        return (sums[0] + gains[None], sums[1] + shifts[None])

    zero = jnp.zeros((1, 512), F32)
    sums = lax.fori_loop(0, ROWS // TILE, body, (zero, zero))
    norms[0:1, :] = sums[0]
    norms[1:2, :] = sums[1]


def local_call(kernel, outs, scratch, args, name):
    vmem = pl.BlockSpec(memory_space=pltpu.VMEM)
    return pl.pallas_call(
        kernel,
        out_shape=tuple(jax.ShapeDtypeStruct(*o) for o in outs),
        in_specs=[vmem] * len(args),
        out_specs=(vmem,) * len(outs),
        scratch_shapes=[pltpu.VMEM(*v) for v in scratch],
        compiler_params=pltpu.CompilerParams(vmem_limit_bytes=60 << 20),
        name=name,
    )(*args)


STEP_DIMS = {"c": 1, "x": 2, "y": 4, "l": 8, "g": 16}
GATHERS = ((0, 0, 512, ("g", "l", "y", "x")), (1, 0, 512, ("g", "l", "x", "y")))
STARTS = (("g", "l", "y", "x", "c"), ("x", "g", "l", "y", "c"), ("g", "y", "x", "l", "c"))
ATTEND_ORDER = ("c", "x", "y", "l", "g")


def coordinates():
    dp = lax.axis_index("dp")
    head = lax.axis_index("head")
    bits = {
        "c": head % 2,
        "x": head // 2,
        "y": dp % 2,
        "l": (dp // 2) % 2,
        "g": dp // 4,
    }
    steps = {"c": (0, 1), "x": (0, 2), "y": (1, 0), "l": (2, 0), "g": (4, 0)}
    peers = {}
    for name, (along_dp, along_head) in steps.items():
        turn = 1 - 2 * bits[name]
        peers[name] = (dp + along_dp * turn, head + along_head * turn)
    return dp, head, bits, peers


def remote(src, dst, send_sem, recv_sem, peer):
    return pltpu.make_async_remote_copy(
        src_ref=src,
        dst_ref=dst,
        send_sem=send_sem,
        recv_sem=recv_sem,
        device_id=peer,
        device_id_type=pl.DeviceIdType.MESH,
    )


def tile_of(fixed, free, place):
    total = 0
    for name, bit in fixed.items():
        total = total + STEP_DIMS[name] * bit
    for i, name in enumerate(free):
        total = total + STEP_DIMS[name] * ((place // 2**i) % 2)
    return total


def scatter_start(acc, got, base, fixed, name, free, bits, peer, sems, slot):
    for place in range(2 ** len(free)):
        away = tile_of({**fixed, name: 1 - bits[name]}, free, place)
        remote(
            acc.at[away], got.at[base + place], sems[0].at[slot], sems[1].at[slot], peer
        ).start()


def scatter_end(acc, got, base, fixed, name, free, bits, peer, sems, slot):
    count = 2 ** len(free)
    span = got.at[pl.ds(base, count)]
    remote(span, span, sems[0].at[slot], sems[1].at[slot], peer).wait()
    rows = acc.shape[1]

    def body(i):
        here = tile_of({**fixed, name: bits[name]}, free, i)
        acc[here] = (acc[here].astype(F32) + got[base + i].astype(F32)).astype(LOW)

    each(count, body)


def gather_start(ref, done, name, bits, peer, sems, slot):
    fixed = {d: bits[d] for d in STEP_DIMS if d not in done}
    for place in range(2 ** len(done)):
        part = ref.at[tile_of(fixed, done, place)]
        remote(part, part, sems[0].at[slot], sems[1].at[slot], peer).start()


def gather_end(ref, done, peer, sems, slot):
    span = ref.at[pl.ds(0, 2 ** len(done))]
    remote(span, span, sems[0].at[slot], sems[1].at[slot], peer).wait()


def paired(block):
    parts = [block[:, i * 64 : i * 64 + 64] for i in (0, 3, 1, 4, 2, 5)]
    return jnp.concatenate(parts, axis=1)


def unpaired(block):
    parts = [block[:, i * 64 : i * 64 + 64] for i in (0, 2, 4, 1, 3, 5)]
    return jnp.concatenate(parts, axis=1)


class Slots:
    def __init__(self):
        self.used = 0

    def __call__(self, count):
        start = self.used
        self.used += count
        return start


def update_step(pool, now, later, count, blocks, lanes, gram, mix):
    for low, high in ((0, 512), (256, 512)):
        rows = slice(low, low + 256)
        cols = slice(low, high)
        total = dot_back(pool[now, rows, :], pool[now, cols, :])
        for b in range(1, count):
            total = total + dot_back(pool[now + b, rows, :], pool[now + b, cols, :])
        made = total.astype(LOW)
        gram[rows, cols] = made
        if low == 0:
            gram[256:512, 0:256] = made[:, 256:512].T
    for low, high in ((0, 512), (256, 512)):
        rows = slice(low, low + 256)
        cols = slice(low, high)
        made = (
            ns_b * gram[rows, cols].astype(F32) + ns_c * dot(gram[rows, :], gram[:, cols])
        ).astype(LOW)
        mix[rows, cols] = made
        if low == 0:
            mix[256:512, 0:256] = made[:, 256:512].T

    def next_body(i):
        b = blocks[0] + i
        value = pool[now + b, :, lanes]
        pool[later + b, :, lanes] = (ns_a * value.astype(F32) + dot(mix[...], value)).astype(LOW)

    each(blocks[1], next_body)


def layer_kernel(
    tokens, segments, out_grad, params, w_qkv, m_qkv, w_out, m_out, w_up, m_up, w_down, m_down,
    layer_out, input_grad, start_a, start_u, start_d, ortho_q, ortho_o, ortho_u, ortho_d, norm_sum, scal,
    first, mixed, context, bias, wqkv, wout, wup, wdown, pool, middle, second, second_t, out_grad_t,
    active, hidden_grad, result, second_grad, acc_a, acc_u, acc_d, got_a, got_u, got_d,
    mom_full, mom_x, mom_u, mom_d, mom_a, norm_got, norm_far, stat_got, stat_far, gram, mix, send, recv,
):
    dp, head, bits, peers = coordinates()
    me = dp * 4 + head
    sibling = peers["c"]
    across = (dp, 3 - head)
    sems = (send, recv)
    slots = Slots()
    S_Q, S_O, S_M, S_MA = slots(4), slots(4), slots(2), slots(4)
    S_W, S_CORE, S_CHUNK, S_LG = slots(16), slots(20), slots(24), slots(16)
    S_A, S_NORM, S_STAT, S_START, S_SIDE, S_ORTHO = (
        slots(12), slots(2), slots(2), slots(15), slots(2), slots(8)
    )
    barrier = pltpu.get_barrier_semaphore()

    partners = (sibling, peers["x"], across)

    def along(i):
        return ((dp + 1 + i) % 8, head)

    def greet(peer):
        pl.semaphore_signal(barrier, inc=1, device_id=peer, device_id_type=pl.DeviceIdType.MESH)

    for peer in partners:
        greet(peer)
    each(7, lambda i: greet(along(i)))
    wqkv[head] = paired(w_qkv[...].astype(LOW))
    wout[pl.ds(pl.multiple_of(head * 128, 128), 128), :] = w_out[...].astype(LOW)
    mine = pl.ds(pl.multiple_of(me * 64, 64), 64)
    wup[mine, :] = w_up[...].astype(LOW)
    wdown[mine, :] = w_down[...].astype(LOW)
    pl.semaphore_wait(barrier, 10)

    def block_q(who):
        return wqkv.at[who]

    def block_o(who):
        return wout.at[pl.ds(pl.multiple_of(who * 128, 128), 128)]

    def weight_copy(block, who, slot, peer):
        return remote(block(who), block(who), send.at[slot], recv.at[slot], peer)

    def weight_tiles(i, k, far):
        matrix, start, count, order = GATHERS[i]
        done = order[: max(k, 0)]
        fixed = {d: bits[d] for d in STEP_DIMS if d not in done}
        if far and k >= 0:
            fixed[order[k]] = 1 - bits[order[k]]
        name = "c" if far else order[k]
        slot = S_CORE + i * 5 + k + 1 if far else S_W + i * 4 + k
        for place in range(2 ** len(done)):
            row = pl.multiple_of(tile_of(fixed, done, place) * 64, 64)
            part = (wup, wdown)[matrix].at[pl.ds(row, 64), pl.ds(start, count)]
            remote(part, part, send.at[slot], recv.at[slot], peers[name]).start()

    def weight_wait(i, k, far):
        matrix, start, count, _ = GATHERS[i]
        slot = S_CORE + i * 5 + k + 1 if far else S_W + i * 4 + k
        span = (wup, wdown)[matrix].at[pl.ds(0, 64 * 2 ** max(k, 0)), pl.ds(start, count)]
        remote(span, span, send.at[slot], recv.at[slot], sibling).wait()

    for i in range(len(GATHERS)):
        weight_tiles(i, 0, False)
    weight_copy(block_q, head, S_Q + 1, sibling).start()
    weight_copy(block_q, head, S_Q + 2, peers["x"]).start()
    other_half = pl.ds(pl.multiple_of((1 - bits["c"]) * 256, 256), 256)

    def moment_copy(i, ref):
        return remote(ref.at[:, other_half], mom_x.at[i], send.at[S_M + i], recv.at[S_M + i], sibling)

    moment_copy(0, m_up).start()
    moment_copy(1, m_down).start()

    parts = range(len(GATHERS))

    def weight_step(k):
        for i in parts:
            weight_wait(i, k, False)
            if k < 3:
                weight_tiles(i, k + 1, False)
        for i in parts:
            weight_tiles(i, k, True)

    weight_copy(block_o, head, S_O + 1, sibling).start()
    weight_copy(block_o, head, S_O + 2, peers["x"]).start()
    for i in parts:
        weight_tiles(i, -1, True)
    first_phase(tokens, params, first)
    bias_phase(segments, head, bias)
    mom_full[:, 0:384] = paired(m_qkv[...])
    mom_full[:, 384:512] = m_out[...].T

    def rank_of(c, x):
        return c * 16 + x * 8 + bits["y"] * 4 + bits["l"] * 2 + bits["g"]

    def rank_rows(who):
        return pl.ds(pl.multiple_of(rank_of(who % 2, who // 2) * 16, 16), 16)

    def rows_copy(j):
        who = partners[j][1]
        return remote(
            mom_full.at[rank_rows(who)], mom_a.at[head], send.at[S_MA + j], recv.at[S_MA + j], partners[j]
        )

    for j in range(3):
        rows_copy(j).start()
    mom_a[head] = mom_full[rank_rows(head), :]

    def pair_body(j):
        pair = (bits["c"] + j % 2) % 2 + 2 * ((bits["x"] + j // 2) % 2)
        mixed_phase(pair, first, wqkv, mixed)
        attend_phase(pair, mixed, bias, pool, context)

        @pl.when(j == 0)
        def _():
            weight_step(0)
            turn_phase(out_grad, out_grad_t)
            weight_copy(block_q, head, S_Q + 1, sibling).wait()
            weight_copy(block_o, head, S_O + 1, sibling).wait()

        @pl.when(j == 1)
        def _():
            weight_copy(block_q, head, S_Q + 2, peers["x"]).wait()
            weight_copy(block_q, peers["x"][1], S_Q + 3, sibling).start()
            weight_step(1)
            weight_copy(block_o, head, S_O + 2, peers["x"]).wait()
            weight_copy(block_o, peers["x"][1], S_O + 3, sibling).start()

        @pl.when(j == 2)
        def _():
            weight_copy(block_q, head, S_Q + 3, sibling).wait()
            weight_copy(block_o, head, S_O + 3, sibling).wait()

    each(PAIRS, pair_body)
    weight_step(2)
    second_phase(tokens, context, wout, params, middle, second)
    turn_phase(second, second_t)
    result[...] = jnp.zeros_like(result)
    second_grad[...] = jnp.zeros_like(second_grad)
    weight_step(3)
    for k in range(-1, 4):
        for i in parts:
            weight_wait(i, k, True)

    chunk_orders = ((acc_u, got_u, ("c", "x", "y")), (acc_d, got_d, ("c", "y", "x")))

    def chunk_args(q, k, order):
        fixed = {"g": q // 2, "l": q % 2}
        for name in order[:k]:
            fixed[name] = bits[name]
        return fixed, order[k], order[k + 1 :]

    def chunk_start(q, k):
        for i, (acc, got, order) in enumerate(chunk_orders):
            fixed, name, free = chunk_args(q, k, order)
            scatter_start(
                acc, got, q * 7 + (0, 4, 6)[k], fixed, name, free, bits, peers[name], sems,
                S_CHUNK + q * 6 + i * 3 + k,
            )

    def chunk_end(q, k):
        for i, (acc, got, order) in enumerate(chunk_orders):
            fixed, name, free = chunk_args(q, k, order)
            scatter_end(
                acc, got, q * 7 + (0, 4, 6)[k], fixed, name, free, bits, peers[name], sems,
                S_CHUNK + q * 6 + i * 3 + k,
            )

    def feed_body(q):
        feed_phase(
            q, second, second_t, out_grad, out_grad_t, wup, wdown, active, hidden_grad,
            result, second_grad, acc_u, acc_d,
        )
        chunk_start(q, 0)

        @pl.when(q >= 1)
        def _():
            chunk_end(q - 1, 0)
            chunk_start(q - 1, 1)

        @pl.when(q >= 3)
        def _():
            chunk_end(q - 3, 1)
            chunk_start(q - 3, 2)

    each(WIDE // CHUNK, feed_body)
    middle_phase(
        params, middle, result, second_grad, out_grad, wout,
        layer_out, input_grad, second, active, norm_got.at[head],
    )
    chunk_end(3, 0)
    chunk_start(3, 1)
    chunk_end(1, 1)
    chunk_start(1, 2)
    turn_phase(second, second_t)
    out_phase(second_t, context, acc_a)
    turn_phase(first, second_t)

    depth = dp // 2

    def owner_copy(i, acc, got, q):
        tile = tile_of({"g": q // 2, "l": q % 2, "c": bits["c"], "x": bits["x"], "y": bits["y"]}, (), 0)
        other = (2 * q + bits["y"], head)
        return remote(
            acc.at[tile], got.at[28 + (depth - q + 3) % 4], send.at[S_LG + 2 * q + i],
            recv.at[S_LG + 8 + 3 * i + (depth - q + 3) % 4], other,
        )

    def owner_start(q):
        @pl.when(depth != q)
        def _():
            for i, (acc, got, _) in enumerate(chunk_orders):
                owner_copy(i, acc, got, q).start()

    def owner_sent(q):
        @pl.when(depth != q)
        def _():
            for i, (acc, got, _) in enumerate(chunk_orders):
                owner_copy(i, acc, got, q).wait_send()

    def owner_end():
        for i, (acc, got, _) in enumerate(chunk_orders):
            for way in range(3):
                remote(
                    got.at[28 + way], got.at[28 + way], send.at[S_LG], recv.at[S_LG + 8 + 3 * i + way], sibling
                ).wait_recv()
            total = acc[me].astype(F32)
            for way in range(3):
                total = total + got[28 + way].astype(F32)
            acc[me] = total.astype(LOW)

    spans = []
    low_row = 0
    for k, name in enumerate(ATTEND_ORDER):
        size = 256 >> k
        spans.append((name, size, low_row + bits[name] * size, low_row + (1 - bits[name]) * size))
        low_row = low_row + bits[name] * size

    def aligned(row, size):
        return pl.ds(pl.multiple_of(row, 16), size)

    def attend_copy(pair, k):
        name, size, _, give = spans[k]
        return remote(
            acc_a.at[pair, aligned(give, size)], got_a.at[pair, pl.ds(512 - 2 * size, size)],
            send.at[S_A + pair * 3 + k], recv.at[S_A + pair * 3 + k], peers[name],
        )

    quarter = spans[1][2]

    def place_of(group):
        return (group % 2) * 4 + ((group // 2) % 2) * 2 + group // 4

    def attend_start(pair, k):
        if k < 2:
            attend_copy(pair, k).start()
            return

        def body(i):
            other = (dp + 1 + i) % 8
            remote(
                acc_a.at[pair, aligned(quarter + place_of(other) * 16, 16)],
                got_a.at[pair, aligned(384 + (6 - i) * 16, 16)],
                send.at[S_A + pair * 3 + 2], recv.at[S_A + pair * 3 + 2], (other, head),
            ).start()

        each(7, body)

    def attend_next(pair, k):
        if k == 2:
            span = got_a.at[pair, pl.ds(384, 112)]
            remote(span, span, send.at[S_A + pair * 3 + 2], recv.at[S_A + pair * 3 + 2], sibling).wait()
            here = aligned(low_row, 16)
            total = acc_a[pair, here, :].astype(F32)
            for i in range(1, 8):
                total = total + got_a[pair, 368 + i * 16 : 384 + i * 16, :].astype(F32)
            acc_a[pair, here, :] = total.astype(LOW)
            return
        attend_copy(pair, k).wait()
        _, size, keep, _ = spans[k]

        def body(i):
            here = aligned(keep + i * 64, 64)
            come = aligned(512 - 2 * size + i * 64, 64)
            acc_a[pair, here, :] = (
                acc_a[pair, here, :].astype(F32) + got_a[pair, come, :].astype(F32)
            ).astype(LOW)

        each(size // 64, body)
        attend_start(pair, k + 1)

    def at(wanted, pair):
        return pl.when(pair == wanted)

    def back_body(pair):
        attend_back_phase(pair, 0, mixed, pool, context, active)

        @at(0, pair)
        def _():
            chunk_end(0, 2)
            owner_start(0)
            chunk_end(2, 1)
            chunk_start(2, 2)

        @at(1, pair)
        def _():
            attend_next(0, 0)
            chunk_end(3, 1)
            chunk_start(3, 2)

        @at(2, pair)
        def _():
            attend_next(1, 0)
            attend_next(0, 1)

        @at(3, pair)
        def _():
            attend_next(2, 0)
            attend_next(1, 1)

        attend_back_phase(pair, 1, mixed, pool, context, active)
        qkv_phase(pair, mixed, second_t, acc_a)
        attend_start(pair, 0)

        @at(0, pair)
        def _():
            chunk_end(1, 2)
            owner_start(1)

        @at(1, pair)
        def _():
            chunk_end(2, 2)
            owner_start(2)

        @at(2, pair)
        def _():
            chunk_end(3, 2)
            owner_start(3)

    each(PAIRS, back_body)
    attend_next(3, 0)
    attend_next(2, 1)
    attend_next(0, 2)
    input_phase(params, tokens, mixed, wqkv, input_grad, norm_got.at[head])

    def tell(ref, slot):
        for peer in partners:
            remote(ref.at[head], ref.at[head], send.at[slot], recv.at[slot], peer).start()

    def tell_on(ref, far, slot):
        span = ref.at[pl.ds(0, 3)]
        remote(span, span, send.at[slot], recv.at[slot], sibling).wait()
        far[dp] = (ref[0] + ref[1]) + (ref[2] + ref[3])

        def body(i):
            remote(
                far.at[dp], far.at[dp], send.at[slot + 1], recv.at[slot + 1], along(i)
            ).start()

        each(7, body)

    def told_of(far, slot):
        span = far.at[pl.ds(0, 7)]
        remote(span, span, send.at[slot + 1], recv.at[slot + 1], sibling).wait()
        return jnp.sum(far[...], axis=0)

    tell(norm_got, S_NORM)
    attend_next(3, 1)
    attend_next(1, 2)
    tell_on(norm_got, norm_far, S_NORM)
    for q in range(4):
        owner_sent(q)
    owner_end()
    moment_copy(0, m_up).wait()
    moment_copy(1, m_down).wait()
    keep_half = pl.ds(pl.multiple_of(bits["c"] * 256, 256), 256)
    for i, (ref, out) in enumerate(((m_up, mom_u), (m_down, mom_d))):
        own = ref[:, keep_half]
        far = mom_x[i]
        low_half = jnp.where(bits["c"] == 0, own, far)
        high_half = jnp.where(bits["c"] == 0, far, own)
        out[...] = jnp.concatenate([low_half, high_half], axis=0).T
    for j in range(3):
        rows_copy(j).wait()

    def total_of(value):
        return jnp.sum(jnp.sum(value, axis=0, keepdims=True), axis=1, keepdims=True)

    lane = lax.broadcasted_iota(jnp.int32, (8, 128), 1)
    column = lax.broadcasted_iota(jnp.int32, (1, 512), 1)
    grad_u = acc_u[me].astype(F32)
    grad_d = acc_d[me].astype(F32)
    stats = jnp.zeros((8, 128), F32)
    for m, (moment, grad) in enumerate(((mom_u[...], grad_u), (mom_d[...], grad_d))):
        for i, product in enumerate((moment * moment, moment * grad, grad * grad)):
            stats = jnp.where(lane == 6 + 3 * m + i, total_of(product), stats)
    attend_next(2, 2)
    attend_next(3, 2)
    vector = told_of(norm_far, S_NORM)
    norm_sum[...] = vector
    vector_total = total_of(vector * vector)
    my_rows = aligned(low_row, 16)
    for i in range(3):
        inside = jnp.zeros((1, 512), F32)
        for pair in range(PAIRS):
            moment = mom_a[pair]
            grad = acc_a[pair, my_rows, :].astype(F32)
            product = (moment * moment, moment * grad, grad * grad)[i]
            inside = inside + jnp.sum(product, axis=0, keepdims=True)
        stats = jnp.where(lane == i, total_of(jnp.where(column < 384, inside, 0.0)), stats)
        stats = jnp.where(lane == 3 + i, total_of(jnp.where(column < 384, 0.0, inside)), stats)
    stat_got[head] = stats
    tell(stat_got, S_STAT)
    tell_on(stat_got, stat_far, S_STAT)
    stats = told_of(stat_far, S_STAT)

    def stat(i):
        return jnp.sum(jnp.where(lane == i, stats, 0.0), axis=1, keepdims=True)[0:1]

    norm = jnp.sqrt(stat(2) + stat(5) + stat(8) + stat(11) + vector_total)
    clip = jnp.minimum(1.0, 1.0 / (norm + 1e-06))
    sizes = []
    for m in range(4):
        square = (
            momentum_decay * momentum_decay * stat(3 * m)
            + 2.0 * momentum_decay * clip * stat(3 * m + 1)
            + clip * clip * stat(3 * m + 2)
        )
        sizes.append(jnp.sqrt(jnp.maximum(square, 0.0)) + 1e-07)
    told = jnp.where(lane == 0, norm, clip)
    for m in range(4):
        told = jnp.where(lane == 2 + m, sizes[m], told)
    scal[...] = told
    scale_a = jnp.where(column < 384, 1.0 / sizes[0], 1.0 / sizes[1])
    got_u[me] = ((momentum_decay * mom_u[...] + clip * grad_u) * (1.0 / sizes[2])).astype(LOW)
    got_d[me] = ((momentum_decay * mom_d[...] + clip * grad_d) * (1.0 / sizes[3])).astype(LOW)
    for pair in range(PAIRS):
        grad = acc_a[pair, my_rows, :].astype(F32)
        pool[pair, my_rows, :] = ((momentum_decay * mom_a[pair] + clip * grad) * scale_a).astype(LOW)

    mine_half = pl.ds(pl.multiple_of(bits["c"] * 256, 256), 256)

    def side_copy(i):
        src, dst = ((got_u, start_u), (got_d, start_d))[i]
        return remote(
            src.at[me], dst.at[mine_half], send.at[S_SIDE + i], recv.at[S_SIDE + i], sibling
        )

    side_copy(0).start()
    side_copy(1).start()
    start_u[mine_half, :] = got_u[me]
    start_d[mine_half, :] = got_d[me]

    def start_copy(k):
        name, size, keep, _ = spans[4 - k]
        part = pool.at[pl.ds(0, 4), aligned(keep, size)]
        return remote(part, part, send.at[S_START + 3 * k], recv.at[S_START + 3 * k], peers[name])

    tiles = ((got_u, STARTS[1]), (got_d, STARTS[2]))
    half_rows = aligned(spans[0][2], 256)
    pair_part = pool.at[pl.ds(head + 1 - 2 * bits["c"], 1), half_rows]
    all_part = pool.at[pl.ds(0, 4), half_rows]

    def core_copy(part):
        return remote(part, part, send.at[S_START + 12], recv.at[S_START + 12], sibling)

    def core_tiles(late):
        @pl.when(bits["c"] == 1)
        def _():
            row = spans[1][3] if late else spans[1][2]
            core_copy(pool.at[pl.ds(0, 4), aligned(row, 128)]).start()

        @pl.when(bits["c"] == 0)
        def _():
            for x, (got, order) in enumerate(tiles):
                @pl.when(bits["x"] == x)
                def _(got=got, order=order):
                    flipped = {**bits, order[3]: 1 - bits[order[3]]} if late else bits
                    gather_start(got, order[:3], "c", flipped, sibling, sems, S_START + 13)

    def core_early():
        core_tiles(False)

    for k in range(5):
        if k > 0:
            start_copy(k - 1).wait()
        if k < 4:
            start_copy(k).start()
        for m, (got, order) in enumerate(tiles):
            if k > 0:
                gather_end(got, order[: k - 1], peers[order[k - 1]], sems, S_START + 3 * k - 2 + m)
            if k < 4:
                gather_start(
                    got, order[:k], order[k], bits, peers[order[k]], sems, S_START + 3 * k + 1 + m
                )
        if k == 3:
            core_early()
    core_tiles(True)

    @pl.when(bits["c"] == 1)
    def _():
        def slice_body(i):
            rows = rows_at(i, 256)
            start_a[rows, :] = pool[head, rows, :]

        for x, (got, order) in enumerate(tiles):
            @pl.when(bits["x"] == x)
            def _(got=got, order=order, x=x):
                span = got.at[pl.ds(0, 16)]
                remote(span, span, send.at[S_START + 13], recv.at[S_START + 13], sibling).wait_recv()

                def body(i):
                    for j in range(4):
                        for c in range(2):
                            pool[4 + i, c * 256 : c * 256 + 256, j * 128 : j * 128 + 128] = got[
                                i * 8 + j * 2 + c
                            ]

                each(4, body)

        core_copy(pair_part).wait_recv()
        core_copy(all_part).wait_send()
        each(2, slice_body)

    @pl.when(bits["c"] == 0)
    def _():
        core_copy(pair_part).start()
        core_copy(all_part).wait_recv()

        def body(i):
            rows = rows_at(i, 256)
            start_a[rows, :] = pool[head, rows, :]
            for p in range(PAIRS):
                for r in range(3):
                    group = p * 3 + r
                    pool[4 + group // 4, rows, (group % 4) * 128 : (group % 4) * 128 + 128] = pool[
                        p, rows, r * 128 : r * 128 + 128
                    ]
                pool[7, rows, p * 128 : p * 128 + 128] = pool[p, rows, 384:512]

        each(2, body)
        core_copy(pair_part).wait_send()
        span = got_u.at[pl.ds(0, 16)]
        remote(span, span, send.at[S_START + 13], recv.at[S_START + 13], sibling).wait_send()

    side_copy(0).wait()
    side_copy(1).wait()

    every = pl.ds(0, 512)
    outs = (ortho_u, ortho_d)

    def out_copy(src, dst, i, peer):
        return remote(src, dst, send.at[S_ORTHO + i], recv.at[S_ORTHO + i], peer)

    def group_of(r):
        group = bits["x"] * 6 + r
        return pool.at[8 + group // 4, :, pl.ds(pl.multiple_of((group % 4) * 128, 128), 128)]

    def out_of(who):
        return pool.at[11, :, pl.ds(pl.multiple_of(who * 128, 128), 128)]

    @pl.when(bits["c"] == 0)
    def _():
        def turn_body(turn):
            now = 4 + (turn % 2) * 4
            later = 12 - now
            update_step(pool, now, later, 3, (0, 3), every, gram, mix)
            update_step(pool, now + 3, later + 3, 1, (0, 1), every, gram, mix)

        each(NS_STEPS - 1, turn_body)
        update_step(pool, 4, 8, 3, (bits["x"], 2), every, gram, mix)
        for r in range(3):
            out_copy(group_of(3 + r), ortho_q.at[:, pl.ds(r * 128, 128)], 0, sibling).start()
        for r in range(3):
            ortho_q[:, r * 128 : r * 128 + 128] = group_of(r)[...]
        columns = pl.ds(pl.multiple_of(bits["x"] * 256, 256), 256)
        update_step(pool, 7, 11, 1, (0, 1), columns, gram, mix)
        out_copy(out_of(head + 1), ortho_o, 1, sibling).start()
        ortho_o[...] = out_of(head)[...]
        out_copy(ortho_q, ortho_q, 0, sibling).wait_send()
        out_copy(ortho_o, ortho_o, 1, sibling).wait_send()

    @pl.when(bits["c"] == 1)
    def _():
        def turn_body(turn):
            now = 4 + (turn % 2) * 4
            update_step(pool, now, 12 - now, 4, (0, 4), every, gram, mix)

        each(NS_STEPS - 1, turn_body)
        wanted = dp // 2
        update_step(pool, 4, 8, 4, (wanted, 1), every, gram, mix)

        def block_of(x):
            block = dp * 2 + x
            return pool.at[8 + wanted, :, pl.ds(pl.multiple_of((block % 4) * 128, 128), 128)]

        for x in range(2):
            @pl.when(bits["x"] == x)
            def _(x=x):
                targets = ((across, 1 - x), (peers["x"], 1 - x), (sibling, x))
                for j, (peer, side) in enumerate(targets):
                    remote(
                        block_of(side), outs[x], send.at[S_ORTHO + 2 + j], recv.at[S_ORTHO + 2 + x], peer
                    ).start()
                outs[x][...] = block_of(x)[...]
                for j, (peer, side) in enumerate(targets):
                    remote(
                        block_of(side), outs[x], send.at[S_ORTHO + 2 + j], recv.at[S_ORTHO + 2 + x], peer
                    ).wait_send()

        out_copy(ortho_q, ortho_q, 0, sibling).wait_recv()
        out_copy(ortho_o, ortho_o, 1, sibling).wait_recv()

    for x in range(2):
        @pl.when(head != 2 * x + 1)
        def _(x=x):
            out_copy(outs[x], outs[x], 2 + x, sibling).wait_recv()


def layer_call(*args):
    shape = jax.ShapeDtypeStruct
    vmem = pl.BlockSpec(memory_space=pltpu.VMEM)
    outs = (
        shape((ROWS, 512), LOW), shape((ROWS, 512), F32),
        shape((512, 512), LOW), shape((512, 128), LOW), shape((512, 128), LOW),
        shape((512, 384), LOW), shape((512, 128), LOW), shape((512, 128), LOW), shape((512, 128), LOW),
        shape((4, 512), F32), shape((8, 128), F32),
    )
    scratch = [
        ((ROWS, 512), LOW),
        ((PAIRS, ROWS, 384), LOW),
        ((ROWS, 512), LOW),
        ((ROWS, SEQ), LOW),
        ((PAIRS, 512, 384), LOW),
        ((512, 512), LOW),
        ((WIDE, 512), LOW),
        ((WIDE, 512), LOW),
        ((16, 512, 512), LOW),
        ((ROWS, 512), F32),
        ((ROWS, 512), LOW),
        ((512, ROWS), LOW),
        ((512, ROWS), LOW),
        ((ROWS, CHUNK), LOW),
        ((ROWS, CHUNK), LOW),
        ((ROWS, 512), F32),
        ((ROWS, 512), F32),
        ((PAIRS, 512, 512), LOW),
        ((32, 256, 128), LOW),
        ((32, 256, 128), LOW),
        ((PAIRS, 512, 512), LOW),
        ((32, 256, 128), LOW),
        ((32, 256, 128), LOW),
        ((512, 512), F32),
        ((2, 64, 256), F32),
        ((256, 128), F32),
        ((256, 128), F32),
        ((PAIRS, 16, 512), F32),
        ((4, 4, 512), F32),
        ((8, 4, 512), F32),
        ((4, 8, 128), F32),
        ((8, 8, 128), F32),
        ((512, 512), LOW),
        ((512, 512), LOW),
    ]
    return pl.pallas_call(
        layer_kernel,
        out_shape=outs,
        in_specs=[vmem] * len(args),
        out_specs=(vmem,) * len(outs),
        scratch_shapes=[pltpu.VMEM(*v) for v in scratch]
        + [pltpu.SemaphoreType.DMA((128,)), pltpu.SemaphoreType.DMA((128,))],
        compiler_params=pltpu.CompilerParams(
            collective_id=1, has_side_effects=True, vmem_limit_bytes=VMEM_BYTES
        ),
        name="layer",
    )(*args)


def update_kernel(
    start_a, start_u, start_d, ortho_q, ortho_o, ortho_u, ortho_d, norm_sum, scal,
    w_qkv, w_out, w_up, w_down, norm_first, norm_second,
    new_q, mom_q, new_o, mom_o, new_u, mom_u, new_d, mom_d, clipped, first_new, second_new, norm,
):
    core = lax.axis_index("head") % 2
    clip = scal[0:1, 1:2]
    keep = 1.0 - muon_rate * muon_decay

    def fresh(weight, factor, ortho):
        return weight * keep - muon_rate * factor * ortho

    new_q[...] = fresh(w_qkv[...], math.sqrt(3.0), unpaired(ortho_q[...].astype(F32)))
    mom_q[...] = unpaired(start_a[:, 0:384].astype(F32)) * scal[0:1, 2:3]
    new_o[...] = fresh(w_out[...], math.sqrt(SEQ / 8.0), ortho_o[...].astype(F32).T)
    mom_o[...] = start_a[:, 384:512].astype(F32).T * scal[0:1, 3:4]
    for weight, ortho, start, new, mom, i in (
        (w_up, ortho_u, start_u, new_u, mom_u, 4),
        (w_down, ortho_d, start_d, new_d, mom_d, 5),
    ):
        turned = ortho[...].astype(F32).T
        turned = jnp.where(core == 0, turned[0:64], turned[64:128])
        new[...] = fresh(weight[...], math.sqrt(max(1.0, FF / 512)), turned)
        turned = start[...].astype(F32).T
        mom[...] = jnp.where(core == 0, turned[0:64], turned[64:128]) * scal[0:1, i : i + 1]
    norm[...] = scal[0:1, 0:1]
    clip_grad = clip * norm_sum[...]
    clipped[...] = clip_grad
    first_new[...] = beta_one * norm_first[...] + (1.0 - beta_one) * clip_grad
    second_new[...] = beta_two * norm_second[...] + (1.0 - beta_two) * clip_grad * clip_grad


def fast_shards(
    tokens,
    segments,
    out_grad,
    norm_params,
    norm_first,
    norm_second,
    qkv_weight,
    qkv_moment,
    out_weight,
    out_moment,
    up_weight,
    up_moment,
    down_weight,
    down_moment,
):
    (
        layer_out, input_grad, start_a, start_u, start_d, ortho_q, ortho_o, ortho_u, ortho_d, norm_sum, scal
    ) = layer_call(
        tokens, segments.reshape(segments.shape[0] // 128, 128), out_grad, norm_params,
        qkv_weight, qkv_moment, out_weight, out_moment,
        up_weight.T, up_moment.T, down_weight.T, down_moment.T,
    )
    tall = ((64, 512), F32)
    new_q, mom_q, new_o, mom_o, new_u, mom_u, new_d, mom_d, clipped, first_new, second_new, norm = local_call(
        update_kernel,
        [((512, 384), F32)] * 2 + [((128, 512), F32)] * 2 + [tall] * 4 + [((4, 512), F32)] * 3 + [((1, 1), F32)],
        [],
        (
            start_a, start_u, start_d, ortho_q, ortho_o, ortho_u, ortho_d, norm_sum, scal,
            qkv_weight, out_weight, up_weight.T, down_weight.T, norm_first, norm_second,
        ),
        "update",
    )
    return (
        layer_out, input_grad, norm.reshape(()), clipped, first_new, second_new,
        new_q, mom_q, new_o, mom_o, new_u.T, mom_u.T, new_d.T, mom_d.T,
    )


def general_update(
    whole_qkv, whole_out, up_grad, down_grad, vector_part,
    qkv_moment, out_moment, up_moment, down_moment,
):
    everywhere = ("dp", "head")
    narrow = out_moment.shape[0]
    up_part, down_part = (
        lax.psum_scatter(
            up_grad.astype(jnp.bfloat16), everywhere, scatter_dimension=1, tiled=True
        ).astype(jnp.float32),
        lax.psum_scatter(
            down_grad.astype(jnp.bfloat16), everywhere, scatter_dimension=1, tiled=True
        ).astype(jnp.float32),
    )
    qkv_part = lax.psum_scatter(
        whole_qkv.astype(jnp.bfloat16), "head", scatter_dimension=1, tiled=True
    )
    out_part = lax.psum_scatter(
        whole_out.astype(jnp.bfloat16), "head", scatter_dimension=0, tiled=True
    )
    qkv_sum, out_sum = (
        lax.psum(qkv_part, "dp").astype(jnp.float32),
        lax.psum(out_part, "dp").astype(jnp.float32),
    )
    leading = (lax.axis_index("dp") == 0).astype(jnp.float32)
    moments = [qkv_moment, out_moment, up_moment, down_moment]
    grads = [qkv_sum, out_sum, up_part, down_part]
    stats = jnp.stack(
        [
            squares_of(qkv_moment, qkv_sum, leading),
            squares_of(out_moment, out_sum, leading),
            squares_of(up_moment, up_part, 1.0),
            squares_of(down_moment, down_part, 1.0),
        ]
    )
    vector_sum, stat_sum = lax.psum((vector_part, stats), everywhere)
    grad_norm = jnp.sqrt(jnp.sum(stat_sum[:, 2]) + jnp.sum(vector_sum * vector_sum))
    clip = jnp.minimum(1.0, 1.0 / (grad_norm + 1e-06))
    sizes = jnp.sqrt(
        momentum_decay * momentum_decay * stat_sum[:, 0]
        + 2.0 * momentum_decay * clip * stat_sum[:, 1]
        + clip * clip * stat_sum[:, 2]
    )
    new_moments = [momentum_decay * moments[index] + clip * grads[index] for index in range(4)]
    starts = [
        (new_moments[index] / (sizes[index] + 1e-07)).astype(jnp.bfloat16) for index in range(4)
    ]
    blocks = [
        lax.all_gather(starts[0], "head", axis=1, tiled=True),
        lax.all_gather(starts[1], "head", axis=0, tiled=True),
        lax.all_gather(starts[2], everywhere, axis=1, tiled=True),
        lax.all_gather(starts[3], everywhere, axis=1, tiled=True),
    ]
    for turn in range(NS_STEPS):
        updated = []
        for index in range(4):
            form = gram_right if index == 1 else gram_left
            gram = form(blocks[index]).astype(jnp.bfloat16)
            mix = (
                ns_b * gram.astype(jnp.float32)
                + ns_c * jnp.dot(gram, gram, preferred_element_type=jnp.float32)
            ).astype(jnp.bfloat16)
            if index == 1:
                product = jnp.dot(blocks[index], mix, preferred_element_type=jnp.float32)
            else:
                product = jnp.dot(mix, blocks[index], preferred_element_type=jnp.float32)
            updated.append(
                (ns_a * blocks[index].astype(jnp.float32) + product).astype(jnp.bfloat16)
            )
        blocks = updated
    share = up_moment.shape[1]
    along = lax.axis_index("head")
    offset = (lax.axis_index("dp") * lax.axis_size("head") + along) * share
    owned = [
        lax.dynamic_slice_in_dim(blocks[0], along * qkv_moment.shape[1], qkv_moment.shape[1], 1),
        lax.dynamic_slice_in_dim(blocks[1], along * narrow, narrow, 0),
        lax.dynamic_slice_in_dim(blocks[2], offset, share, 1),
        lax.dynamic_slice_in_dim(blocks[3], offset, share, 1),
    ]
    return (owned, new_moments, vector_sum, grad_norm, clip)


def general_shards(
    tokens,
    segments,
    out_grad,
    norm_params,
    norm_first,
    norm_second,
    qkv_weight,
    qkv_moment,
    out_weight,
    out_moment,
    up_weight,
    up_moment,
    down_weight,
    down_moment,
):
    width = tokens.shape[1]
    rows = tokens.shape[0]
    narrow = out_weight.shape[0]
    sequences = rows // SEQ
    heads = width // HEAD_DIM
    everywhere = ("dp", "head")
    inputs = tokens.astype(jnp.float32)
    first, first_plain, first_factor = normalize(inputs, norm_params[0], norm_params[1])
    first_low = first.astype(jnp.bfloat16)
    qkv_full = lax.all_gather(qkv_weight.astype(jnp.bfloat16), "head", axis=1, tiled=True)
    out_full = lax.all_gather(out_weight.astype(jnp.bfloat16), "head", axis=0, tiled=True)
    up_all = lax.all_gather(up_weight.astype(jnp.bfloat16), everywhere, axis=1, tiled=True)
    down_all = lax.all_gather(down_weight.astype(jnp.bfloat16), everywhere, axis=1, tiled=True)
    mixed = jnp.dot(first_low, qkv_full, preferred_element_type=jnp.float32).astype(jnp.bfloat16)
    mixed = mixed.reshape(sequences, SEQ, heads, 3, HEAD_DIM)
    segment_rows = lax.dynamic_slice_in_dim(segments, lax.axis_index("head") * rows, rows, 0)
    segment_rows = segment_rows.reshape(sequences, SEQ)
    query = mixed[:, :, :, 0]
    keys = mixed[:, :, :, 1]
    values = mixed[:, :, :, 2]
    context, lse = lax.map(attend_forward, (query, keys, values, segment_rows))
    context = context.reshape(rows, width)
    attended = jnp.dot(context, out_full, preferred_element_type=jnp.float32)
    middle = inputs + attended
    second, second_plain, second_factor = normalize(middle, norm_params[2], norm_params[3])
    second_low = second.astype(jnp.bfloat16)
    hidden = jnp.dot(second_low, up_all, preferred_element_type=jnp.float32)
    switch = jax.nn.sigmoid(1.702 * hidden)
    active = (hidden * switch).astype(jnp.bfloat16)
    result = middle + lax.dot_general(
        active, down_all, (((1,), (1,)), ((), ())), preferred_element_type=jnp.float32
    )
    layer_out = result.astype(jnp.bfloat16)
    down_grad = lax.dot_general(
        out_grad, active, (((0,), (0,)), ((), ())), preferred_element_type=jnp.float32
    )
    active_grad = jnp.dot(out_grad, down_all, preferred_element_type=jnp.float32)
    hidden_grad = (active_grad * (switch + 1.702 * hidden * switch * (1.0 - switch))).astype(
        jnp.bfloat16
    )
    up_grad = lax.dot_general(
        second_low, hidden_grad, (((0,), (0,)), ((), ())), preferred_element_type=jnp.float32
    )
    second_grad = lax.dot_general(
        hidden_grad, up_all, (((1,), (1,)), ((), ())), preferred_element_type=jnp.float32
    )
    middle_lower, gain_two, shift_two = normalize_back(
        second_grad, second_plain, second_factor, norm_params[2]
    )
    middle_grad = out_grad.astype(jnp.float32) + middle_lower
    attended_low = middle_grad.astype(jnp.bfloat16)
    context_grad = lax.dot_general(
        attended_low, out_full, (((1,), (1,)), ((), ())), preferred_element_type=jnp.float32
    ).astype(jnp.bfloat16)
    whole_out = lax.dot_general(
        context, attended_low, (((0,), (0,)), ((), ())), preferred_element_type=jnp.float32
    )
    context_grad = context_grad.reshape(sequences, SEQ, heads, HEAD_DIM)
    mixed_grad = lax.map(attend_backward, (query, keys, values, segment_rows, context_grad, lse))
    mixed_grad = mixed_grad.reshape(rows, 3 * width)
    whole_qkv = lax.dot_general(
        first_low, mixed_grad, (((0,), (0,)), ((), ())), preferred_element_type=jnp.float32
    )
    first_grad = lax.dot_general(
        mixed_grad, qkv_full, (((1,), (1,)), ((), ())), preferred_element_type=jnp.float32
    )
    input_lower, gain_one, shift_one = normalize_back(
        first_grad, first_plain, first_factor, norm_params[0]
    )
    input_grad = middle_grad + input_lower
    vector_part = jnp.stack([gain_one, shift_one, gain_two, shift_two])
    (owned, new_moments, vector_sum, grad_norm, clip) = general_update(
        whole_qkv, whole_out, up_grad, down_grad, vector_part,
        qkv_moment, out_moment, up_moment, down_moment,
    )
    weights = [qkv_weight, out_weight, up_weight, down_weight]
    factors = [
        math.sqrt(3.0),
        math.sqrt(SEQ / 8.0),
        math.sqrt(max(1.0, FF / width)),
        math.sqrt(max(1.0, FF / width)),
    ]
    new_weights = [
        weights[index] * (1.0 - muon_rate * muon_decay)
        - muon_rate * factors[index] * owned[index].astype(jnp.float32)
        for index in range(4)
    ]
    clipped = clip * vector_sum
    first_new = beta_one * norm_first + (1.0 - beta_one) * clipped
    second_new = beta_two * norm_second + (1.0 - beta_two) * clipped * clipped
    return (
        layer_out,
        input_grad,
        grad_norm,
        clipped,
        first_new,
        second_new,
        new_weights[0],
        new_moments[0],
        new_weights[1],
        new_moments[1],
        new_weights[2],
        new_moments[2],
        new_weights[3],
        new_moments[3],
    )


def solution(mesh):
    placed = (
        P(("dp", "head"), None),
        P("dp"),
        P(("dp", "head"), None),
        P(),
        P(),
        P(),
        P(None, "head"),
        P(None, "head"),
        P("head", None),
        P("head", None),
        P(None, ("dp", "head")),
        P(None, ("dp", "head")),
        P(None, ("dp", "head")),
        P(None, ("dp", "head")),
    )
    fast = mesh.shape["dp"] == 8 and mesh.shape["head"] == 4
    return jax.shard_map(
        fast_shards if fast else general_shards,
        mesh=mesh,
        in_specs=placed,
        out_specs=(
            P(("dp", "head"), None),
            P(("dp", "head"), None),
            P(),
            P(),
            P(),
            P(),
            P(None, "head"),
            P(None, "head"),
            P("head", None),
            P("head", None),
            P(None, ("dp", "head")),
            P(None, ("dp", "head")),
            P(None, ("dp", "head")),
            P(None, ("dp", "head")),
        ),
        check_vma=False,
    )
```

```python
import math

import jax
import jax.numpy as jnp
from jax import lax
from jax.experimental import pallas as pl
from jax.experimental.pallas import tpu as pltpu
from jax.sharding import PartitionSpec as P

HEAD_DIM = 64
FF = 2048
SEQ = 512
NS_STEPS = 5


neg_fill = -1000000000.0
norm_eps = 1e-05
ns_a = 3.4445
ns_b = -4.775
ns_c = 2.0315
momentum_decay = 0.95
muon_rate = 0.5
muon_decay = 0.01
beta_one = 0.9
beta_two = 0.95


def normalize(values, gain, shift):
    mean = jnp.mean(values, axis=-1, keepdims=True)
    centered = values - mean
    factor = lax.rsqrt(jnp.mean(centered * centered, axis=-1, keepdims=True) + norm_eps)
    plain = centered * factor
    return (plain * gain + shift, plain, factor)


def normalize_back(upper, plain, factor, gain):
    inner = upper * gain
    lower = factor * (
        inner
        - jnp.mean(inner, axis=-1, keepdims=True)
        - plain * jnp.mean(inner * plain, axis=-1, keepdims=True)
    )
    return (lower, jnp.sum(upper * plain, axis=0), jnp.sum(upper, axis=0))


def masked_scores(query, keys, segment):
    scores = jnp.einsum(
        "qhd,khd->hqk", query, keys, preferred_element_type=jnp.float32
    ) * HEAD_DIM ** (-0.5)
    same = segment[:, None] == segment[None, :]
    return jnp.where(same[None], scores, neg_fill)


def attend_forward(block):
    query, keys, values, segment = block
    scores = masked_scores(query, keys, segment)
    top = jnp.max(scores, axis=-1, keepdims=True)
    weights = jnp.exp(scores - top)
    total = jnp.sum(weights, axis=-1, keepdims=True)
    probs = (weights / total).astype(jnp.bfloat16)
    context = jnp.einsum("hqk,khd->qhd", probs, values, preferred_element_type=jnp.float32)
    return (context.astype(jnp.bfloat16), top + jnp.log(total))


def attend_backward(block):
    query, keys, values, segment, context_grad, lse = block
    scores = masked_scores(query, keys, segment)
    probs = jnp.exp(scores - lse)
    probs_low = probs.astype(jnp.bfloat16)
    probs_grad = jnp.einsum(
        "qhd,khd->hqk", context_grad, values, preferred_element_type=jnp.float32
    )
    inner = jnp.sum(probs * probs_grad, axis=-1, keepdims=True)
    score_grad = (probs * (probs_grad - inner)).astype(jnp.bfloat16)
    query_grad = jnp.einsum(
        "hqk,khd->qhd", score_grad, keys, preferred_element_type=jnp.float32
    ) * HEAD_DIM ** (-0.5)
    key_grad = jnp.einsum(
        "hqk,qhd->khd", score_grad, query, preferred_element_type=jnp.float32
    ) * HEAD_DIM ** (-0.5)
    value_grad = jnp.einsum(
        "hqk,qhd->khd", probs_low, context_grad, preferred_element_type=jnp.float32
    )
    return jnp.stack([query_grad, key_grad, value_grad], axis=2).astype(jnp.bfloat16)


def gram_left(block):
    return lax.dot_general(
        block, block, (((1,), (1,)), ((), ())), preferred_element_type=jnp.float32
    )


def gram_right(block):
    return lax.dot_general(
        block, block, (((0,), (0,)), ((), ())), preferred_element_type=jnp.float32
    )


def squares_of(moment, grad, weight):
    return (
        jnp.stack([jnp.sum(moment * moment), jnp.sum(moment * grad), jnp.sum(grad * grad)]) * weight
    )


ROWS = 1024
TILE = 512
PAIRS = 4
WIDE = 2048
CHUNK = 512
VMEM_BYTES = 62 << 20
LOW = jnp.bfloat16
F32 = jnp.float32


def dot(one, two):
    return jnp.dot(one, two, preferred_element_type=F32)


def dot_back(one, two):
    return lax.dot_general(one, two, (((1,), (1,)), ((), ())), preferred_element_type=F32)


def dot_rows(one, two):
    return lax.dot_general(one, two, (((0,), (0,)), ((), ())), preferred_element_type=F32)


def each(count, body):
    def step(i, carry):
        body(i)
        return carry

    lax.fori_loop(0, count, step, 0)


def rows_at(i, size):
    return pl.ds(pl.multiple_of(i * size, size), size)


def first_phase(tokens, params, first):
    gain = params[0:1, :]
    shift = params[1:2, :]

    def body(i):
        here = rows_at(i, 128)
        plain_gain, _, _ = normalize(tokens[here, :].astype(F32), gain, shift)
        first[here, :] = plain_gain.astype(LOW)

    each(ROWS // 128, body)


def mixed_phase(pair, first, wqkv, mixed):
    def body(i):
        mixed[pair] = dot(first[...], wqkv[pair]).astype(LOW)

    body(0)


def bias_phase(segments, head, bias):
    for seq in range(ROWS // SEQ):
        start = (head * (ROWS // SEQ) + seq) * (SEQ // 128)
        row = jnp.concatenate(
            [segments[pl.ds(start + i, 1), :] for i in range(SEQ // 128)], axis=1
        ).astype(F32)
        column = jnp.broadcast_to(row, (8, SEQ)).T[:, 0:1]
        bias[seq * SEQ : seq * SEQ + SEQ, :] = jnp.where(column == row, 0.0, neg_fill).astype(LOW)


def attend_phase(pair, mixed, bias, probs, context):
    lane = lax.broadcasted_iota(jnp.int32, (1, 128), 1)
    left = (lane < HEAD_DIM).astype(LOW)

    def body(seq):
        here = rows_at(seq, SEQ)
        query = mixed[pair, here, 0:128] * LOW(HEAD_DIM ** (-0.5))
        keys = mixed[pair, here, 128:256]
        values = mixed[pair, here, 256:384]
        allowed = bias[here, :].astype(F32)
        outs = []
        for half in range(2):
            mask = left if half == 0 else LOW(1.0) - left
            scores = dot_back(keys, query * mask) + allowed
            top = jnp.max(scores, axis=0, keepdims=True)
            weights = jnp.exp(scores - top)
            total = jnp.sum(weights, axis=0, keepdims=True)
            prob = (weights * (1.0 / total)).astype(LOW)
            probs[pair * 4 + half * 2 + seq] = prob
            outs.append(dot_rows(prob, values))
        context[here, pl.ds(pl.multiple_of(pair * 128, 128), 128)] = jnp.where(
            lane < HEAD_DIM, outs[0], outs[1]
        ).astype(LOW)

    each(ROWS // SEQ, body)


def second_phase(tokens, context, wout, params, middle, second):
    gain = params[2:3, :]
    shift = params[3:4, :]

    def body(i):
        here = rows_at(i, TILE)
        value = tokens[here, :].astype(F32) + dot(context[here, :], wout[...])
        middle[here, :] = value
        normal, _, _ = normalize(value, gain, shift)
        second[here, :] = normal.astype(LOW)

    each(ROWS // TILE, body)


def turn_phase(src, dst):
    def body(i):
        here = rows_at(i, 256)
        dst[:, here] = src[here, :].T

    each(ROWS // 256, body)


def feed_phase(
    chunk, second, second_t, out_grad, out_grad_t, up, down, active, hidden_grad,
    result, second_grad, g_up, g_down,
):
    units = rows_at(chunk, CHUNK)

    def body(i):
        here = rows_at(i, TILE)
        hidden = dot_back(second[here, :], up[units, :])
        switch = 0.5 * jnp.tanh(0.851 * hidden) + 0.5
        act = (hidden * switch).astype(LOW)
        active[here, :] = act
        grad = dot_back(out_grad[here, :], down[units, :])
        back = (grad * (switch + 1.702 * hidden * switch * (1.0 - switch))).astype(LOW)
        hidden_grad[here, :] = back
        result[here, :] += dot(act, down[units, :])
        second_grad[here, :] += dot(back, up[units, :])

    each(ROWS // TILE, body)

    for turned, wide, out in ((out_grad_t, active, g_down), (second_t, hidden_grad, g_up)):
        grad = dot(turned[...], wide[...]).astype(LOW)
        for j in range(CHUNK // 128):
            for c in range(2):
                out[chunk * 8 + j * 2 + c] = grad[c * 256 : c * 256 + 256, j * 128 : j * 128 + 128]


def middle_phase(
    params, middle, result, second_grad, out_grad, wout,
    layer_out, middle_grad, attended_low, context_grad, norms,
):
    gain = params[2:3, :]

    def body(i, sums):
        here = rows_at(i, TILE)
        value = middle[here, :]
        layer_out[here, :] = (value + result[here, :]).astype(LOW)
        _, plain, factor = normalize(value, gain, gain)
        upper = second_grad[here, :]
        lower, gains, shifts = normalize_back(upper, plain, factor, gain)
        total = out_grad[here, :].astype(F32) + lower
        middle_grad[here, :] = total
        low = total.astype(LOW)
        attended_low[here, :] = low
        context_grad[here, :] = dot_back(low, wout[...]).astype(LOW)
        return (sums[0] + gains[None], sums[1] + shifts[None])

    zero = jnp.zeros((1, 512), F32)
    sums = lax.fori_loop(0, ROWS // TILE, body, (zero, zero))
    norms[2:3, :] = sums[0]
    norms[3:4, :] = sums[1]


def out_phase(attended_t, context, g_attend):
    def body(i):
        here = rows_at(i, 512)
        grad = dot(attended_t[here, :], context[...]).astype(LOW)
        for p in range(PAIRS):
            g_attend[p, here, 384:512] = grad[:, p * 128 : p * 128 + 128]

    body(0)


def attend_back_phase(pair, seq, mixed, probs, context, context_grad):
    lane = lax.broadcasted_iota(jnp.int32, (1, 128), 1)
    left = (lane < HEAD_DIM).astype(LOW)
    scale = HEAD_DIM ** (-0.5)
    here = rows_at(seq, SEQ)
    query = mixed[pair, here, 0:128]
    keys = mixed[pair, here, 128:256]
    values = mixed[pair, here, 256:384]
    upper = context_grad[here, pl.ds(pl.multiple_of(pair * 128, 128), 128)]
    product = upper.astype(F32) * context[
        here, pl.ds(pl.multiple_of(pair * 128, 128), 128)
    ].astype(F32)
    product_high = product.astype(LOW)
    product_low = (product - product_high.astype(F32)).astype(LOW)
    marks = lax.broadcasted_iota(jnp.int32, (8, 128), 1) // HEAD_DIM
    marks = (marks == lax.broadcasted_iota(jnp.int32, (8, 128), 0)).astype(LOW)
    inners = dot_back(marks, product_high) + dot_back(marks, product_low)
    outs = []
    for half in range(2):
        mask = left if half == 0 else LOW(1.0) - left
        above = upper * mask
        prob_low = probs[pair * 4 + half * 2 + seq]
        prob = prob_low.astype(F32)
        prob_grad = dot_back(values, above)
        inner = inners[half : half + 1, :]
        score_grad = (prob * (prob_grad - inner)).astype(LOW)
        outs.append((dot_rows(score_grad, keys), dot(score_grad, query), dot(prob_low, above)))
    pick = lane < HEAD_DIM
    mixed[pair, here, 0:128] = (jnp.where(pick, outs[0][0], outs[1][0]) * scale).astype(LOW)
    mixed[pair, here, 128:256] = (jnp.where(pick, outs[0][1], outs[1][1]) * scale).astype(LOW)
    mixed[pair, here, 256:384] = (outs[0][2] + outs[1][2]).astype(LOW)


def qkv_phase(pair, mixed, first_t, g_attend):
    g_attend[pair, :, 0:384] = dot(first_t[...], mixed[pair]).astype(LOW)


def input_phase(params, tokens, mixed, wqkv, input_grad, norms):
    gain = params[0:1, :]

    def body(i, sums):
        here = rows_at(i, TILE)
        _, plain, factor = normalize(tokens[here, :].astype(F32), gain, gain)
        first_grad = dot_back(mixed[0, here, :], wqkv[0])
        for pair in range(1, PAIRS):
            first_grad = first_grad + dot_back(mixed[pair, here, :], wqkv[pair])
        lower, gains, shifts = normalize_back(first_grad, plain, factor, gain)
        input_grad[here, :] += lower
        return (sums[0] + gains[None], sums[1] + shifts[None])

    zero = jnp.zeros((1, 512), F32)
    sums = lax.fori_loop(0, ROWS // TILE, body, (zero, zero))
    norms[0:1, :] = sums[0]
    norms[1:2, :] = sums[1]


def local_call(kernel, outs, scratch, args, name):
    vmem = pl.BlockSpec(memory_space=pltpu.VMEM)
    return pl.pallas_call(
        kernel,
        out_shape=tuple(jax.ShapeDtypeStruct(*o) for o in outs),
        in_specs=[vmem] * len(args),
        out_specs=(vmem,) * len(outs),
        scratch_shapes=[pltpu.VMEM(*v) for v in scratch],
        compiler_params=pltpu.CompilerParams(vmem_limit_bytes=60 << 20),
        name=name,
    )(*args)


STEP_DIMS = {"c": 1, "x": 2, "y": 4, "l": 8, "g": 16}
GATHERS = ((0, 0, 512, ("g", "l", "y", "x")), (1, 0, 512, ("g", "l", "x", "y")))
STARTS = (("g", "l", "y", "x", "c"), ("x", "g", "l", "y", "c"), ("g", "y", "x", "l", "c"))
ATTEND_ORDER = ("c", "x", "y", "l", "g")


def coordinates():
    dp = lax.axis_index("dp")
    head = lax.axis_index("head")
    bits = {
        "c": head % 2,
        "x": head // 2,
        "y": dp % 2,
        "l": (dp // 2) % 2,
        "g": dp // 4,
    }
    steps = {"c": (0, 1), "x": (0, 2), "y": (1, 0), "l": (2, 0), "g": (4, 0)}
    peers = {}
    for name, (along_dp, along_head) in steps.items():
        turn = 1 - 2 * bits[name]
        peers[name] = (dp + along_dp * turn, head + along_head * turn)
    return dp, head, bits, peers


def remote(src, dst, send_sem, recv_sem, peer):
    return pltpu.make_async_remote_copy(
        src_ref=src,
        dst_ref=dst,
        send_sem=send_sem,
        recv_sem=recv_sem,
        device_id=peer,
        device_id_type=pl.DeviceIdType.MESH,
    )


def tile_of(fixed, free, place):
    total = 0
    for name, bit in fixed.items():
        total = total + STEP_DIMS[name] * bit
    for i, name in enumerate(free):
        total = total + STEP_DIMS[name] * ((place // 2**i) % 2)
    return total


def scatter_start(acc, got, base, fixed, name, free, bits, peer, sems, slot):
    for place in range(2 ** len(free)):
        away = tile_of({**fixed, name: 1 - bits[name]}, free, place)
        remote(
            acc.at[away], got.at[base + place], sems[0].at[slot], sems[1].at[slot], peer
        ).start()


def scatter_end(acc, got, base, fixed, name, free, bits, peer, sems, slot):
    count = 2 ** len(free)
    span = got.at[pl.ds(base, count)]
    remote(span, span, sems[0].at[slot], sems[1].at[slot], peer).wait()
    rows = acc.shape[1]

    def body(i):
        here = tile_of({**fixed, name: bits[name]}, free, i)
        acc[here] = (acc[here].astype(F32) + got[base + i].astype(F32)).astype(LOW)

    each(count, body)


def gather_start(ref, done, name, bits, peer, sems, slot):
    fixed = {d: bits[d] for d in STEP_DIMS if d not in done}
    for place in range(2 ** len(done)):
        part = ref.at[tile_of(fixed, done, place)]
        remote(part, part, sems[0].at[slot], sems[1].at[slot], peer).start()


def gather_end(ref, done, peer, sems, slot):
    span = ref.at[pl.ds(0, 2 ** len(done))]
    remote(span, span, sems[0].at[slot], sems[1].at[slot], peer).wait()


def paired(block):
    parts = [block[:, i * 64 : i * 64 + 64] for i in (0, 3, 1, 4, 2, 5)]
    return jnp.concatenate(parts, axis=1)


def unpaired(block):
    parts = [block[:, i * 64 : i * 64 + 64] for i in (0, 2, 4, 1, 3, 5)]
    return jnp.concatenate(parts, axis=1)


class Slots:
    def __init__(self):
        self.used = 0

    def __call__(self, count):
        start = self.used
        self.used += count
        return start


def update_step(pool, now, later, count, blocks, lanes, gram, mix):
    for low, high in ((0, 512), (256, 512)):
        rows = slice(low, low + 256)
        cols = slice(low, high)
        total = dot_back(pool[now, rows, :], pool[now, cols, :])
        for b in range(1, count):
            total = total + dot_back(pool[now + b, rows, :], pool[now + b, cols, :])
        made = total.astype(LOW)
        gram[rows, cols] = made
        if low == 0:
            gram[256:512, 0:256] = made[:, 256:512].T
    for low, high in ((0, 512), (256, 512)):
        rows = slice(low, low + 256)
        cols = slice(low, high)
        made = (
            ns_b * gram[rows, cols].astype(F32) + ns_c * dot(gram[rows, :], gram[:, cols])
        ).astype(LOW)
        mix[rows, cols] = made
        if low == 0:
            mix[256:512, 0:256] = made[:, 256:512].T

    def next_body(i):
        b = blocks[0] + i
        value = pool[now + b, :, lanes]
        pool[later + b, :, lanes] = (ns_a * value.astype(F32) + dot(mix[...], value)).astype(LOW)

    each(blocks[1], next_body)


def layer_kernel(
    tokens, segments, out_grad, params, w_qkv, m_qkv, w_out, m_out, w_up, m_up, w_down, m_down,
    layer_out, input_grad, start_a, start_u, start_d, ortho_q, ortho_o, ortho_u, ortho_d, norm_sum, scal,
    first, mixed, context, bias, wqkv, wout, wup, wdown, pool, middle, second, second_t, out_grad_t,
    active, hidden_grad, result, second_grad, acc_a, acc_u, acc_d, got_a, got_u, got_d,
    mom_full, mom_x, mom_u, mom_d, mom_a, norm_got, norm_far, stat_got, stat_far, gram, mix, send, recv,
):
    dp, head, bits, peers = coordinates()
    me = dp * 4 + head
    sibling = peers["c"]
    across = (dp, 3 - head)
    sems = (send, recv)
    slots = Slots()
    S_Q, S_O, S_M, S_MA = slots(4), slots(4), slots(2), slots(4)
    S_W, S_CORE, S_CHUNK, S_LG = slots(16), slots(20), slots(24), slots(16)
    S_A, S_NORM, S_STAT, S_START, S_SIDE, S_ORTHO = (
        slots(12), slots(2), slots(2), slots(15), slots(2), slots(8)
    )
    barrier = pltpu.get_barrier_semaphore()

    partners = (sibling, peers["x"], across)

    def along(i):
        return ((dp + 1 + i) % 8, head)

    def greet(peer):
        pl.semaphore_signal(barrier, inc=1, device_id=peer, device_id_type=pl.DeviceIdType.MESH)

    for peer in partners:
        greet(peer)
    each(7, lambda i: greet(along(i)))
    wqkv[head] = paired(w_qkv[...].astype(LOW))
    wout[pl.ds(pl.multiple_of(head * 128, 128), 128), :] = w_out[...].astype(LOW)
    mine = pl.ds(pl.multiple_of(me * 64, 64), 64)
    wup[mine, :] = w_up[...].astype(LOW)
    wdown[mine, :] = w_down[...].astype(LOW)
    pl.semaphore_wait(barrier, 10)

    def block_q(who):
        return wqkv.at[who]

    def block_o(who):
        return wout.at[pl.ds(pl.multiple_of(who * 128, 128), 128)]

    def weight_copy(block, who, slot, peer):
        return remote(block(who), block(who), send.at[slot], recv.at[slot], peer)

    def weight_tiles(i, k, far, half=None):
        matrix, start, count, order = GATHERS[i]
        done = order[: max(k, 0)]
        fixed = {d: bits[d] for d in STEP_DIMS if d not in done}
        if far and k >= 0:
            fixed[order[k]] = 1 - bits[order[k]]
        name = "c" if far else order[k]
        slot = S_CORE + i * 5 + k + 1 if far else S_W + i * 4 + k
        if half == 1 and not far:
            slot = S_W + 8 + i
        places = range(2 ** len(done)) if half is None else range(half * 4, half * 4 + 4)
        for place in places:
            row = pl.multiple_of(tile_of(fixed, done, place) * 64, 64)
            part = (wup, wdown)[matrix].at[pl.ds(row, 64), pl.ds(start, count)]
            remote(part, part, send.at[slot], recv.at[slot], peers[name]).start()

    def weight_wait(i, k, far):
        matrix, start, count, _ = GATHERS[i]
        slot = S_CORE + i * 5 + k + 1 if far else S_W + i * 4 + k
        span = (wup, wdown)[matrix].at[pl.ds(0, 64 * 2 ** max(k, 0)), pl.ds(start, count)]
        remote(span, span, send.at[slot], recv.at[slot], sibling).wait()

    for i in range(len(GATHERS)):
        weight_tiles(i, 0, False)
    weight_copy(block_q, head, S_Q + 1, sibling).start()
    weight_copy(block_q, head, S_Q + 2, peers["x"]).start()
    other_half = pl.ds(pl.multiple_of((1 - bits["c"]) * 256, 256), 256)

    def moment_copy(i, ref):
        return remote(ref.at[:, other_half], mom_x.at[i], send.at[S_M + i], recv.at[S_M + i], sibling)

    moment_copy(0, m_up).start()
    moment_copy(1, m_down).start()

    parts = range(len(GATHERS))

    def weight_step(k):
        if k < 3:
            for i in parts:
                weight_wait(i, k, False)
                for half in (None,) if k < 2 else (0, 1):
                    weight_tiles(i, k + 1, False, half)
            for i in parts:
                weight_tiles(i, k, True)
            return
        for half in range(2):
            for i in parts:
                slot = S_W + 8 + i if half else S_W + i * 4 + 3
                span = (wup, wdown)[GATHERS[i][0]].at[pl.ds(0, 256)]
                remote(span, span, send.at[slot], recv.at[slot], sibling).wait()
                weight_tiles(i, 3, True, half)

    weight_copy(block_o, head, S_O + 1, sibling).start()
    weight_copy(block_o, head, S_O + 2, peers["x"]).start()
    for i in parts:
        weight_tiles(i, -1, True)
    first_phase(tokens, params, first)
    bias_phase(segments, head, bias)
    mom_full[:, 0:384] = paired(m_qkv[...])
    mom_full[:, 384:512] = m_out[...].T

    def rank_of(c, x):
        return c * 16 + x * 8 + bits["y"] * 4 + bits["l"] * 2 + bits["g"]

    def rank_rows(who):
        return pl.ds(pl.multiple_of(rank_of(who % 2, who // 2) * 16, 16), 16)

    def rows_copy(j):
        who = partners[j][1]
        return remote(
            mom_full.at[rank_rows(who)], mom_a.at[head], send.at[S_MA + j], recv.at[S_MA + j], partners[j]
        )

    for j in range(3):
        rows_copy(j).start()
    mom_a[head] = mom_full[rank_rows(head), :]

    def pair_body(j):
        pair = (bits["c"] + j % 2) % 2 + 2 * ((bits["x"] + j // 2) % 2)
        mixed_phase(pair, first, wqkv, mixed)
        attend_phase(pair, mixed, bias, pool, context)

        @pl.when(j == 0)
        def _():
            weight_step(0)
            turn_phase(out_grad, out_grad_t)
            weight_copy(block_q, head, S_Q + 1, sibling).wait()
            weight_copy(block_o, head, S_O + 1, sibling).wait()

        @pl.when(j == 1)
        def _():
            weight_copy(block_q, head, S_Q + 2, peers["x"]).wait()
            weight_copy(block_q, peers["x"][1], S_Q + 3, sibling).start()
            weight_step(1)
            weight_copy(block_o, head, S_O + 2, peers["x"]).wait()
            weight_copy(block_o, peers["x"][1], S_O + 3, sibling).start()

        @pl.when(j == 2)
        def _():
            weight_copy(block_q, head, S_Q + 3, sibling).wait()
            weight_copy(block_o, head, S_O + 3, sibling).wait()

    each(PAIRS, pair_body)
    weight_step(2)
    second_phase(tokens, context, wout, params, middle, second)
    turn_phase(second, second_t)
    result[...] = jnp.zeros_like(result)
    second_grad[...] = jnp.zeros_like(second_grad)
    weight_step(3)
    for k in range(-1, 4):
        for i in parts:
            weight_wait(i, k, True)

    chunk_orders = ((acc_u, got_u, ("c", "x", "y")), (acc_d, got_d, ("c", "y", "x")))

    def chunk_args(q, k, order):
        fixed = {"g": q // 2, "l": q % 2}
        for name in order[:k]:
            fixed[name] = bits[name]
        return fixed, order[k], order[k + 1 :]

    def chunk_start(q, k):
        for i, (acc, got, order) in enumerate(chunk_orders):
            fixed, name, free = chunk_args(q, k, order)
            scatter_start(
                acc, got, q * 7 + (0, 4, 6)[k], fixed, name, free, bits, peers[name], sems,
                S_CHUNK + q * 6 + i * 3 + k,
            )

    def chunk_end(q, k):
        for i, (acc, got, order) in enumerate(chunk_orders):
            fixed, name, free = chunk_args(q, k, order)
            scatter_end(
                acc, got, q * 7 + (0, 4, 6)[k], fixed, name, free, bits, peers[name], sems,
                S_CHUNK + q * 6 + i * 3 + k,
            )

    def feed_body(q):
        feed_phase(
            q, second, second_t, out_grad, out_grad_t, wup, wdown, active, hidden_grad,
            result, second_grad, acc_u, acc_d,
        )
        chunk_start(q, 0)

        @pl.when(q >= 1)
        def _():
            chunk_end(q - 1, 0)
            chunk_start(q - 1, 1)

        @pl.when(q >= 3)
        def _():
            chunk_end(q - 3, 1)
            chunk_start(q - 3, 2)

    each(WIDE // CHUNK, feed_body)
    middle_phase(
        params, middle, result, second_grad, out_grad, wout,
        layer_out, input_grad, second, active, norm_got.at[head],
    )
    chunk_end(3, 0)
    chunk_start(3, 1)
    chunk_end(1, 1)
    chunk_start(1, 2)
    turn_phase(second, second_t)
    out_phase(second_t, context, acc_a)
    turn_phase(first, second_t)

    depth = dp // 2

    def owner_copy(i, acc, got, q):
        tile = tile_of({"g": q // 2, "l": q % 2, "c": bits["c"], "x": bits["x"], "y": bits["y"]}, (), 0)
        other = (2 * q + bits["y"], head)
        return remote(
            acc.at[tile], got.at[28 + (depth - q + 3) % 4], send.at[S_LG + 2 * q + i],
            recv.at[S_LG + 8 + 3 * i + (depth - q + 3) % 4], other,
        )

    def owner_start(q):
        @pl.when(depth != q)
        def _():
            for i, (acc, got, _) in enumerate(chunk_orders):
                owner_copy(i, acc, got, q).start()

    def owner_sent(q):
        @pl.when(depth != q)
        def _():
            for i, (acc, got, _) in enumerate(chunk_orders):
                owner_copy(i, acc, got, q).wait_send()

    def owner_end():
        for i, (acc, got, _) in enumerate(chunk_orders):
            for way in range(3):
                remote(
                    got.at[28 + way], got.at[28 + way], send.at[S_LG], recv.at[S_LG + 8 + 3 * i + way], sibling
                ).wait_recv()
            total = acc[me].astype(F32)
            for way in range(3):
                total = total + got[28 + way].astype(F32)
            acc[me] = total.astype(LOW)

    spans = []
    low_row = 0
    for k, name in enumerate(ATTEND_ORDER):
        size = 256 >> k
        spans.append((name, size, low_row + bits[name] * size, low_row + (1 - bits[name]) * size))
        low_row = low_row + bits[name] * size

    def aligned(row, size):
        return pl.ds(pl.multiple_of(row, 16), size)

    def attend_copy(pair, k):
        name, size, _, give = spans[k]
        return remote(
            acc_a.at[pair, aligned(give, size)], got_a.at[pair, pl.ds(512 - 2 * size, size)],
            send.at[S_A + pair * 3 + k], recv.at[S_A + pair * 3 + k], peers[name],
        )

    quarter = spans[1][2]

    def place_of(group):
        return (group % 2) * 4 + ((group // 2) % 2) * 2 + group // 4

    def attend_start(pair, k):
        if k < 2:
            attend_copy(pair, k).start()
            return

        def body(i):
            other = (dp + 1 + i) % 8
            remote(
                acc_a.at[pair, aligned(quarter + place_of(other) * 16, 16)],
                got_a.at[pair, aligned(384 + (6 - i) * 16, 16)],
                send.at[S_A + pair * 3 + 2], recv.at[S_A + pair * 3 + 2], (other, head),
            ).start()

        each(7, body)

    def attend_next(pair, k):
        if k == 2:
            span = got_a.at[pair, pl.ds(384, 112)]
            remote(span, span, send.at[S_A + pair * 3 + 2], recv.at[S_A + pair * 3 + 2], sibling).wait()
            here = aligned(low_row, 16)
            total = acc_a[pair, here, :].astype(F32)
            for i in range(1, 8):
                total = total + got_a[pair, 368 + i * 16 : 384 + i * 16, :].astype(F32)
            acc_a[pair, here, :] = total.astype(LOW)
            return
        attend_copy(pair, k).wait()
        _, size, keep, _ = spans[k]

        def body(i):
            here = aligned(keep + i * 64, 64)
            come = aligned(512 - 2 * size + i * 64, 64)
            acc_a[pair, here, :] = (
                acc_a[pair, here, :].astype(F32) + got_a[pair, come, :].astype(F32)
            ).astype(LOW)

        each(size // 64, body)
        attend_start(pair, k + 1)

    def at(wanted, pair):
        return pl.when(pair == wanted)

    def back_body(pair):
        attend_back_phase(pair, 0, mixed, pool, context, active)

        @at(0, pair)
        def _():
            chunk_end(0, 2)
            owner_start(0)
            chunk_end(2, 1)
            chunk_start(2, 2)

        @at(1, pair)
        def _():
            attend_next(0, 0)
            chunk_end(3, 1)
            chunk_start(3, 2)

        @at(2, pair)
        def _():
            attend_next(1, 0)
            attend_next(0, 1)

        @at(3, pair)
        def _():
            attend_next(2, 0)
            attend_next(1, 1)

        attend_back_phase(pair, 1, mixed, pool, context, active)
        qkv_phase(pair, mixed, second_t, acc_a)
        attend_start(pair, 0)

        @at(0, pair)
        def _():
            chunk_end(1, 2)
            owner_start(1)

        @at(1, pair)
        def _():
            chunk_end(2, 2)
            owner_start(2)

        @at(2, pair)
        def _():
            chunk_end(3, 2)
            owner_start(3)

    each(PAIRS, back_body)
    attend_next(3, 0)
    attend_next(2, 1)
    attend_next(0, 2)
    input_phase(params, tokens, mixed, wqkv, input_grad, norm_got.at[head])

    def tell(ref, slot):
        for peer in partners:
            remote(ref.at[head], ref.at[head], send.at[slot], recv.at[slot], peer).start()

    def tell_on(ref, far, slot):
        span = ref.at[pl.ds(0, 3)]
        remote(span, span, send.at[slot], recv.at[slot], sibling).wait()
        far[dp] = (ref[0] + ref[1]) + (ref[2] + ref[3])

        def body(i):
            remote(
                far.at[dp], far.at[dp], send.at[slot + 1], recv.at[slot + 1], along(i)
            ).start()

        each(7, body)

    def told_of(far, slot):
        span = far.at[pl.ds(0, 7)]
        remote(span, span, send.at[slot + 1], recv.at[slot + 1], sibling).wait()
        return jnp.sum(far[...], axis=0)

    tell(norm_got, S_NORM)
    attend_next(3, 1)
    attend_next(1, 2)
    tell_on(norm_got, norm_far, S_NORM)
    for q in range(4):
        owner_sent(q)
    owner_end()
    moment_copy(0, m_up).wait()
    moment_copy(1, m_down).wait()
    keep_half = pl.ds(pl.multiple_of(bits["c"] * 256, 256), 256)
    for i, (ref, out) in enumerate(((m_up, mom_u), (m_down, mom_d))):
        own = ref[:, keep_half]
        far = mom_x[i]
        low_half = jnp.where(bits["c"] == 0, own, far)
        high_half = jnp.where(bits["c"] == 0, far, own)
        out[...] = jnp.concatenate([low_half, high_half], axis=0).T
    for j in range(3):
        rows_copy(j).wait()

    def total_of(value):
        return jnp.sum(jnp.sum(value, axis=0, keepdims=True), axis=1, keepdims=True)

    lane = lax.broadcasted_iota(jnp.int32, (8, 128), 1)
    column = lax.broadcasted_iota(jnp.int32, (1, 512), 1)
    grad_u = acc_u[me].astype(F32)
    grad_d = acc_d[me].astype(F32)
    stats = jnp.zeros((8, 128), F32)
    for m, (moment, grad) in enumerate(((mom_u[...], grad_u), (mom_d[...], grad_d))):
        for i, product in enumerate((moment * moment, moment * grad, grad * grad)):
            stats = jnp.where(lane == 6 + 3 * m + i, total_of(product), stats)
    attend_next(2, 2)
    attend_next(3, 2)
    vector = told_of(norm_far, S_NORM)
    norm_sum[...] = vector
    vector_total = total_of(vector * vector)
    my_rows = aligned(low_row, 16)
    for i in range(3):
        inside = jnp.zeros((1, 512), F32)
        for pair in range(PAIRS):
            moment = mom_a[pair]
            grad = acc_a[pair, my_rows, :].astype(F32)
            product = (moment * moment, moment * grad, grad * grad)[i]
            inside = inside + jnp.sum(product, axis=0, keepdims=True)
        stats = jnp.where(lane == i, total_of(jnp.where(column < 384, inside, 0.0)), stats)
        stats = jnp.where(lane == 3 + i, total_of(jnp.where(column < 384, 0.0, inside)), stats)
    stat_got[head] = stats
    tell(stat_got, S_STAT)
    tell_on(stat_got, stat_far, S_STAT)
    stats = told_of(stat_far, S_STAT)

    def stat(i):
        return jnp.sum(jnp.where(lane == i, stats, 0.0), axis=1, keepdims=True)[0:1]

    norm = jnp.sqrt(stat(2) + stat(5) + stat(8) + stat(11) + vector_total)
    clip = jnp.minimum(1.0, 1.0 / (norm + 1e-06))
    sizes = []
    for m in range(4):
        square = (
            momentum_decay * momentum_decay * stat(3 * m)
            + 2.0 * momentum_decay * clip * stat(3 * m + 1)
            + clip * clip * stat(3 * m + 2)
        )
        sizes.append(jnp.sqrt(jnp.maximum(square, 0.0)) + 1e-07)
    told = jnp.where(lane == 0, norm, clip)
    for m in range(4):
        told = jnp.where(lane == 2 + m, sizes[m], told)
    scal[...] = told
    scale_a = jnp.where(column < 384, 1.0 / sizes[0], 1.0 / sizes[1])
    got_u[me] = ((momentum_decay * mom_u[...] + clip * grad_u) * (1.0 / sizes[2])).astype(LOW)
    got_d[me] = ((momentum_decay * mom_d[...] + clip * grad_d) * (1.0 / sizes[3])).astype(LOW)
    for pair in range(PAIRS):
        grad = acc_a[pair, my_rows, :].astype(F32)
        pool[pair, my_rows, :] = ((momentum_decay * mom_a[pair] + clip * grad) * scale_a).astype(LOW)

    mine_half = pl.ds(pl.multiple_of(bits["c"] * 256, 256), 256)

    def side_copy(i):
        src, dst = ((got_u, start_u), (got_d, start_d))[i]
        return remote(
            src.at[me], dst.at[mine_half], send.at[S_SIDE + i], recv.at[S_SIDE + i], sibling
        )

    side_copy(0).start()
    side_copy(1).start()
    start_u[mine_half, :] = got_u[me]
    start_d[mine_half, :] = got_d[me]

    def start_copy(k):
        name, size, keep, _ = spans[4 - k]
        part = pool.at[pl.ds(0, 4), aligned(keep, size)]
        return remote(part, part, send.at[S_START + 3 * k], recv.at[S_START + 3 * k], peers[name])

    tiles = ((got_u, STARTS[1]), (got_d, STARTS[2]))
    half_rows = aligned(spans[0][2], 256)
    pair_part = pool.at[pl.ds(head + 1 - 2 * bits["c"], 1), half_rows]
    all_part = pool.at[pl.ds(0, 4), half_rows]

    def core_copy(part):
        return remote(part, part, send.at[S_START + 12], recv.at[S_START + 12], sibling)

    def core_tiles(late):
        @pl.when(bits["c"] == 1)
        def _():
            row = spans[1][3] if late else spans[1][2]
            core_copy(pool.at[pl.ds(0, 4), aligned(row, 128)]).start()

        @pl.when(bits["c"] == 0)
        def _():
            for x, (got, order) in enumerate(tiles):
                @pl.when(bits["x"] == x)
                def _(got=got, order=order):
                    flipped = {**bits, order[3]: 1 - bits[order[3]]} if late else bits
                    gather_start(got, order[:3], "c", flipped, sibling, sems, S_START + 13)

    def core_early():
        core_tiles(False)

    for k in range(5):
        if k > 0:
            start_copy(k - 1).wait()
        if k < 4:
            start_copy(k).start()
        for m, (got, order) in enumerate(tiles):
            if k > 0:
                gather_end(got, order[: k - 1], peers[order[k - 1]], sems, S_START + 3 * k - 2 + m)
            if k < 4:
                gather_start(
                    got, order[:k], order[k], bits, peers[order[k]], sems, S_START + 3 * k + 1 + m
                )
        if k == 3:
            core_early()
    core_tiles(True)

    @pl.when(bits["c"] == 1)
    def _():
        def slice_body(i):
            rows = rows_at(i, 256)
            start_a[rows, :] = pool[head, rows, :]

        for x, (got, order) in enumerate(tiles):
            @pl.when(bits["x"] == x)
            def _(got=got, order=order, x=x):
                span = got.at[pl.ds(0, 16)]
                remote(span, span, send.at[S_START + 13], recv.at[S_START + 13], sibling).wait_recv()

                def body(i):
                    for j in range(4):
                        for c in range(2):
                            pool[4 + i, c * 256 : c * 256 + 256, j * 128 : j * 128 + 128] = got[
                                i * 8 + j * 2 + c
                            ]

                each(4, body)

        core_copy(pair_part).wait_recv()
        core_copy(all_part).wait_send()
        each(2, slice_body)

    @pl.when(bits["c"] == 0)
    def _():
        core_copy(pair_part).start()
        core_copy(all_part).wait_recv()

        def body(i):
            rows = rows_at(i, 256)
            start_a[rows, :] = pool[head, rows, :]
            for p in range(PAIRS):
                for r in range(3):
                    group = p * 3 + r
                    pool[4 + group // 4, rows, (group % 4) * 128 : (group % 4) * 128 + 128] = pool[
                        p, rows, r * 128 : r * 128 + 128
                    ]
                pool[7, rows, p * 128 : p * 128 + 128] = pool[p, rows, 384:512]

        each(2, body)
        core_copy(pair_part).wait_send()
        span = got_u.at[pl.ds(0, 16)]
        remote(span, span, send.at[S_START + 13], recv.at[S_START + 13], sibling).wait_send()

    side_copy(0).wait()
    side_copy(1).wait()

    every = pl.ds(0, 512)
    outs = (ortho_u, ortho_d)

    def out_copy(src, dst, i, peer):
        return remote(src, dst, send.at[S_ORTHO + i], recv.at[S_ORTHO + i], peer)

    def group_of(r):
        group = bits["x"] * 6 + r
        return pool.at[8 + group // 4, :, pl.ds(pl.multiple_of((group % 4) * 128, 128), 128)]

    def out_of(who):
        return pool.at[11, :, pl.ds(pl.multiple_of(who * 128, 128), 128)]

    @pl.when(bits["c"] == 0)
    def _():
        def turn_body(turn):
            now = 4 + (turn % 2) * 4
            later = 12 - now
            update_step(pool, now, later, 3, (0, 3), every, gram, mix)
            update_step(pool, now + 3, later + 3, 1, (0, 1), every, gram, mix)

        each(NS_STEPS - 1, turn_body)
        update_step(pool, 4, 8, 3, (bits["x"], 2), every, gram, mix)
        for r in range(3):
            out_copy(group_of(3 + r), ortho_q.at[:, pl.ds(r * 128, 128)], 0, sibling).start()
        for r in range(3):
            ortho_q[:, r * 128 : r * 128 + 128] = group_of(r)[...]
        columns = pl.ds(pl.multiple_of(bits["x"] * 256, 256), 256)
        update_step(pool, 7, 11, 1, (0, 1), columns, gram, mix)
        out_copy(out_of(head + 1), ortho_o, 1, sibling).start()
        ortho_o[...] = out_of(head)[...]
        out_copy(ortho_q, ortho_q, 0, sibling).wait_send()
        out_copy(ortho_o, ortho_o, 1, sibling).wait_send()

    @pl.when(bits["c"] == 1)
    def _():
        def turn_body(turn):
            now = 4 + (turn % 2) * 4
            update_step(pool, now, 12 - now, 4, (0, 4), every, gram, mix)

        each(NS_STEPS - 1, turn_body)
        wanted = dp // 2
        update_step(pool, 4, 8, 4, (wanted, 1), every, gram, mix)

        def block_of(x):
            block = dp * 2 + x
            return pool.at[8 + wanted, :, pl.ds(pl.multiple_of((block % 4) * 128, 128), 128)]

        for x in range(2):
            @pl.when(bits["x"] == x)
            def _(x=x):
                targets = ((across, 1 - x), (peers["x"], 1 - x), (sibling, x))
                for j, (peer, side) in enumerate(targets):
                    remote(
                        block_of(side), outs[x], send.at[S_ORTHO + 2 + j], recv.at[S_ORTHO + 2 + x], peer
                    ).start()
                outs[x][...] = block_of(x)[...]
                for j, (peer, side) in enumerate(targets):
                    remote(
                        block_of(side), outs[x], send.at[S_ORTHO + 2 + j], recv.at[S_ORTHO + 2 + x], peer
                    ).wait_send()

        out_copy(ortho_q, ortho_q, 0, sibling).wait_recv()
        out_copy(ortho_o, ortho_o, 1, sibling).wait_recv()

    for x in range(2):
        @pl.when(head != 2 * x + 1)
        def _(x=x):
            out_copy(outs[x], outs[x], 2 + x, sibling).wait_recv()


def layer_call(*args):
    shape = jax.ShapeDtypeStruct
    vmem = pl.BlockSpec(memory_space=pltpu.VMEM)
    outs = (
        shape((ROWS, 512), LOW), shape((ROWS, 512), F32),
        shape((512, 512), LOW), shape((512, 128), LOW), shape((512, 128), LOW),
        shape((512, 384), LOW), shape((512, 128), LOW), shape((512, 128), LOW), shape((512, 128), LOW),
        shape((4, 512), F32), shape((8, 128), F32),
    )
    scratch = [
        ((ROWS, 512), LOW),
        ((PAIRS, ROWS, 384), LOW),
        ((ROWS, 512), LOW),
        ((ROWS, SEQ), LOW),
        ((PAIRS, 512, 384), LOW),
        ((512, 512), LOW),
        ((WIDE, 512), LOW),
        ((WIDE, 512), LOW),
        ((16, 512, 512), LOW),
        ((ROWS, 512), F32),
        ((ROWS, 512), LOW),
        ((512, ROWS), LOW),
        ((512, ROWS), LOW),
        ((ROWS, CHUNK), LOW),
        ((ROWS, CHUNK), LOW),
        ((ROWS, 512), F32),
        ((ROWS, 512), F32),
        ((PAIRS, 512, 512), LOW),
        ((32, 256, 128), LOW),
        ((32, 256, 128), LOW),
        ((PAIRS, 512, 512), LOW),
        ((32, 256, 128), LOW),
        ((32, 256, 128), LOW),
        ((512, 512), F32),
        ((2, 64, 256), F32),
        ((256, 128), F32),
        ((256, 128), F32),
        ((PAIRS, 16, 512), F32),
        ((4, 4, 512), F32),
        ((8, 4, 512), F32),
        ((4, 8, 128), F32),
        ((8, 8, 128), F32),
        ((512, 512), LOW),
        ((512, 512), LOW),
    ]
    return pl.pallas_call(
        layer_kernel,
        out_shape=outs,
        in_specs=[vmem] * len(args),
        out_specs=(vmem,) * len(outs),
        scratch_shapes=[pltpu.VMEM(*v) for v in scratch]
        + [pltpu.SemaphoreType.DMA((128,)), pltpu.SemaphoreType.DMA((128,))],
        compiler_params=pltpu.CompilerParams(
            collective_id=1, has_side_effects=True, vmem_limit_bytes=VMEM_BYTES
        ),
        name="layer",
    )(*args)


def update_kernel(
    start_a, start_u, start_d, ortho_q, ortho_o, ortho_u, ortho_d, norm_sum, scal,
    w_qkv, w_out, w_up, w_down, norm_first, norm_second,
    new_q, mom_q, new_o, mom_o, new_u, mom_u, new_d, mom_d, clipped, first_new, second_new, norm,
):
    core = lax.axis_index("head") % 2
    clip = scal[0:1, 1:2]
    keep = 1.0 - muon_rate * muon_decay

    def fresh(weight, factor, ortho):
        return weight * keep - muon_rate * factor * ortho

    new_q[...] = fresh(w_qkv[...], math.sqrt(3.0), unpaired(ortho_q[...].astype(F32)))
    mom_q[...] = unpaired(start_a[:, 0:384].astype(F32)) * scal[0:1, 2:3]
    new_o[...] = fresh(w_out[...], math.sqrt(SEQ / 8.0), ortho_o[...].astype(F32).T)
    mom_o[...] = start_a[:, 384:512].astype(F32).T * scal[0:1, 3:4]
    for weight, ortho, start, new, mom, i in (
        (w_up, ortho_u, start_u, new_u, mom_u, 4),
        (w_down, ortho_d, start_d, new_d, mom_d, 5),
    ):
        turned = ortho[...].astype(F32).T
        turned = jnp.where(core == 0, turned[0:64], turned[64:128])
        new[...] = fresh(weight[...], math.sqrt(max(1.0, FF / 512)), turned)
        turned = start[...].astype(F32).T
        mom[...] = jnp.where(core == 0, turned[0:64], turned[64:128]) * scal[0:1, i : i + 1]
    norm[...] = scal[0:1, 0:1]
    clip_grad = clip * norm_sum[...]
    clipped[...] = clip_grad
    first_new[...] = beta_one * norm_first[...] + (1.0 - beta_one) * clip_grad
    second_new[...] = beta_two * norm_second[...] + (1.0 - beta_two) * clip_grad * clip_grad


def fast_shards(
    tokens,
    segments,
    out_grad,
    norm_params,
    norm_first,
    norm_second,
    qkv_weight,
    qkv_moment,
    out_weight,
    out_moment,
    up_weight,
    up_moment,
    down_weight,
    down_moment,
):
    (
        layer_out, input_grad, start_a, start_u, start_d, ortho_q, ortho_o, ortho_u, ortho_d, norm_sum, scal
    ) = layer_call(
        tokens, segments.reshape(segments.shape[0] // 128, 128), out_grad, norm_params,
        qkv_weight, qkv_moment, out_weight, out_moment,
        up_weight.T, up_moment.T, down_weight.T, down_moment.T,
    )
    tall = ((64, 512), F32)
    new_q, mom_q, new_o, mom_o, new_u, mom_u, new_d, mom_d, clipped, first_new, second_new, norm = local_call(
        update_kernel,
        [((512, 384), F32)] * 2 + [((128, 512), F32)] * 2 + [tall] * 4 + [((4, 512), F32)] * 3 + [((1, 1), F32)],
        [],
        (
            start_a, start_u, start_d, ortho_q, ortho_o, ortho_u, ortho_d, norm_sum, scal,
            qkv_weight, out_weight, up_weight.T, down_weight.T, norm_first, norm_second,
        ),
        "update",
    )
    return (
        layer_out, input_grad, norm.reshape(()), clipped, first_new, second_new,
        new_q, mom_q, new_o, mom_o, new_u.T, mom_u.T, new_d.T, mom_d.T,
    )


def general_update(
    whole_qkv, whole_out, up_grad, down_grad, vector_part,
    qkv_moment, out_moment, up_moment, down_moment,
):
    everywhere = ("dp", "head")
    narrow = out_moment.shape[0]
    up_part, down_part = (
        lax.psum_scatter(
            up_grad.astype(jnp.bfloat16), everywhere, scatter_dimension=1, tiled=True
        ).astype(jnp.float32),
        lax.psum_scatter(
            down_grad.astype(jnp.bfloat16), everywhere, scatter_dimension=1, tiled=True
        ).astype(jnp.float32),
    )
    qkv_part = lax.psum_scatter(
        whole_qkv.astype(jnp.bfloat16), "head", scatter_dimension=1, tiled=True
    )
    out_part = lax.psum_scatter(
        whole_out.astype(jnp.bfloat16), "head", scatter_dimension=0, tiled=True
    )
    qkv_sum, out_sum = (
        lax.psum(qkv_part, "dp").astype(jnp.float32),
        lax.psum(out_part, "dp").astype(jnp.float32),
    )
    leading = (lax.axis_index("dp") == 0).astype(jnp.float32)
    moments = [qkv_moment, out_moment, up_moment, down_moment]
    grads = [qkv_sum, out_sum, up_part, down_part]
    stats = jnp.stack(
        [
            squares_of(qkv_moment, qkv_sum, leading),
            squares_of(out_moment, out_sum, leading),
            squares_of(up_moment, up_part, 1.0),
            squares_of(down_moment, down_part, 1.0),
        ]
    )
    vector_sum, stat_sum = lax.psum((vector_part, stats), everywhere)
    grad_norm = jnp.sqrt(jnp.sum(stat_sum[:, 2]) + jnp.sum(vector_sum * vector_sum))
    clip = jnp.minimum(1.0, 1.0 / (grad_norm + 1e-06))
    sizes = jnp.sqrt(
        momentum_decay * momentum_decay * stat_sum[:, 0]
        + 2.0 * momentum_decay * clip * stat_sum[:, 1]
        + clip * clip * stat_sum[:, 2]
    )
    new_moments = [momentum_decay * moments[index] + clip * grads[index] for index in range(4)]
    starts = [
        (new_moments[index] / (sizes[index] + 1e-07)).astype(jnp.bfloat16) for index in range(4)
    ]
    blocks = [
        lax.all_gather(starts[0], "head", axis=1, tiled=True),
        lax.all_gather(starts[1], "head", axis=0, tiled=True),
        lax.all_gather(starts[2], everywhere, axis=1, tiled=True),
        lax.all_gather(starts[3], everywhere, axis=1, tiled=True),
    ]
    for turn in range(NS_STEPS):
        updated = []
        for index in range(4):
            form = gram_right if index == 1 else gram_left
            gram = form(blocks[index]).astype(jnp.bfloat16)
            mix = (
                ns_b * gram.astype(jnp.float32)
                + ns_c * jnp.dot(gram, gram, preferred_element_type=jnp.float32)
            ).astype(jnp.bfloat16)
            if index == 1:
                product = jnp.dot(blocks[index], mix, preferred_element_type=jnp.float32)
            else:
                product = jnp.dot(mix, blocks[index], preferred_element_type=jnp.float32)
            updated.append(
                (ns_a * blocks[index].astype(jnp.float32) + product).astype(jnp.bfloat16)
            )
        blocks = updated
    share = up_moment.shape[1]
    along = lax.axis_index("head")
    offset = (lax.axis_index("dp") * lax.axis_size("head") + along) * share
    owned = [
        lax.dynamic_slice_in_dim(blocks[0], along * qkv_moment.shape[1], qkv_moment.shape[1], 1),
        lax.dynamic_slice_in_dim(blocks[1], along * narrow, narrow, 0),
        lax.dynamic_slice_in_dim(blocks[2], offset, share, 1),
        lax.dynamic_slice_in_dim(blocks[3], offset, share, 1),
    ]
    return (owned, new_moments, vector_sum, grad_norm, clip)


def general_shards(
    tokens,
    segments,
    out_grad,
    norm_params,
    norm_first,
    norm_second,
    qkv_weight,
    qkv_moment,
    out_weight,
    out_moment,
    up_weight,
    up_moment,
    down_weight,
    down_moment,
):
    width = tokens.shape[1]
    rows = tokens.shape[0]
    narrow = out_weight.shape[0]
    sequences = rows // SEQ
    heads = width // HEAD_DIM
    everywhere = ("dp", "head")
    inputs = tokens.astype(jnp.float32)
    first, first_plain, first_factor = normalize(inputs, norm_params[0], norm_params[1])
    first_low = first.astype(jnp.bfloat16)
    qkv_full = lax.all_gather(qkv_weight.astype(jnp.bfloat16), "head", axis=1, tiled=True)
    out_full = lax.all_gather(out_weight.astype(jnp.bfloat16), "head", axis=0, tiled=True)
    up_all = lax.all_gather(up_weight.astype(jnp.bfloat16), everywhere, axis=1, tiled=True)
    down_all = lax.all_gather(down_weight.astype(jnp.bfloat16), everywhere, axis=1, tiled=True)
    mixed = jnp.dot(first_low, qkv_full, preferred_element_type=jnp.float32).astype(jnp.bfloat16)
    mixed = mixed.reshape(sequences, SEQ, heads, 3, HEAD_DIM)
    segment_rows = lax.dynamic_slice_in_dim(segments, lax.axis_index("head") * rows, rows, 0)
    segment_rows = segment_rows.reshape(sequences, SEQ)
    query = mixed[:, :, :, 0]
    keys = mixed[:, :, :, 1]
    values = mixed[:, :, :, 2]
    context, lse = lax.map(attend_forward, (query, keys, values, segment_rows))
    context = context.reshape(rows, width)
    attended = jnp.dot(context, out_full, preferred_element_type=jnp.float32)
    middle = inputs + attended
    second, second_plain, second_factor = normalize(middle, norm_params[2], norm_params[3])
    second_low = second.astype(jnp.bfloat16)
    hidden = jnp.dot(second_low, up_all, preferred_element_type=jnp.float32)
    switch = jax.nn.sigmoid(1.702 * hidden)
    active = (hidden * switch).astype(jnp.bfloat16)
    result = middle + lax.dot_general(
        active, down_all, (((1,), (1,)), ((), ())), preferred_element_type=jnp.float32
    )
    layer_out = result.astype(jnp.bfloat16)
    down_grad = lax.dot_general(
        out_grad, active, (((0,), (0,)), ((), ())), preferred_element_type=jnp.float32
    )
    active_grad = jnp.dot(out_grad, down_all, preferred_element_type=jnp.float32)
    hidden_grad = (active_grad * (switch + 1.702 * hidden * switch * (1.0 - switch))).astype(
        jnp.bfloat16
    )
    up_grad = lax.dot_general(
        second_low, hidden_grad, (((0,), (0,)), ((), ())), preferred_element_type=jnp.float32
    )
    second_grad = lax.dot_general(
        hidden_grad, up_all, (((1,), (1,)), ((), ())), preferred_element_type=jnp.float32
    )
    middle_lower, gain_two, shift_two = normalize_back(
        second_grad, second_plain, second_factor, norm_params[2]
    )
    middle_grad = out_grad.astype(jnp.float32) + middle_lower
    attended_low = middle_grad.astype(jnp.bfloat16)
    context_grad = lax.dot_general(
        attended_low, out_full, (((1,), (1,)), ((), ())), preferred_element_type=jnp.float32
    ).astype(jnp.bfloat16)
    whole_out = lax.dot_general(
        context, attended_low, (((0,), (0,)), ((), ())), preferred_element_type=jnp.float32
    )
    context_grad = context_grad.reshape(sequences, SEQ, heads, HEAD_DIM)
    mixed_grad = lax.map(attend_backward, (query, keys, values, segment_rows, context_grad, lse))
    mixed_grad = mixed_grad.reshape(rows, 3 * width)
    whole_qkv = lax.dot_general(
        first_low, mixed_grad, (((0,), (0,)), ((), ())), preferred_element_type=jnp.float32
    )
    first_grad = lax.dot_general(
        mixed_grad, qkv_full, (((1,), (1,)), ((), ())), preferred_element_type=jnp.float32
    )
    input_lower, gain_one, shift_one = normalize_back(
        first_grad, first_plain, first_factor, norm_params[0]
    )
    input_grad = middle_grad + input_lower
    vector_part = jnp.stack([gain_one, shift_one, gain_two, shift_two])
    (owned, new_moments, vector_sum, grad_norm, clip) = general_update(
        whole_qkv, whole_out, up_grad, down_grad, vector_part,
        qkv_moment, out_moment, up_moment, down_moment,
    )
    weights = [qkv_weight, out_weight, up_weight, down_weight]
    factors = [
        math.sqrt(3.0),
        math.sqrt(SEQ / 8.0),
        math.sqrt(max(1.0, FF / width)),
        math.sqrt(max(1.0, FF / width)),
    ]
    new_weights = [
        weights[index] * (1.0 - muon_rate * muon_decay)
        - muon_rate * factors[index] * owned[index].astype(jnp.float32)
        for index in range(4)
    ]
    clipped = clip * vector_sum
    first_new = beta_one * norm_first + (1.0 - beta_one) * clipped
    second_new = beta_two * norm_second + (1.0 - beta_two) * clipped * clipped
    return (
        layer_out,
        input_grad,
        grad_norm,
        clipped,
        first_new,
        second_new,
        new_weights[0],
        new_moments[0],
        new_weights[1],
        new_moments[1],
        new_weights[2],
        new_moments[2],
        new_weights[3],
        new_moments[3],
    )


def solution(mesh):
    placed = (
        P(("dp", "head"), None),
        P("dp"),
        P(("dp", "head"), None),
        P(),
        P(),
        P(),
        P(None, "head"),
        P(None, "head"),
        P("head", None),
        P("head", None),
        P(None, ("dp", "head")),
        P(None, ("dp", "head")),
        P(None, ("dp", "head")),
        P(None, ("dp", "head")),
    )
    fast = mesh.shape["dp"] == 8 and mesh.shape["head"] == 4
    return jax.shard_map(
        fast_shards if fast else general_shards,
        mesh=mesh,
        in_specs=placed,
        out_specs=(
            P(("dp", "head"), None),
            P(("dp", "head"), None),
            P(),
            P(),
            P(),
            P(),
            P(None, "head"),
            P(None, "head"),
            P("head", None),
            P("head", None),
            P(None, ("dp", "head")),
            P(None, ("dp", "head")),
            P(None, ("dp", "head")),
            P(None, ("dp", "head")),
        ),
        check_vma=False,
    )
```
